32 devices in a mesh: dp: 16 (over z, x, core), tensor: 2 (over y).
Axes of the slice: x: 2, y: 2, z: 4, core: 2. Of those that a mesh axis runs over, the one named last changes fastest.
Arguments:
- inputs: bfloat16 [10240, 2048], P('dp'), may hold values from -6 to 6
- doc_lengths: int32 [16, 8], P('dp'), may hold values from 1 to 320, 640 in all within a row
- norm1_gain: float32 [2048], replicated, may hold values from 0.5 to 1.5
- norm1_bias: float32 [2048], replicated, may hold values from -1.75 to 1.75
- qkv_weight: bfloat16 [2048, 8, 3, 256], P('dp', 'tensor'), may hold values from -0.125 to 0.125
- qkv_bias: float32 [8, 3, 256], P('tensor'), may hold values from -3 to 3
- out_weight: bfloat16 [8, 256, 2048], P('tensor', None, 'dp'), may hold values from -0.75 to 0.75
- out_bias: float32 [2048], replicated, may hold values from -1.75 to 1.75
- norm2_gain: float32 [2048], replicated, may hold values from 0.5 to 1.5
- norm2_bias: float32 [2048], replicated, may hold values from -1.75 to 1.75
- up_weight: bfloat16 [2048, 8192], P('dp', 'tensor'), may hold values from -0.125 to 0.125
- up_bias: float32 [8192], P('tensor'), may hold values from -3 to 3
- down_weight: bfloat16 [8192, 2048], P('tensor', 'dp'), may hold values from -0.0625 to 0.0625
- down_bias: float32 [2048], replicated, may hold values from -1.75 to 1.75
- cotangent: bfloat16 [10240, 2048], P('dp'), may hold values from -6 to 6
Outputs:
- outputs: bfloat16 [10240, 2048], P('dp')
- grad_inputs: float32 [10240, 2048], P('dp')
- grad_norm1_gain: float32 [2048], replicated
- grad_norm1_bias: float32 [2048], replicated
- grad_qkv_weight: float32 [2048, 8, 3, 256], P('dp', 'tensor')
- grad_qkv_bias: float32 [8, 3, 256], P('tensor')
- grad_out_weight: float32 [8, 256, 2048], P('tensor', None, 'dp')
- grad_output_bias: float32 [2048], replicated
- grad_norm2_gain: float32 [2048], replicated
- grad_norm2_bias: float32 [2048], replicated
- grad_up_weight: float32 [2048, 8192], P('dp', 'tensor')
- grad_up_bias: float32 [8192], P('tensor')
- grad_down_weight: float32 [8192, 2048], P('tensor', 'dp')
- attn_rms: float32 [], replicated
- ffn_rms: float32 [], replicated
The draws below stay inside these ranges and needn't reach their ends.
Inputs may be any that keep to these rules, and one draw needn't show every extreme that they name: `doc_lengths`: each row's 8 lengths sum to 640, and the largest in each row is 320.
All inputs are finite; a program needn't handle non-finite values.
Results may differ from the reference program's by a relative error of at most 0.01.
Values may be sent and summed in bfloat16 or wider, within the bound.
No kernel may reach another device: no remote copies, remote signals or barrier semaphores. Data moves between devices by JAX's collectives and lax.ppermute only.
A program may use at most 256 MiB of HBM per device.

```python
import math
import jax
import jax.numpy as jnp
import numpy as np
from jax import lax

D = 2048
HEADS = 8
HD = 256
ROT = 64
FF = 8192
TOK_DEV = 640
DOCS = 8
SEQ = 640
ROWS = 16
TOKENS = 10240


def with_spikes(array, rng, source, target, parts, factor):
    owner, partner = [(jnp.arange(array.shape[dim]) // (array.shape[dim] // parts)).reshape([-1 if axis == dim else 1 for axis in range(array.ndim)]) for dim in (source, target)]
    chosen = jax.random.permutation(rng, parts)[partner]
    strong = (owner == chosen) | (owner == (partner + parts // 2) % parts)
    return jnp.where(strong, factor * array, array)


def shard_levels(own_key, dims, cuts, smallest, high):
    factor_of = 1.0
    for axis_at, blocks in cuts:
        heights = jax.random.uniform(jax.random.fold_in(jax.random.fold_in(own_key, 6), axis_at), (blocks,), jnp.float32, smallest / len(cuts), high / len(cuts))
        factor_of = factor_of * jnp.repeat(jnp.exp(heights), dims[axis_at] // blocks).reshape((-1,) + (1,) * (len(dims) - 1 - axis_at))
    return factor_of


def length_profile(amount, total, limit, lean):
    portions = [(1 << 20) // math.isqrt(grade ** lean) + 1 for grade in range(2, amount + 1)]
    surplus, given = total - limit - (amount - 1), [1] * (amount - 1)
    while surplus > 0:
        movable = [i for i in range(amount - 1) if given[i] < limit]
        pool, budget = sum([portions[i] for i in movable]), surplus
        for i in movable:
            extra = min(limit - given[i], max(1, budget * portions[i] // pool), surplus)
            given[i] = given[i] + extra
            surplus = surplus - extra
    return np.array([limit] + given)


def uneven(key, number_of, total, reach, lean):
    if number_of == 2:
        one = jax.random.randint(key, (), max(1, total - reach), min(reach, total - 1) + 1)
        return jnp.stack([one, total - one])
    sizes = jnp.asarray(length_profile(number_of, total, reach, lean), jnp.int32)
    couples = (number_of - 1) // 2
    source_of, taker = sizes[1:1 + 2 * couples:2], sizes[2:2 + 2 * couples:2]
    room = jnp.minimum(source_of - 1, reach - taker)
    moved = jax.random.randint(jax.random.fold_in(key, 1), (couples,), 0, 1 << 20) % (room + 1)
    sizes = sizes.at[1:1 + 2 * couples:2].set(source_of - moved).at[2:2 + 2 * couples:2].set(taker + moved)
    return sizes[jax.random.permutation(jax.random.fold_in(key, 2), number_of)]


def centred(rng, dims, width, bound, cuts=(), kind=jnp.bfloat16):
    values = jax.random.normal(rng, dims, jnp.float32) * width
    if len(cuts) > 0:
        values = shard_levels(rng, dims, cuts, -0.22, 0.18) * values
    return jnp.clip(values, min=-bound, max=bound).astype(kind)


def gaussian_with(rng, dims, width, most, shards, heavy, kind=jnp.bfloat16):
    entries = width * jax.random.normal(rng, dims, jnp.float32)
    if shards:
        entries = entries * shard_levels(rng, dims, shards, -0.22, 0.18)
    return jnp.clip(with_spikes(entries, jax.random.fold_in(rng, 3), *heavy), -most, most).astype(kind)


def setup_inputs(seed: int = 0) -> dict:
    key_list = jax.random.split(jax.random.key(seed), 16)
    return {
        "inputs": gaussian_with(key_list[0], (TOKENS, D), 1.0, 6.0, ((0, 16),), (0, 1, 16, 2.0)),
        "doc_lengths": jax.vmap(lambda own: uneven(own, DOCS, SEQ, TOK_DEV // 2, 2))(jax.random.split(key_list[1], ROWS)).reshape((ROWS, DOCS)).astype(jnp.int32),
        "norm1_gain": jnp.clip(1.0 + 0.1 * jax.random.normal(key_list[2], (D,), jnp.float32), 0.5, 1.5),
        "norm1_bias": centred(key_list[3], (D,), 0.3, 1.75, (), jnp.float32),
        "qkv_weight": centred(key_list[4], (D, HEADS, 3, HD), D ** -0.5, 0.125, ((0, 16), (1, 2))),
        "qkv_bias": centred(key_list[5], (HEADS, 3, HD), 0.5, 3.0, ((0, 2),), jnp.float32),
        "out_weight": centred(key_list[6], (HEADS, HD, D), (D // 32) ** -0.5, 0.75, ((0, 2), (2, 16))),
        "out_bias": centred(key_list[7], (D,), 0.3, 1.75, (), jnp.float32),
        "norm2_gain": jnp.clip(1.0 + 0.1 * jax.random.normal(key_list[8], (D,), jnp.float32), 0.5, 1.5),
        "norm2_bias": centred(key_list[9], (D,), 0.3, 1.75, (), jnp.float32),
        "up_weight": centred(key_list[10], (D, FF), D ** -0.5, 0.125, ((0, 16), (1, 2))),
        "up_bias": centred(key_list[11], (FF,), 0.5, 3.0, ((0, 2),), jnp.float32),
        "down_weight": centred(key_list[12], (FF, D), FF ** -0.5, 0.0625, ((0, 2), (1, 16))),
        "down_bias": centred(key_list[13], (D,), 0.3, 1.75, (), jnp.float32),
        "cotangent": gaussian_with(key_list[14], (TOKENS, D), 1.0, 6.0, ((0, 16),), (0, 1, 16, 2.0)),
    }


norm_epsilon = 1e-05
highest = lax.Precision.HIGHEST

@jax.custom_vjp
def low(v):
    return lax.optimization_barrier(v.astype(jnp.bfloat16)).astype(jnp.float32)

@jax.custom_vjp
def low_back(v):
    return v

def low_keep(v):
    return (low(v), None)

def low_pass(kept, grad):
    return (grad,)

def back_keep(v):
    return (v, None)

def back_low(kept, grad):
    return (low(grad),)
low.defvjp(low_keep, low_pass)
low_back.defvjp(back_keep, back_low)

def layer_norm(values_in, gain, shift):
    centre = values_in - lax.optimization_barrier(jnp.mean(values_in, axis=-1, keepdims=True))
    spread = lax.optimization_barrier(jnp.mean(centre * centre, axis=-1, keepdims=True))
    return centre * lax.rsqrt(spread + norm_epsilon) * gain + shift

def rotate(values_in, position):
    half_dims = ROT // 2
    exponent = jnp.arange(half_dims, dtype=jnp.float32) * (-2.0 / ROT)
    frequency = jnp.power(10000.0, exponent)
    angle = position[..., None] * frequency
    angle = jnp.concatenate([angle, angle], axis=-1)[..., None, :]
    cosine = jnp.cos(angle)
    sine = jnp.sin(angle)
    rotary = values_in[..., :ROT]
    turned = jnp.concatenate([-rotary[..., half_dims:], rotary[..., :half_dims]], axis=-1)
    return jnp.concatenate([rotary * cosine + turned * sine, values_in[..., ROT:]], axis=-1)

def doc_info(lengths, place):
    ends = jnp.cumsum(lengths).astype(jnp.int32)
    passed = place[:, None] >= ends[None, :]
    segment = lax.optimization_barrier(jnp.sum(passed.astype(jnp.int32), axis=1)).astype(jnp.int32)
    start = lax.optimization_barrier(jnp.sum(jnp.where(passed, lengths[None, :], 0), axis=1)).astype(jnp.int32)
    return (segment, (place - start).astype(jnp.float32))

def forward(inputs_in, lengths, norm1_gain, norm1_bias, qkv_weight, qkv_bias, out_weight, out_bias, norm2_gain, norm2_bias, up_weight, up_bias, down_weight, down_bias):
    place = jnp.arange(SEQ, dtype=jnp.int32)
    segment, position = jax.vmap(lambda row_lengths: doc_info(row_lengths, place))(lengths)
    allowed = (segment[:, :, None] == segment[:, None, :]) & (place[:, None] >= place[None, :])[None]
    normed = low(layer_norm(inputs_in, norm1_gain, norm1_bias))
    projected = jnp.einsum('gtd,dhce->gthce', normed, qkv_weight, precision=highest) + qkv_bias
    query = low(rotate(low_back(projected[:, :, :, 0]), position))
    key_rot = low(rotate(low_back(projected[:, :, :, 1]), position))
    value = low(low_back(projected[:, :, :, 2]))
    scores = low_back(jnp.einsum('gqhe,gkhe->ghqk', query, key_rot, precision=highest)) * HD ** (-0.5)
    scores = jnp.where(allowed[:, None], scores, -1e+30)
    shifted = jnp.exp(scores - lax.optimization_barrier(jnp.max(scores, axis=-1, keepdims=True)))
    weights = low(shifted / lax.optimization_barrier(jnp.sum(shifted, axis=-1, keepdims=True)))
    heads = low(low_back(jnp.einsum('ghqk,gkhe->gqhe', weights, value, precision=highest)))
    attention = jnp.einsum('gqhe,hed->gqd', heads, out_weight, precision=highest) + out_bias
    mixed = low(layer_norm(inputs_in, norm2_gain, norm2_bias))
    hidden = low_back(jnp.einsum('gtd,df->gtf', mixed, up_weight, precision=highest) + up_bias)
    activation = low(jax.nn.gelu(hidden, approximate=False))
    feed_forward = jnp.einsum('gtf,fd->gtd', activation, down_weight, precision=highest) + down_bias
    squares = jnp.stack([jnp.sum(attention * attention), jnp.sum(feed_forward * feed_forward)])
    return (inputs_in + attention + feed_forward, squares)

def reference(inputs, doc_lengths, norm1_gain, norm1_bias, qkv_weight, qkv_bias, out_weight, out_bias, norm2_gain, norm2_bias, up_weight, up_bias, down_weight, down_bias, cotangent):
    group_rows = 4
    steps_count = ROWS // group_rows
    rows_in = inputs.astype(jnp.float32).reshape(steps_count, group_rows, SEQ, D)
    grads_in = cotangent.astype(jnp.float32).reshape(steps_count, group_rows, SEQ, D)
    lengths_in = doc_lengths.reshape(steps_count, group_rows, DOCS)
    params = (norm1_gain, norm1_bias, qkv_weight.astype(jnp.float32), qkv_bias, out_weight.astype(jnp.float32), out_bias, norm2_gain, norm2_bias, up_weight.astype(jnp.float32), up_bias, down_weight.astype(jnp.float32), down_bias)

    def one_step(running, scan_item):
        rows_now, grads_now, lengths_now = scan_item

        def apply_layer(rows_arg, *param_args):
            return forward(rows_arg, lengths_now, *param_args)
        result, pullback, squares = jax.vjp(apply_layer, rows_now, *params, has_aux=True)
        cotangents = pullback(grads_now)
        summed_grads = tuple((summed + addend for summed, addend in zip(running[0], cotangents[1:])))
        return ((summed_grads, running[1] + squares), (result, cotangents[0]))
    start_totals = (tuple((jnp.zeros_like(parameter) for parameter in params)), jnp.zeros((2,), jnp.float32))
    (totals, square_total), (results, input_grads) = lax.scan(one_step, start_totals, (rows_in, grads_in, lengths_in))
    outputs = results.reshape(TOKENS, D).astype(jnp.bfloat16)
    grad_inputs = input_grads.reshape(TOKENS, D)
    rms_pair = jnp.sqrt(square_total / (TOKENS * D))
    return (outputs, grad_inputs, totals[0], totals[1], totals[2], totals[3], totals[4], totals[5], totals[6], totals[7], totals[8], totals[9], totals[10], rms_pair[0], rms_pair[1])
```

```python
import jax
import jax.numpy as jnp
from jax import lax
from jax.sharding import Mesh
from jax.sharding import PartitionSpec as P

HD = 256
ROT = 64
EPS = 1e-05
LOW = jnp.bfloat16
WIDE = jnp.float32
GROUP = ("x", "c")
EVERY = ("z", "x", "c", "y")


def dot(left, right, dims):
    return lax.dot_general(left, right, (dims, ((), ())), preferred_element_type=WIDE)


def swap(value, axis):
    return lax.ppermute(value, axis, [(0, 1), (1, 0)])


def pick(value, index, axis):
    return lax.dynamic_index_in_dim(value, index, axis, keepdims=False)


def ordered(index, own, other, axis):
    first = jnp.where(index == 0, own, other)
    second = jnp.where(index == 0, other, own)
    return jnp.stack([first, second], axis=axis)


def spread_columns(shard, xi, ci):
    rows, _, cols = shard.shape
    shard = shard.reshape(rows, 2, 2, cols)
    pair = ordered(ci, pick(shard, ci, 2), swap(pick(shard, 1 - ci, 2), "c"), 0)
    quad = ordered(xi, pick(pair, xi, 2), swap(pick(pair, 1 - xi, 2), "x"), 0)
    return quad.reshape(4 * rows, cols)


def return_columns(block, xi, ci):
    rows, cols = block.shape[0] // 4, block.shape[1]
    quad = block.reshape(2, 2, rows, cols)
    pair = ordered(xi, pick(quad, xi, 0), swap(pick(quad, 1 - xi, 0), "x"), 0)
    back = ordered(ci, pick(pair, ci, 1), swap(pick(pair, 1 - ci, 1), "c"), 1)
    return jnp.transpose(back, (2, 0, 1, 3)).reshape(rows, 4, cols)


def gather_line(block, zi, count):
    right, left = [block], [block]
    for step in range(1, count):
        right.append(lax.ppermute(right[-1], "z", [(i, i + 1) for i in range(step - 1, count - 1)]))
        left.append(lax.ppermute(left[-1], "z", [(i, i - 1) for i in range(1, count - step + 1)]))
    rows = block.shape[0]
    full = jnp.zeros((count * rows, block.shape[1]), block.dtype)
    for step in range(count):
        part = block if step == 0 else jnp.where(zi >= step, right[step], left[count - step])
        full = lax.dynamic_update_slice_in_dim(full, part, lax.rem(zi - step + count, count) * rows, 0)
    return full


def gather_group(rows_in, yi):
    half = rows_in.shape[0] // 2
    near = swap(lax.dynamic_slice_in_dim(rows_in, yi * half, half, 0), "x")
    far = swap(near, "y")
    across = ordered(yi, near, far, 0).reshape(rows_in.shape)
    both = jnp.stack([rows_in, across])
    return jnp.concatenate([both, swap(both, "c")])


def reduce_group(product, xi, ci, yi):
    sent = swap(product(slice(2, 4)).astype(LOW), "c")
    over = swap((product(slice(1, 2)) + sent[1:2]).astype(LOW), "x")
    total = (product(slice(0, 1)) + sent[0:1] + over).astype(LOW)[0]
    half = total.shape[0] // 2
    mine = lax.dynamic_slice_in_dim(total, yi * half, half, 0)
    theirs = swap(lax.dynamic_slice_in_dim(total, (1 - yi) * half, half, 0), "y")
    return mine.astype(WIDE) + theirs.astype(WIDE)


def sum_everywhere(value, count):
    for axis in ("c", "x", "y"):
        value = value + swap(value, axis)
    step = 1
    while step < count:
        value = value + lax.ppermute(value, "z", [(i, i ^ step) for i in range(count)])
        step *= 2
    return value


def doc_info(lengths, place):
    ends = jnp.cumsum(lengths)
    passed = place[:, None] >= ends[None, :]
    segment = jnp.sum(passed.astype(jnp.int32), axis=1)
    start = jnp.sum(jnp.where(passed, lengths[None, :], 0), axis=1)
    return segment, (place - start).astype(WIDE)


def rotate(values_in, cosine, sine):
    half = ROT // 2
    rotary = values_in[..., :ROT]
    turned = jnp.concatenate([-rotary[..., half:], rotary[..., :half]], axis=-1)
    return jnp.concatenate([rotary * cosine + turned * sine, values_in[..., ROT:]], axis=-1)


def per_device(
    inputs,
    doc_lengths,
    norm1_gain,
    norm1_bias,
    qkv_weight,
    qkv_bias,
    out_weight,
    out_bias,
    norm2_gain,
    norm2_bias,
    up_weight,
    up_bias,
    down_weight,
    down_bias,
    cotangent,
):
    rows, width = inputs.shape
    count = lax.axis_size("z")
    zi, xi, ci, yi = [lax.axis_index(axis) for axis in EVERY]
    place = xi * 2 + ci
    hidden_part = up_bias.shape[0] // 4
    part_rows = up_weight.shape[0]
    head_width = 3 * HD

    up_rows = gather_line(
        spread_columns(up_weight.reshape(part_rows, 4, hidden_part), xi, ci), zi, count
    )
    x_all = gather_group(inputs, yi)
    down_cols = gather_line(
        spread_columns(down_weight.T.reshape(part_rows, 4, hidden_part), xi, ci), zi, count
    )
    dy_all = gather_group(cotangent, yi)
    attn_shard = jnp.concatenate(
        [qkv_weight.reshape(part_rows, 4, head_width), jnp.transpose(out_weight, (2, 0, 1))], axis=2
    )
    attn_rows = gather_line(spread_columns(attn_shard, xi, ci), zi, count)
    qkv_rows, out_cols = attn_rows[:, :head_width], attn_rows[:, head_width:]
    lengths_pair = jnp.concatenate([doc_lengths, swap(doc_lengths, "x")])
    lengths_all = jnp.concatenate([lengths_pair, swap(lengths_pair, "c")])

    x_wide = x_all.astype(WIDE)
    centre = x_wide - jnp.mean(x_wide, axis=-1, keepdims=True)
    spread = jnp.mean(centre * centre, axis=-1, keepdims=True)
    unit = centre * lax.rsqrt(spread + EPS)
    normed = (unit * norm1_gain + norm1_bias).astype(LOW).reshape(4 * rows, width)
    mixed = (unit * norm2_gain + norm2_bias).astype(LOW).reshape(4 * rows, width)
    dy_flat = dy_all.reshape(4 * rows, width)

    hidden = dot(mixed, up_rows, ((1,), (0,))) + pick(up_bias.reshape(4, -1), place, 0)
    cdf = 0.5 * (1.0 + lax.erf(hidden * (0.5**0.5)))
    density = jnp.exp(-0.5 * hidden * hidden) * 0.3989422804014327
    active = (hidden * cdf).astype(LOW)
    slope = (cdf + hidden * density).astype(LOW)
    grad_down = dot(dy_flat, active, ((0,), (0,))).astype(LOW)
    down_part = lax.psum_scatter(grad_down, "z", scatter_dimension=0, tiled=True)

    grad_hidden = (dot(dy_flat, down_cols, ((1,), (0,))) * slope.astype(WIDE)).astype(LOW)
    up_bias_term = jnp.sum(grad_hidden, axis=0, dtype=WIDE)
    grad_up = dot(mixed, grad_hidden, ((0,), (0,))).astype(LOW)
    up_part = lax.psum_scatter(grad_up, "z", scatter_dimension=0, tiled=True)
    active_seq = active.reshape(4, rows, -1)
    ffn_half = reduce_group(
        lambda which: dot(active_seq[which], down_cols, ((2,), (1,))), xi, ci, yi
    )

    segment, position = jax.vmap(lambda one: doc_info(one, jnp.arange(rows, dtype=jnp.int32)))(
        lengths_all
    )
    ordinal = jnp.arange(rows, dtype=jnp.int32)
    allowed = (segment[:, :, None] == segment[:, None, :]) & (
        ordinal[:, None] >= ordinal[None, :]
    )[None]
    exponent = jnp.arange(ROT // 2, dtype=WIDE) * (-2.0 / ROT)
    angle = position[..., None] * jnp.power(10000.0, exponent)
    angle = jnp.concatenate([angle, angle], axis=-1)
    cosine, sine = jnp.cos(angle), jnp.sin(angle)

    projected = dot(normed, qkv_rows, ((1,), (0,))) + pick(qkv_bias, place, 0).reshape(-1)
    projected = projected.reshape(4, rows, 3, HD)
    query = rotate(projected[:, :, 0], cosine, sine).astype(LOW)
    keys = rotate(projected[:, :, 1], cosine, sine).astype(LOW)
    value = projected[:, :, 2].astype(LOW)
    grad_heads = dot(dy_flat, out_cols, ((1,), (0,))).astype(LOW).reshape(4, rows, HD)
    scale = HD ** (-0.5)
    scores = jnp.einsum("bqe,bke->bqk", query, keys, preferred_element_type=WIDE) * scale
    scores = jnp.where(allowed, scores, -1e30)
    shifted = jnp.exp(scores - jnp.max(scores, axis=-1, keepdims=True))
    prob = shifted / jnp.sum(shifted, axis=-1, keepdims=True)
    prob_low = prob.astype(LOW)
    heads = jnp.einsum("bqk,bke->bqe", prob_low, value, preferred_element_type=WIDE).astype(LOW)
    grad_prob = jnp.einsum("bqe,bke->bqk", grad_heads, value, preferred_element_type=WIDE)
    weighted = jnp.sum(grad_prob * prob, axis=-1, keepdims=True)
    grad_scores = (prob * (grad_prob - weighted) * scale).astype(LOW)
    grad_query = jnp.einsum("bqk,bke->bqe", grad_scores, keys, preferred_element_type=WIDE)
    grad_keys = jnp.einsum("bqk,bqe->bke", grad_scores, query, preferred_element_type=WIDE)
    grad_value = jnp.einsum("bqk,bqe->bke", prob_low, grad_heads, preferred_element_type=WIDE)
    grad_projected = jnp.concatenate(
        [rotate(grad_query, cosine, -sine), rotate(grad_keys, cosine, -sine), grad_value], axis=-1
    ).astype(LOW)
    flat_grad = grad_projected.reshape(4 * rows, head_width)
    qkv_bias_term = jnp.sum(flat_grad, axis=0, dtype=WIDE)
    heads_flat = heads.reshape(4 * rows, HD)
    grad_qkv = dot(normed, flat_grad, ((0,), (0,))).astype(LOW)
    grad_out = dot(dy_flat, heads_flat, ((0,), (0,))).astype(LOW)
    attn_part = lax.psum_scatter(
        jnp.concatenate([grad_qkv, grad_out], axis=1), "z", scatter_dimension=0, tiled=True
    )
    attn_half = reduce_group(lambda which: dot(heads[which], out_cols, ((2,), (1,))), xi, ci, yi)

    hidden_seq = grad_hidden.reshape(4, rows, -1)
    input_half = reduce_group(
        lambda which: dot(grad_projected[which], qkv_rows, ((2,), (1,))) * norm1_gain
        + dot(hidden_seq[which], up_rows, ((2,), (1,))) * norm2_gain,
        xi,
        ci,
        yi,
    )

    half = rows // 2
    x_half = lax.dynamic_slice_in_dim(inputs, yi * half, half, 0).astype(WIDE)
    attn_branch = attn_half + out_bias
    ffn_branch = ffn_half + down_bias
    out_half = (x_half + attn_branch + ffn_branch).astype(LOW)
    outputs = ordered(yi, out_half, swap(out_half, "y"), 0).reshape(rows, width)

    centre_half = x_half - jnp.mean(x_half, axis=-1, keepdims=True)
    scale_half = lax.rsqrt(jnp.mean(centre_half * centre_half, axis=-1, keepdims=True) + EPS)
    unit_half = centre_half * scale_half
    back_half = (
        scale_half
        * (
            input_half
            - jnp.mean(input_half, axis=-1, keepdims=True)
            - unit_half * jnp.mean(input_half * unit_half, axis=-1, keepdims=True)
        )
    ).astype(LOW)
    back = ordered(yi, back_half, swap(back_half, "y"), 0).reshape(rows, width)
    grad_inputs = cotangent.astype(WIDE) + back.astype(WIDE)

    def norm_terms(weight, grad, bias_term, gain, shift):
        weight = weight.astype(WIDE)
        shift_term = jnp.sum(weight * bias_term, axis=1)
        gain_term = (jnp.sum(weight * grad.astype(WIDE), axis=1) - shift * shift_term) / gain
        return gain_term, shift_term

    gain1, shift1 = norm_terms(qkv_rows, grad_qkv, qkv_bias_term, norm1_gain, norm1_bias)
    gain2, shift2 = norm_terms(up_rows, grad_up, up_bias_term, norm2_gain, norm2_bias)
    slot = (jnp.arange(8, dtype=jnp.int32) == yi * 4 + place).astype(WIDE)[:, None]
    small = jnp.concatenate(
        [
            gain1,
            shift1,
            gain2,
            shift2,
            jnp.sum(dy_flat, axis=0, dtype=WIDE) * 0.125,
            (slot * qkv_bias_term).reshape(-1),
            (slot * up_bias_term).reshape(-1),
            jnp.stack([jnp.sum(attn_branch * attn_branch), jnp.sum(ffn_branch * ffn_branch)]),
        ]
    )
    small = sum_everywhere(small, count)
    sizes = [width] * 5 + [8 * head_width, 8 * hidden_part]
    starts = [sum(sizes[:i]) for i in range(len(sizes) + 1)]
    pieces = [small[a:b] for a, b in zip(starts[:-1], starts[1:])]
    qkv_bias_sum = pick(pieces[5].reshape(2, 4, 3, HD), yi, 0)
    up_bias_sum = pick(pieces[6].reshape(2, 4 * hidden_part), yi, 0)
    rms_pair = jnp.sqrt(small[starts[-1] :] / float(rows * 4 * count * width))

    up_sum = return_columns(up_part, xi, ci).reshape(part_rows, 4 * hidden_part).astype(WIDE)
    down_sum = return_columns(down_part, xi, ci).reshape(part_rows, 4 * hidden_part).T.astype(WIDE)
    attn_sum = return_columns(attn_part, xi, ci)
    qkv_sum = attn_sum[:, :, :head_width].reshape(part_rows, 4, 3, HD).astype(WIDE)
    out_sum = jnp.transpose(attn_sum[:, :, head_width:], (1, 2, 0)).astype(WIDE)
    return (
        outputs,
        grad_inputs,
        pieces[0],
        pieces[1],
        qkv_sum,
        qkv_bias_sum,
        out_sum,
        pieces[4],
        pieces[2],
        pieces[3],
        up_sum,
        up_bias_sum,
        down_sum,
        rms_pair[0],
        rms_pair[1],
    )


def solution(mesh):
    dp = mesh.shape["dp"]
    grid = Mesh(mesh.devices.reshape(dp // 4, 2, 2, mesh.shape["tensor"]), EVERY)
    dp = ("z", "x", "c")
    in_specs = (
        P(dp, None),
        P(dp, None),
        P(),
        P(),
        P(dp, "y", None, None),
        P("y", None, None),
        P("y", None, dp),
        P(),
        P(),
        P(),
        P(dp, "y"),
        P("y"),
        P("y", dp),
        P(),
        P(dp, None),
    )
    out_specs = (
        P(dp, None),
        P(dp, None),
        P(),
        P(),
        P(dp, "y", None, None),
        P("y", None, None),
        P("y", None, dp),
        P(),
        P(),
        P(),
        P(dp, "y"),
        P("y"),
        P("y", dp),
        P(),
        P(),
    )
    return jax.shard_map(
        per_device, mesh=grid, in_specs=in_specs, out_specs=out_specs, check_vma=False
    )
```

```python
import jax
import jax.numpy as jnp
from jax import lax
from jax.experimental import pallas as pl
from jax.experimental.pallas import tpu as pltpu
from jax.sharding import Mesh
from jax.sharding import PartitionSpec as P

HD = 256
ROT = 64
EPS = 1e-05
LOW = jnp.bfloat16
WIDE = jnp.float32
GROUP = ("x", "c")
EVERY = ("z", "x", "c", "y")


SMALL = pl.CostEstimate(flops=1 << 20, bytes_accessed=1 << 20, transcendentals=0)


def dot(left, right, dims):
    return lax.dot_general(left, right, (dims, ((), ())), preferred_element_type=WIDE)


def swap(value, axis):
    return lax.ppermute(value, axis, [(0, 1), (1, 0)])


def pick(value, index, axis):
    return lax.dynamic_index_in_dim(value, index, axis, keepdims=False)


def ordered(index, own, other, axis):
    first = jnp.where(index == 0, own, other)
    second = jnp.where(index == 0, other, own)
    return jnp.stack([first, second], axis=axis)


def trade(block, place):
    return [block(place)] + [
        lax.ppermute(block(place ^ step), GROUP, [(i, i ^ step) for i in range(4)])
        for step in range(1, 4)
    ]


class Line:
    def __init__(self, block, zi, count):
        self.block, self.zi, self.count = block, zi, count
        self.right, self.left = [block], [block]

    def hop(self, *waits):
        step, count = len(self.right), self.count
        if step == count:
            return
        right, left = after((self.right[-1], self.left[-1]), *waits)
        self.right.append(
            lax.ppermute(right, "z", [(i, i + 1) for i in range(step - 1, count - 1)])
        )
        self.left.append(lax.ppermute(left, "z", [(i, i - 1) for i in range(1, count - step + 1)]))

    def finish(self, *waits):
        while len(self.right) < self.count:
            self.hop(*waits)
        return self.right[-1], self.left[-1]

    def refs(self):
        return [self.block] + self.right[1:] + self.left[1:]


def add_kernel(index, term, *rest):
    received, results = rest[:-2], rest[-2:]
    for side in range(2):

        @pl.when(pl.program_id(0) == side)
        def _(side=side):
            value = term[0]
            if received:
                value = (value.astype(WIDE) + received[side][...].astype(WIDE)).astype(LOW)
            results[side][...] = value


def picked(terms, indices, received):
    _, rows, columns = terms.shape
    block = pl.BlockSpec((rows, columns), lambda i, index: (0, 0))
    return pl.pallas_call(
        add_kernel,
        grid_spec=pltpu.PrefetchScalarGridSpec(
            num_scalar_prefetch=1,
            grid=(2,),
            in_specs=[pl.BlockSpec((1, rows, columns), lambda i, index: (index[i], 0, 0))]
            + [block] * len(received),
            out_specs=[block] * 2,
        ),
        out_shape=[jax.ShapeDtypeStruct((rows, columns), LOW)] * 2,
        cost_estimate=SMALL,
    )(jnp.stack(indices), terms, *received)


class Sums:
    def __init__(self, terms, zi, count):
        self.terms, self.zi, self.count, self.step = terms, zi, count, 0
        self.right = self.left = None

    def hop(self):
        count, step = self.count, self.step + 1
        if step == count:
            return
        self.step = step
        right, left = picked(
            self.terms,
            (
                jnp.minimum(count - step + self.zi, count - 1),
                jnp.maximum(self.zi - (count - step), 0),
            ),
            () if self.right is None else (self.right, self.left),
        )
        forth = [(i, i + 1) for i in range(min(step, count - 1))]
        back = [(count - 1 - i, count - 1 - j) for i, j in forth]
        self.right = lax.ppermute(right, "z", forth)
        self.left = lax.ppermute(left, "z", back)

    def finish(self):
        while self.step < self.count - 1:
            self.hop()
        own = pick(self.terms, self.zi, 0).astype(WIDE)
        return (own + self.right.astype(WIDE) + self.left.astype(WIDE)).astype(LOW)


def tie(*values):
    return lax.optimization_barrier(values)


def after(value, *waits):
    return lax.optimization_barrier((value, waits))[0] if waits else value


def cross_first(mine, yi):
    rows, width = mine.shape[0] // 2, mine.shape[1]
    last = mine.reshape(2, 2, 2, rows // 4, width)[:, 1]
    return swap(mine[rows : rows + rows // 2], "x"), swap(pick(last, 1 - yi, 1), "y")


def cross_second(mine, over_x, over_y, yi):
    rows, width = mine.shape[0] // 2, mine.shape[1]
    part = rows // 4
    first = (mine[: rows // 2].astype(WIDE) + over_x.astype(WIDE)).astype(LOW)
    first = first.reshape(2, part, width)
    last = mine.reshape(2, 2, 2, part, width)[:, 1]
    last = pick(last, yi, 1).astype(WIDE) + over_y.astype(WIDE)
    sent = swap(last[1].astype(LOW), "x")
    return pick(first, yi, 0), swap(pick(first, 1 - yi, 0), "y"), last[0], sent


def crossed(own_first, sent_first, own_last, sent_last):
    return jnp.stack(
        [
            own_first.astype(WIDE) + sent_first.astype(WIDE),
            own_last + sent_last.astype(WIDE),
        ]
    )


def own_half(rows_in, yi):
    return pick(rows_in.reshape(2, 2, rows_in.shape[0] // 4, -1), yi, 1)


def whole_rows(half, yi):
    return ordered(yi, half, swap(half, "y"), 1).reshape(4 * half.shape[1], half.shape[2])


def norm_kernel(first, second, norms, *rest):
    normed, mixed, rows_in = rest[-3:]
    for index, ref in enumerate((first, second)):

        @pl.when(pl.program_id(0) == index)
        def _(ref=ref):
            rows_in[...] = ref[...]

    gain1, shift1, gain2, shift2 = [norms[i : i + 1, :] for i in range(4)]

    def norm(step, _):
        chunk = pl.ds(pl.multiple_of(step * 16, 16), 16)
        value = rows_in[chunk, :].astype(WIDE)
        centre = value - jnp.mean(value, axis=-1, keepdims=True)
        unit = centre * lax.rsqrt(jnp.mean(centre * centre, axis=-1, keepdims=True) + EPS)
        normed[chunk, :] = (unit * gain1 + shift1).astype(LOW)
        mixed[chunk, :] = (unit * gain2 + shift2).astype(LOW)
        return 0

    lax.fori_loop(0, rows_in.shape[0] // 16, norm, 0, unroll=4)


def norm_pair(first, second, offset, norms, before):
    rows, width = first.shape
    tile = rows // 2

    def out_place(s, t):
        return (2 * s + offset) * 2 + t, 0

    return pl.pallas_call(
        norm_kernel,
        grid=(2, 2),
        in_specs=[
            pl.BlockSpec((tile, width), lambda s, t: (jnp.where(s == 0, t, 1), 0)),
            pl.BlockSpec((tile, width), lambda s, t: (jnp.where(s == 0, 0, t), 0)),
            pl.BlockSpec((4, width), lambda s, t: (0, 0)),
        ]
        + [pl.BlockSpec(memory_space=pl.ANY)] * len(before),
        out_specs=[pl.BlockSpec((tile, width), out_place)] * 2,
        out_shape=[jax.ShapeDtypeStruct((4 * rows, width), LOW)] * 2,
        scratch_shapes=[pltpu.VMEM((tile, width), LOW)],
        input_output_aliases={3 + i: i for i in range(len(before))},
        cost_estimate=SMALL,
    )(first, second, norms, *before)


def copy_kernel(*refs):
    for index, ref in enumerate(refs[:2]):

        @pl.when(pl.program_id(0) == index)
        def _(ref=ref):
            refs[-1][...] = ref[...]


def copy_pair(first, second, offset, before):
    rows, width = first.shape
    tile = rows // 2
    return pl.pallas_call(
        copy_kernel,
        grid=(2, 2),
        in_specs=[
            pl.BlockSpec((tile, width), lambda s, t: (jnp.where(s == 0, t, 1), 0)),
            pl.BlockSpec((tile, width), lambda s, t: (jnp.where(s == 0, 0, t), 0)),
        ]
        + [pl.BlockSpec(memory_space=pl.ANY)] * len(before),
        out_specs=pl.BlockSpec((tile, width), lambda s, t: ((2 * s + offset) * 2 + t, 0)),
        out_shape=jax.ShapeDtypeStruct((4 * rows, width), LOW),
        input_output_aliases={2: 0} if before else {},
        cost_estimate=SMALL,
    )(first, second, *before)


def pack_kernel(*refs):
    rows = refs[0].shape[0]
    for index, ref in enumerate(refs[:-1]):
        refs[-1][index * rows : (index + 1) * rows, :] = ref[...]


def pack(blocks):
    rows, columns = blocks[0].shape
    return pl.pallas_call(
        pack_kernel,
        out_shape=jax.ShapeDtypeStruct((len(blocks) * rows, columns), LOW),
        cost_estimate=SMALL,
    )(*blocks)


def outer_kernel(*refs):
    result, pairs, start = refs[-1], refs[:-1], 0
    for left, right in zip(pairs[0::2], pairs[1::2]):
        columns = slice(start, start + right.shape[1])
        result[:, columns] = dot(left[...], right[...], ((0,), (0,))).astype(LOW)
        start = columns.stop


def outer(*arrays):
    tokens, width = arrays[0].shape
    tile = width // 4
    columns = sum(right.shape[1] for right in arrays[1::2])
    in_specs = []
    for right in arrays[1::2]:
        in_specs += [
            pl.BlockSpec((tokens, tile), lambda i: (0, i)),
            pl.BlockSpec(right.shape, lambda i: (0, 0), pipeline_mode=pl.Buffered(1)),
        ]
    return pl.pallas_call(
        outer_kernel,
        grid=(4,),
        in_specs=in_specs,
        out_specs=pl.BlockSpec((tile, columns), lambda i: (i, 0)),
        out_shape=jax.ShapeDtypeStruct((width, columns), LOW),
        cost_estimate=SMALL,
    )(*arrays)


def collect(where, refs, count, full, result, copies, kept):
    zi, place = where[0], where[1]
    rows = full.shape[1]

    def move(ref, base, block):
        for step in range(4):
            pltpu.make_async_copy(
                ref.at[pl.ds(base + step * rows, rows)],
                full.at[4 * block + (place ^ step)],
                copies.at[4 * block + step],
            ).start()

    for block in range(count):
        if len(refs) == 1:
            move(refs[0], block * 4 * rows, block)
            continue
        for step in range(count):
            pairs = [(step, block + step), (count - 1 + step, block - step)]
            for index, owner in pairs[: 2 if step else 1]:
                if 0 <= owner < count:

                    @pl.when(zi == owner)
                    def _(index=index):
                        move(refs[index], 0, block)

    for block in range(count):
        for step in range(4):
            pltpu.make_async_copy(
                refs[0].at[pl.ds(0, rows)],
                full.at[4 * block + (place ^ step)],
                copies.at[4 * block + step],
            ).wait()
    pltpu.make_async_copy(full, result, kept).start()


def weighted_call(kernel, where, gathered, count, operands, in_specs, out_specs, out_shape, grid, scratch):
    refs = gathered.refs() if isinstance(gathered, Line) else [gathered]
    rows, columns = refs[0].shape
    rows = rows // 4 if len(refs) > 1 else rows // (4 * count)
    last = grid[0] - 1

    def body(where_ref, *args):
        parts, args = args[: len(refs)], args[len(refs) :]
        inputs, args = args[: len(operands)], args[len(operands) :]
        result, args = args[0], args[1:]
        full, copies, kept = args[-3:]

        @pl.when(pl.program_id(0) == 0)
        def _():
            collect(where_ref, parts, count, full, result, copies, kept)

        kernel(full, *inputs, *args[:-3])

        @pl.when(pl.program_id(0) == last)
        def _():
            pltpu.make_async_copy(full, result, kept).wait()

    result = pl.pallas_call(
        body,
        grid_spec=pltpu.PrefetchScalarGridSpec(
            num_scalar_prefetch=1,
            grid=grid,
            in_specs=[pl.BlockSpec(memory_space=pl.ANY)] * len(refs) + in_specs,
            out_specs=[pl.BlockSpec(memory_space=pl.ANY)] + out_specs,
            scratch_shapes=scratch
            + [
                pltpu.VMEM((4 * count, rows, columns), LOW),
                pltpu.SemaphoreType.DMA((4 * count,)),
                pltpu.SemaphoreType.DMA,
            ],
        ),
        out_shape=[jax.ShapeDtypeStruct((4 * count, rows, columns), LOW)] + out_shape,
        cost_estimate=SMALL,
    )(where, *refs, *operands)
    return [result[0].reshape(4 * count * rows, columns)] + list(result[1:])


def up_kernel(full, mixed, bias, active, slope):
    weight = full.reshape(full.shape[0] * full.shape[1], full.shape[2])
    for start in range(0, weight.shape[1], 256):
        columns = slice(start, start + 256)
        hidden = dot(mixed[...], weight[:, columns], ((1,), (0,))) + bias[:, columns]
        cdf = 0.5 * (1.0 + lax.erf(hidden * (0.5**0.5)))
        density = jnp.exp(-0.5 * hidden * hidden) * 0.3989422804014327
        active[:, columns] = (hidden * cdf).astype(LOW)
        slope[:, columns] = (cdf + hidden * density).astype(LOW)


def up_forward(where, gathered, count, mixed, bias):
    tokens, width = mixed.shape
    columns = bias.shape[1]
    tile = tokens // 8

    def rows_of(size):
        return pl.BlockSpec((tile, size), lambda i, z: (i, 0))

    return weighted_call(
        up_kernel,
        where,
        gathered,
        count,
        (mixed, bias),
        [rows_of(width), pl.BlockSpec((1, columns), lambda i, z: (0, 0))],
        [rows_of(columns)] * 2,
        [jax.ShapeDtypeStruct((tokens, columns), LOW)] * 2,
        (8,),
        [],
    )


def down_kernel(full, dy, slope, grad, total):
    weight = full.reshape(full.shape[0] * full.shape[1], full.shape[2])

    @pl.when(pl.program_id(0) == 0)
    def _():
        total[...] = jnp.zeros_like(total)

    for start in range(0, weight.shape[1], 256):
        columns = slice(start, start + 256)
        value = dot(dy[...], weight[:, columns], ((1,), (0,))) * slope[:, columns].astype(WIDE)
        value = value.astype(LOW)
        grad[:, columns] = value
        total[:, columns] += jnp.sum(value.astype(WIDE), axis=0, keepdims=True)


def down_backward(where, gathered, count, dy, slope):
    tokens, width = dy.shape
    columns = slope.shape[1]
    tile = tokens // 8

    def rows_of(size):
        return pl.BlockSpec((tile, size), lambda i, z: (i, 0))

    return weighted_call(
        down_kernel,
        where,
        gathered,
        count,
        (dy, slope),
        [rows_of(width), rows_of(columns)],
        [rows_of(columns), pl.BlockSpec((1, columns), lambda i, z: (0, 0))],
        [
            jax.ShapeDtypeStruct((tokens, columns), LOW),
            jax.ShapeDtypeStruct((1, columns), WIDE),
        ],
        (8,),
        [],
    )


def input_kernel(attn, hidden, attn_weight, up_weight, gains, *rest):
    result = rest[-1]
    for start in range(0, result.shape[1], 512):
        columns = slice(start, start + 512)
        value = (
            dot(attn[...], attn_weight[columns, : attn.shape[1]], ((1,), (1,))) * gains[0:1, columns]
        )
        value += dot(hidden[...], up_weight[columns, :], ((1,), (1,))) * gains[1:2, columns]
        if len(rest) == 2:
            value += rest[0][:, columns].astype(WIDE)
        result[:, columns] = value.astype(LOW)


def input_terms(first, attn, hidden, attn_weight, up_weight, gains, sent):
    tokens = attn.shape[0] // 2
    width = gains.shape[1]
    tile = tokens // 4
    skip = first // tile

    def rows_of(size, start):
        return pl.BlockSpec((tile, size), lambda i: (i + start, 0))

    def whole(array):
        return pl.BlockSpec(array.shape, lambda i: (0, 0), pipeline_mode=pl.Buffered(1))

    extra = () if sent is None else (sent,)
    return pl.pallas_call(
        input_kernel,
        grid=(4,),
        in_specs=[
            rows_of(attn.shape[1], skip),
            rows_of(hidden.shape[1], skip),
            whole(attn_weight),
            whole(up_weight),
            whole(gains),
        ]
        + [rows_of(width, 0)] * len(extra),
        out_specs=rows_of(width, 0),
        out_shape=jax.ShapeDtypeStruct((tokens, width), LOW),
        cost_estimate=SMALL,
    )(attn, hidden, attn_weight, up_weight, gains, *extra)


def attention_kernel(full, normed, dy, bias, cosine, sine, begin, heads, grad, total, *scratch):
    q_s, k_s, v_s, g_s, dk_s, dv_s = scratch
    weight = full.reshape(full.shape[0] * full.shape[1], full.shape[2])
    rows = normed.shape[0]
    lane = lax.broadcasted_iota(jnp.int32, (1, 128), 1)
    scale = HD ** (-0.5)

    def turn(value, sign):
        low = value[:, :128]
        sine_now = sine[0] * sign
        ahead = pltpu.roll(low, 128 - ROT // 2, 1) * jnp.where(lane < ROT // 2, -sine_now, 0.0)
        behind = pltpu.roll(low, ROT // 2, 1) * jnp.where(lane < ROT // 2, 0.0, sine_now)
        return jnp.concatenate([low * cosine[0] + ahead + behind, value[:, 128:]], axis=1)

    def project(index):
        columns = slice(index * HD, (index + 1) * HD)
        return dot(normed[...], weight[:, columns], ((1,), (0,))) + bias[:, columns]

    q_s[...] = turn(project(0), 1.0).astype(LOW)
    k_s[...] = turn(project(1), 1.0).astype(LOW)
    v_s[...] = project(2).astype(LOW)
    g_s[...] = dot(dy[...], weight[:, 3 * HD :], ((1,), (0,))).astype(LOW)
    dk_s[...] = jnp.zeros_like(dk_s)
    dv_s[...] = jnp.zeros_like(dv_s)
    tile = 128
    for start in range(0, rows, tile):
        here, seen = slice(start, start + tile), slice(0, start + tile)
        query, grad_heads = q_s[here, :], g_s[here, :]
        keys, value = k_s[seen, :], v_s[seen, :]
        scores = dot(query, keys, ((1,), (1,))) * scale
        column = lax.broadcasted_iota(jnp.int32, scores.shape, 1)
        row = lax.broadcasted_iota(jnp.int32, scores.shape, 0) + start
        allowed = (column <= row) & (column >= begin[0, here, :])
        scores = jnp.where(allowed, scores, -1e30)
        shifted = jnp.exp(scores - jnp.max(scores, axis=1, keepdims=True))
        prob = shifted / jnp.sum(shifted, axis=1, keepdims=True)
        low = prob.astype(LOW)
        heads[here, :] = dot(low, value, ((1,), (0,))).astype(LOW)
        grad_prob = dot(grad_heads, value, ((1,), (1,)))
        weighted = jnp.sum(grad_prob * prob, axis=1, keepdims=True)
        grad_scores = (prob * (grad_prob - weighted) * scale).astype(LOW)
        grad_query = dot(grad_scores, keys, ((1,), (0,)))
        cos_here = cosine[0, here, :]
        sine_here = -sine[0, here, :]
        head = grad_query[:, :128]
        ahead = pltpu.roll(head, 128 - ROT // 2, 1) * jnp.where(lane < ROT // 2, -sine_here, 0.0)
        behind = pltpu.roll(head, ROT // 2, 1) * jnp.where(lane < ROT // 2, 0.0, sine_here)
        grad[here, :128] = (head * cos_here + ahead + behind).astype(LOW)
        grad[here, 128:HD] = grad_query[:, 128:].astype(LOW)
        dk_s[seen, :] += dot(grad_scores, query, ((0,), (0,)))
        dv_s[seen, :] += dot(low, grad_heads, ((0,), (0,)))
    grad[:, HD : 2 * HD] = turn(dk_s[...], -1.0).astype(LOW)
    grad[:, 2 * HD :] = dv_s[...].astype(LOW)

    @pl.when(pl.program_id(0) == 0)
    def _():
        total[...] = jnp.zeros_like(total)

    total[...] += jnp.sum(grad[...].astype(WIDE), axis=0, keepdims=True)


def attention(where, gathered, count, normed, dy, bias, cosine, sine, begin):
    tokens, width = normed.shape
    rows = tokens // 4

    def per_sequence(size):
        return pl.BlockSpec((rows, size), lambda s, z: (s, 0))

    def table(size):
        return pl.BlockSpec((1, rows, size), lambda s, z: (s, 0, 0))

    row = pl.BlockSpec((1, 3 * HD), lambda s, z: (0, 0))
    return weighted_call(
        attention_kernel,
        where,
        gathered,
        count,
        (normed, dy, bias, cosine, sine, begin),
        [per_sequence(width), per_sequence(width), row, table(128), table(128), table(1)],
        [per_sequence(HD), per_sequence(3 * HD), row],
        [
            jax.ShapeDtypeStruct((tokens, HD), LOW),
            jax.ShapeDtypeStruct((tokens, 3 * HD), LOW),
            jax.ShapeDtypeStruct((1, 3 * HD), WIDE),
        ],
        (4,),
        [pltpu.VMEM((rows, HD), LOW)] * 4 + [pltpu.VMEM((rows, HD), WIDE)] * 2,
    )


def sum_everywhere(value, count):
    for axis in ("c", "x", "y"):
        value = value + swap(value, axis)
    step = 1
    while step < count:
        value = value + lax.ppermute(value, "z", [(i, i ^ step) for i in range(count)])
        step *= 2
    return value


def doc_start(lengths, place):
    passed = place[:, None] >= jnp.cumsum(lengths)[None, :]
    return jnp.sum(jnp.where(passed, lengths[None, :], 0), axis=1)


def per_device(
    inputs,
    doc_lengths,
    norm1_gain,
    norm1_bias,
    qkv_weight,
    qkv_bias,
    out_weight,
    out_bias,
    norm2_gain,
    norm2_bias,
    up_weight,
    up_bias,
    down_weight,
    down_bias,
    cotangent,
):
    rows, width = inputs.shape
    count = lax.axis_size("z")
    zi, xi, ci, yi = [lax.axis_index(axis) for axis in EVERY]
    place = xi * 2 + ci
    hidden_part = up_bias.shape[0] // 4
    part_rows = up_weight.shape[0]
    head_width = 3 * HD

    norms = jnp.stack([norm1_gain, norm1_bias, norm2_gain, norm2_bias])

    def columns_of(weight):
        return lambda t: lax.dynamic_slice_in_dim(weight, t * hidden_part, hidden_part, 1)

    def rows_of(weight):
        return lambda t: lax.dynamic_slice_in_dim(weight, t * hidden_part, hidden_part, 0).T

    def heads_of(qkv, out):
        return lambda t: jnp.concatenate(
            [pick(qkv, t, 1).reshape(part_rows, head_width), pick(out, t, 0).T], axis=1
        )

    def returned(part):
        return trade(
            lambda t: lax.dynamic_slice_in_dim(part, t * part_rows, part_rows, 0), place
        )

    where = jnp.stack([zi, place])
    half = rows // 2

    def side(array):
        return lax.dynamic_slice_in_dim(array, yi * half, half, 0)

    def stage(line, *values):
        line.right[-1], line.left[-1], values = tie(line.right[-1], line.left[-1], values)
        return values

    up_blocks = trade(columns_of(up_weight), place)
    up_blocks, x_now, x_beside, dy_beside, lengths_x = tie(
        up_blocks, inputs, swap(inputs, "c"), swap(cotangent, "c"), swap(doc_lengths, "x")
    )

    up_line = Line(pack(up_blocks), zi, count)
    up_line.hop()
    x_near, norm_now, weights_now, lengths_x, lengths_now, dy_now = stage(
        up_line,
        swap(side(after(x_now, up_line.block)), "x"),
        norm_pair(x_now, x_beside, 0, norms, ()),
        (qkv_weight, out_weight),
        lengths_x,
        doc_lengths,
        (cotangent, dy_beside),
    )

    up_line.hop()
    lengths_pair = jnp.concatenate([lengths_now, lengths_x])
    x_far, attn_blocks, lengths_other, dy_flat, dy_now = stage(
        up_line,
        swap(x_near, "y"),
        trade(heads_of(*weights_now), place),
        swap(lengths_pair, "c"),
        copy_pair(*dy_now, 0, ()),
        cotangent,
    )

    up_line.finish()
    across = ordered(yi, x_near, x_far, 0).reshape(inputs.shape)
    attn_line = Line(pack(attn_blocks), zi, count)
    dy_near, norm_now, attn_line.block, down_now = stage(
        up_line,
        swap(side(dy_now), "x"),
        norm_pair(across, swap(across, "c"), 1, norms, norm_now),
        attn_line.block,
        down_weight,
    )
    normed, mixed = norm_now
    attn_line.right, attn_line.left = [attn_line.block], [attn_line.block]

    attn_line.hop()
    up_rows, active, slope, dy_far, down_blocks = stage(
        attn_line,
        *up_forward(where, up_line, count, mixed, pick(up_bias.reshape(4, 1, -1), place, 0)),
        swap(dy_near, "y"),
        trade(rows_of(down_now), place),
    )

    attn_line.hop()
    dy_across = ordered(yi, dy_near, dy_far, 0).reshape(cotangent.shape)
    down_line = Line(pack(down_blocks), zi, count)
    dy_flat, down_line.block, active, lengths_pair, lengths_other = stage(
        attn_line,
        copy_pair(dy_across, swap(dy_across, "c"), 1, (dy_flat,)),
        down_line.block,
        active,
        lengths_pair,
        lengths_other,
    )

    attn_line.finish()
    lengths_all = jnp.concatenate([lengths_pair, lengths_other])
    begin = jax.vmap(lambda one: doc_start(one, jnp.arange(rows, dtype=jnp.int32)))(lengths_all)
    ordinal = jnp.arange(rows, dtype=jnp.int32)
    position = (ordinal - begin).astype(WIDE)
    exponent = jnp.arange(ROT // 2, dtype=WIDE) * (-2.0 / ROT)
    angle = position[..., None] * jnp.power(10000.0, exponent)
    angle = jnp.concatenate([angle, angle, jnp.zeros((4, rows, 128 - ROT), WIDE)], axis=-1)
    begin, cosine, sine, down_line.block, grad_down, dy_flat = stage(
        attn_line,
        begin[..., None],
        jnp.cos(angle),
        jnp.sin(angle),
        down_line.block,
        outer(dy_flat, active),
        dy_flat,
    )
    down_line.right, down_line.left = [down_line.block], [down_line.block]

    down_line.hop()
    attn_rows, heads, grad_projected, qkv_bias_term, grad_down = stage(
        down_line,
        *attention(
            where,
            attn_line,
            count,
            normed,
            dy_flat,
            pick(qkv_bias.reshape(4, 1, -1), place, 0),
            cosine,
            sine,
            begin,
        ),
        grad_down,
    )
    qkv_bias_term = qkv_bias_term[0]
    out_cols = attn_rows[:, head_width:]

    down_line.hop()
    down_sums = Sums(grad_down.reshape(count, -1, hidden_part), zi, count)
    down_sums.hop()
    grad_attn, heads, down_sums.right, down_sums.left = stage(
        down_line,
        outer(normed, grad_projected, dy_flat, heads),
        heads,
        down_sums.right,
        down_sums.left,
    )

    def first_terms(value, weight):
        return dot(value[2 * rows :], weight, ((1,), (1,))).astype(LOW)

    def own_terms(value, weight, sent):
        own = dot(value[: 2 * rows], weight, ((1,), (1,)))
        return (own + sent.astype(WIDE)).astype(LOW)

    down_line.finish()
    down_sums.hop()
    attn_sent = swap(first_terms(heads, out_cols), "c")
    attn_mine, grad_attn, down_sums.right, down_sums.left = stage(
        down_line,
        own_terms(heads, out_cols, attn_sent),
        grad_attn,
        down_sums.right,
        down_sums.left,
    )

    attn_part = lax.psum_scatter(grad_attn, "z", scatter_dimension=0, tiled=True)
    down_part = down_sums.finish()
    attn_over = cross_first(attn_mine, yi)
    down_rows, grad_hidden, up_bias_term, active = tie(
        *down_backward(where, down_line, count, dy_flat, slope), active
    )
    up_bias_term = up_bias_term[0]

    ffn_first = first_terms(active, down_rows)
    gains = norms[0::2]
    ffn_sent, sent, attn_over, active, grad_hidden = tie(
        swap(ffn_first, "c"),
        input_terms(
            2 * rows, grad_projected, after(grad_hidden, ffn_first), attn_rows, up_rows, gains, None
        ),
        attn_over,
        active,
        grad_hidden,
    )

    attn_over = cross_second(attn_mine, *attn_over, yi)
    sent_now = swap(sent, "c")
    ffn_mine, grad_hidden = tie(own_terms(active, down_rows, ffn_sent), grad_hidden)
    ffn_over = cross_first(ffn_mine, yi)
    grad_up, attn_over, sent_now = tie(outer(mixed, grad_hidden), attn_over, sent_now)
    attn_half = crossed(*attn_over)

    up_part = lax.psum_scatter(grad_up, "z", scatter_dimension=0, tiled=True)
    mine, ffn_over = tie(
        input_terms(0, grad_projected, grad_hidden, attn_rows, up_rows, gains, sent_now), ffn_over
    )

    input_over, ffn_over = tie(cross_first(mine, yi), cross_second(ffn_mine, *ffn_over, yi))
    attn_branch = attn_half + out_bias
    ffn_branch = crossed(*ffn_over) + down_bias
    x_half = own_half(inputs, yi).astype(WIDE)
    outputs, input_over, down_part, attn_branch, ffn_branch = tie(
        whole_rows((x_half + attn_branch + ffn_branch).astype(LOW), yi),
        cross_second(mine, *input_over, yi),
        down_part,
        attn_branch,
        ffn_branch,
    )
    input_half = crossed(*input_over)
    down_back = returned(down_part)

    centre_half = x_half - jnp.mean(x_half, axis=-1, keepdims=True)
    scale_half = lax.rsqrt(jnp.mean(centre_half * centre_half, axis=-1, keepdims=True) + EPS)
    unit_half = centre_half * scale_half
    back_half = scale_half * (
        input_half
        - jnp.mean(input_half, axis=-1, keepdims=True)
        - unit_half * jnp.mean(input_half * unit_half, axis=-1, keepdims=True)
    )
    back_rows = whole_rows(back_half.astype(LOW), yi)
    grad_inputs = cotangent.astype(WIDE) + back_rows.astype(WIDE)

    def norm_terms(weight, grad, bias_term, gain, shift):
        weight = weight.astype(WIDE)
        shift_term = jnp.sum(weight * bias_term, axis=1)
        gain_term = (jnp.sum(weight * grad.astype(WIDE), axis=1) - shift * shift_term) / gain
        return gain_term, shift_term

    gain1, shift1 = norm_terms(attn_rows[:, :head_width], grad_attn[:, :head_width], qkv_bias_term, norm1_gain, norm1_bias)
    gain2, shift2 = norm_terms(up_rows, grad_up, up_bias_term, norm2_gain, norm2_bias)
    slot = (jnp.arange(8, dtype=jnp.int32) == yi * 4 + place).astype(WIDE)[:, None]
    small = jnp.concatenate(
        [
            gain1,
            shift1,
            gain2,
            shift2,
            jnp.sum(cotangent, axis=0, dtype=WIDE) * 0.5,
            (slot * qkv_bias_term).reshape(-1),
            (slot * up_bias_term).reshape(-1),
            jnp.stack([jnp.sum(attn_branch * attn_branch), jnp.sum(ffn_branch * ffn_branch)]),
        ]
    )
    small = sum_everywhere(small, count)
    sizes = [width] * 5 + [8 * head_width, 8 * hidden_part]
    starts = [sum(sizes[:i]) for i in range(len(sizes) + 1)]
    pieces = [small[a:b] for a, b in zip(starts[:-1], starts[1:])]
    qkv_bias_sum = pick(pieces[5].reshape(2, 4, 3, HD), yi, 0)
    up_bias_sum = pick(pieces[6].reshape(2, 4 * hidden_part), yi, 0)
    rms_pair = jnp.sqrt(small[starts[-1] :] / float(rows * 4 * count * width))

    def placed(blocks, axis):
        size = blocks[0].shape[axis]
        shape = [4 * n if i == axis else n for i, n in enumerate(blocks[0].shape)]
        total = jnp.zeros(shape, WIDE)
        for step, block in enumerate(blocks):
            total = lax.dynamic_update_slice_in_dim(total, block, (place ^ step) * size, axis)
        return total

    def wide(blocks):
        return [block.astype(WIDE) for block in blocks]

    down_sum = placed([block.T for block in wide(down_back)], 0)
    attn_back = wide(returned(after(attn_part, small, *down_back)))
    qkv_sum = placed([block[:, None, :head_width] for block in attn_back], 1)
    qkv_sum = qkv_sum.reshape(part_rows, 4, 3, HD)
    out_sum = placed([block[:, head_width:].T[None] for block in attn_back], 0)
    up_sum = placed(wide(returned(after(up_part, *attn_back))), 1)
    return (
        outputs,
        grad_inputs,
        pieces[0],
        pieces[1],
        qkv_sum,
        qkv_bias_sum,
        out_sum,
        pieces[4],
        pieces[2],
        pieces[3],
        up_sum,
        up_bias_sum,
        down_sum,
        rms_pair[0],
        rms_pair[1],
    )


def solution(mesh):
    dp = mesh.shape["dp"]
    grid = Mesh(mesh.devices.reshape(dp // 4, 2, 2, mesh.shape["tensor"]), EVERY)
    dp = ("z", "x", "c")
    in_specs = (
        P(dp, None),
        P(dp, None),
        P(),
        P(),
        P(dp, "y", None, None),
        P("y", None, None),
        P("y", None, dp),
        P(),
        P(),
        P(),
        P(dp, "y"),
        P("y"),
        P("y", dp),
        P(),
        P(dp, None),
    )
    out_specs = (
        P(dp, None),
        P(dp, None),
        P(),
        P(),
        P(dp, "y", None, None),
        P("y", None, None),
        P("y", None, dp),
        P(),
        P(),
        P(),
        P(dp, "y"),
        P("y"),
        P("y", dp),
        P(),
        P(),
    )
    return jax.shard_map(
        per_device, mesh=grid, in_specs=in_specs, out_specs=out_specs, check_vma=False
    )
```

```python
import jax
import jax.numpy as jnp
from jax import lax
from jax.experimental import pallas as pl
from jax.experimental.pallas import tpu as pltpu
from jax.sharding import Mesh
from jax.sharding import PartitionSpec as P

HD = 256
ROT = 64
EPS = 1e-05
LOW = jnp.bfloat16
WIDE = jnp.float32
GROUP = ("x", "c")
EVERY = ("z", "x", "c", "y")


SMALL = pl.CostEstimate(flops=1 << 20, bytes_accessed=1 << 20, transcendentals=0)


def dot(left, right, dims):
    return lax.dot_general(left, right, (dims, ((), ())), preferred_element_type=WIDE)


def swap(value, axis):
    return lax.ppermute(value, axis, [(0, 1), (1, 0)])


def pick(value, index, axis):
    return lax.dynamic_index_in_dim(value, index, axis, keepdims=False)


def ordered(index, own, other, axis):
    first = jnp.where(index == 0, own, other)
    second = jnp.where(index == 0, other, own)
    return jnp.stack([first, second], axis=axis)


def trade(block, place):
    return [block(place)] + [
        lax.ppermute(block(place ^ step), GROUP, [(i, i ^ step) for i in range(4)])
        for step in range(1, 4)
    ]


class Line:
    def __init__(self, block, zi, count):
        self.block, self.zi, self.count = block, zi, count
        self.right, self.left = [block], [block]

    def hop(self, *waits):
        step, count = len(self.right), self.count
        if step == count:
            return
        right, left = after((self.right[-1], self.left[-1]), *waits)
        self.right.append(
            lax.ppermute(right, "z", [(i, i + 1) for i in range(step - 1, count - 1)])
        )
        self.left.append(lax.ppermute(left, "z", [(i, i - 1) for i in range(1, count - step + 1)]))

    def finish(self, *waits):
        while len(self.right) < self.count:
            self.hop(*waits)
        return self.right[-1], self.left[-1]

    def refs(self):
        return [self.block] + self.right[1:] + self.left[1:]


def add_kernel(index, term, *rest):
    received, results = rest[:-2], rest[-2:]
    for side in range(2):

        @pl.when(pl.program_id(0) == side)
        def _(side=side):
            value = term[0]
            if received:
                value = (value.astype(WIDE) + received[side][...].astype(WIDE)).astype(LOW)
            results[side][...] = value


def picked(terms, indices, received):
    _, rows, columns = terms.shape
    block = pl.BlockSpec((rows, columns), lambda i, index: (0, 0))
    return pl.pallas_call(
        add_kernel,
        grid_spec=pltpu.PrefetchScalarGridSpec(
            num_scalar_prefetch=1,
            grid=(2,),
            in_specs=[pl.BlockSpec((1, rows, columns), lambda i, index: (index[i], 0, 0))]
            + [block] * len(received),
            out_specs=[block] * 2,
        ),
        out_shape=[jax.ShapeDtypeStruct((rows, columns), LOW)] * 2,
        cost_estimate=SMALL,
    )(jnp.stack(indices), terms, *received)


class Sums:
    def __init__(self, terms, zi, count):
        self.terms, self.zi, self.count, self.step = terms, zi, count, 0
        self.right = self.left = None

    def terms_now(self):
        count, step = self.count, self.step + 1
        return picked(
            self.terms,
            (
                jnp.minimum(count - step + self.zi, count - 1),
                jnp.maximum(self.zi - (count - step), 0),
            ),
            () if self.right is None else (self.right, self.left),
        )

    def hop(self, ready=None):
        count, step = self.count, self.step + 1
        if step == count:
            return
        right, left = self.terms_now() if ready is None else ready
        self.step = step
        forth = [(i, i + 1) for i in range(min(step, count - 1))]
        back = [(count - 1 - i, count - 1 - j) for i, j in forth]
        self.right = lax.ppermute(right, "z", forth)
        self.left = lax.ppermute(left, "z", back)

    def finish(self):
        while self.step < self.count - 1:
            self.hop()
        own = pick(self.terms, self.zi, 0).astype(WIDE)
        return (own + self.right.astype(WIDE) + self.left.astype(WIDE)).astype(LOW)


def tie(*values):
    return lax.optimization_barrier(values)


def after(value, *waits):
    return lax.optimization_barrier((value, waits))[0] if waits else value


def cross_first(mine, over, yi):
    rows = mine.shape[0] // 2
    part = rows // 4
    last = [
        lax.dynamic_slice_in_dim(mine, start + (1 - yi) * part, part, 0)
        for start in (rows // 2, rows + rows // 2)
    ]
    return swap(over, "x"), swap(jnp.stack(last), "y")


def cross_kernel(yi, first, last, beyond, over_x, over_y, *rest):
    first_kept, first_sent, last_kept, last_sent, total = rest
    part = last.shape[0]

    def add(step, _):
        chunk = pl.ds(pl.multiple_of(step * 16, 16), 16)
        total[chunk, :] = (first[chunk, :].astype(WIDE) + over_x[chunk, :].astype(WIDE)).astype(LOW)
        return 0

    lax.fori_loop(0, first.shape[0] // 16, add, 0, unroll=4)
    first_kept[...] = total[pl.ds(pl.multiple_of(yi[0] * part, 16), part), :]
    first_sent[...] = total[pl.ds(pl.multiple_of((1 - yi[0]) * part, 16), part), :]

    def add_last(step, _):
        chunk = pl.ds(pl.multiple_of(step * 16, 16), 16)
        last_kept[chunk, :] = last[chunk, :].astype(WIDE) + over_y[0, chunk, :].astype(WIDE)
        value = beyond[chunk, :].astype(WIDE) + over_y[1, chunk, :].astype(WIDE)
        last_sent[chunk, :] = value.astype(LOW)
        return 0

    lax.fori_loop(0, part // 16, add_last, 0, unroll=2)


def cross_second(mine, over_x, over_y, yi):
    rows, width = mine.shape[0] // 2, mine.shape[1]
    part = rows // 4
    kept = jax.ShapeDtypeStruct((part, width), LOW)
    place = pl.BlockSpec((part, width), lambda i, yi: (0, 0))
    first, first_sent, last, last_sent = pl.pallas_call(
        cross_kernel,
        grid_spec=pltpu.PrefetchScalarGridSpec(
            num_scalar_prefetch=1,
            grid=(1,),
            in_specs=[
                pl.BlockSpec((2 * part, width), lambda i, yi: (0, 0)),
                pl.BlockSpec((part, width), lambda i, yi: (2 + yi[0], 0)),
                pl.BlockSpec((part, width), lambda i, yi: (6 + yi[0], 0)),
                pl.BlockSpec((2 * part, width), lambda i, yi: (0, 0)),
                pl.BlockSpec((2, part, width), lambda i, yi: (0, 0, 0)),
            ],
            out_specs=[place] * 4,
            scratch_shapes=[pltpu.VMEM((2 * part, width), LOW)],
        ),
        out_shape=[kept, kept, jax.ShapeDtypeStruct((part, width), WIDE), kept],
        cost_estimate=SMALL,
    )(yi.reshape(1), mine, mine, mine, over_x, over_y)
    return first, swap(first_sent, "y"), last, swap(last_sent, "x")


def crossed(own_first, sent_first, own_last, sent_last):
    return jnp.stack(
        [
            own_first.astype(WIDE) + sent_first.astype(WIDE),
            own_last + sent_last.astype(WIDE),
        ]
    )


def own_half(rows_in, yi):
    return pick(rows_in.reshape(2, 2, rows_in.shape[0] // 4, -1), yi, 1)


def whole_rows(half, yi):
    return ordered(yi, half, swap(half, "y"), 1).reshape(4 * half.shape[1], half.shape[2])


def norm_kernel(first, second, norms, *rest):
    normed, mixed, rows_in = rest[-3:]
    for index, ref in enumerate((first, second)):

        @pl.when(pl.program_id(0) == index)
        def _(ref=ref):
            rows_in[...] = ref[...]

    gain1, shift1, gain2, shift2 = [norms[i : i + 1, :] for i in range(4)]

    def norm(step, _):
        chunk = pl.ds(pl.multiple_of(step * 16, 16), 16)
        value = rows_in[chunk, :].astype(WIDE)
        centre = value - jnp.mean(value, axis=-1, keepdims=True)
        unit = centre * lax.rsqrt(jnp.mean(centre * centre, axis=-1, keepdims=True) + EPS)
        normed[chunk, :] = (unit * gain1 + shift1).astype(LOW)
        mixed[chunk, :] = (unit * gain2 + shift2).astype(LOW)
        return 0

    lax.fori_loop(0, rows_in.shape[0] // 16, norm, 0, unroll=4)


def norm_pair(first, second, offset, norms, before):
    rows, width = first.shape
    tile = rows // 2

    def out_place(s, t):
        return (2 * s + offset) * 2 + t, 0

    return pl.pallas_call(
        norm_kernel,
        grid=(2, 2),
        in_specs=[
            pl.BlockSpec((tile, width), lambda s, t: (jnp.where(s == 0, t, 1), 0)),
            pl.BlockSpec((tile, width), lambda s, t: (jnp.where(s == 0, 0, t), 0)),
            pl.BlockSpec((4, width), lambda s, t: (0, 0)),
        ]
        + [pl.BlockSpec(memory_space=pl.ANY)] * len(before),
        out_specs=[pl.BlockSpec((tile, width), out_place)] * 2,
        out_shape=[jax.ShapeDtypeStruct((4 * rows, width), LOW)] * 2,
        scratch_shapes=[pltpu.VMEM((tile, width), LOW)],
        input_output_aliases={3 + i: i for i in range(len(before))},
        cost_estimate=SMALL,
    )(first, second, norms, *before)


def copy_kernel(*refs):
    for index, ref in enumerate(refs[:2]):

        @pl.when(pl.program_id(0) == index)
        def _(ref=ref):
            refs[-1][...] = ref[...]


def copy_pair(first, second, offset, before):
    rows, width = first.shape
    tile = rows // 2
    return pl.pallas_call(
        copy_kernel,
        grid=(2, 2),
        in_specs=[
            pl.BlockSpec((tile, width), lambda s, t: (jnp.where(s == 0, t, 1), 0)),
            pl.BlockSpec((tile, width), lambda s, t: (jnp.where(s == 0, 0, t), 0)),
        ]
        + [pl.BlockSpec(memory_space=pl.ANY)] * len(before),
        out_specs=pl.BlockSpec((tile, width), lambda s, t: ((2 * s + offset) * 2 + t, 0)),
        out_shape=jax.ShapeDtypeStruct((4 * rows, width), LOW),
        input_output_aliases={2: 0} if before else {},
        cost_estimate=SMALL,
    )(first, second, *before)


def pack_kernel(*refs):
    rows = refs[0].shape[0]
    for index, ref in enumerate(refs[:-1]):
        refs[-1][index * rows : (index + 1) * rows, :] = ref[...]


def pack(blocks):
    rows, columns = blocks[0].shape
    return pl.pallas_call(
        pack_kernel,
        out_shape=jax.ShapeDtypeStruct((len(blocks) * rows, columns), LOW),
        cost_estimate=SMALL,
    )(*blocks)


def outer_kernel(*refs):
    result, pairs, start = refs[-1], refs[:-1], 0
    for left, right in zip(pairs[0::2], pairs[1::2]):
        columns = slice(start, start + right.shape[1])
        result[:, columns] = dot(left[...], right[...], ((0,), (0,))).astype(LOW)
        start = columns.stop


def outer(*arrays):
    tokens, width = arrays[0].shape
    tile = width // 4
    columns = sum(right.shape[1] for right in arrays[1::2])
    in_specs = []
    for right in arrays[1::2]:
        in_specs += [
            pl.BlockSpec((tokens, tile), lambda i: (0, i)),
            pl.BlockSpec(right.shape, lambda i: (0, 0), pipeline_mode=pl.Buffered(1)),
        ]
    return pl.pallas_call(
        outer_kernel,
        grid=(4,),
        in_specs=in_specs,
        out_specs=pl.BlockSpec((tile, columns), lambda i: (i, 0)),
        out_shape=jax.ShapeDtypeStruct((width, columns), LOW),
        cost_estimate=SMALL,
    )(*arrays)


def collect(where, refs, count, full, result, copies, kept):
    zi, place = where[0], where[1]
    rows = full.shape[1]

    def move(ref, base, block):
        for step in range(4):
            pltpu.make_async_copy(
                ref.at[pl.ds(base + step * rows, rows)],
                full.at[4 * block + (place ^ step)],
                copies.at[4 * block + step],
            ).start()

    for block in range(count):
        if len(refs) == 1:
            move(refs[0], block * 4 * rows, block)
            continue
        for step in range(count):
            pairs = [(step, block + step), (count - 1 + step, block - step)]
            for index, owner in pairs[: 2 if step else 1]:
                if 0 <= owner < count:

                    @pl.when(zi == owner)
                    def _(index=index):
                        move(refs[index], 0, block)

    for block in range(count):
        for step in range(4):
            pltpu.make_async_copy(
                refs[0].at[pl.ds(0, rows)],
                full.at[4 * block + (place ^ step)],
                copies.at[4 * block + step],
            ).wait()
    pltpu.make_async_copy(full, result, kept).start()


def weighted_call(kernel, where, gathered, count, operands, in_specs, out_specs, out_shape, grid, scratch):
    refs = gathered.refs() if isinstance(gathered, Line) else [gathered]
    rows, columns = refs[0].shape
    rows = rows // 4 if len(refs) > 1 else rows // (4 * count)
    last = grid[0] - 1

    def body(where_ref, *args):
        parts, args = args[: len(refs)], args[len(refs) :]
        inputs, args = args[: len(operands)], args[len(operands) :]
        result, args = args[0], args[1:]
        full, copies, kept = args[-3:]

        @pl.when(pl.program_id(0) == 0)
        def _():
            collect(where_ref, parts, count, full, result, copies, kept)

        kernel(full, *inputs, *args[:-3])

        @pl.when(pl.program_id(0) == last)
        def _():
            pltpu.make_async_copy(full, result, kept).wait()

    result = pl.pallas_call(
        body,
        grid_spec=pltpu.PrefetchScalarGridSpec(
            num_scalar_prefetch=1,
            grid=grid,
            in_specs=[pl.BlockSpec(memory_space=pl.ANY)] * len(refs) + in_specs,
            out_specs=[pl.BlockSpec(memory_space=pl.ANY)] + out_specs,
            scratch_shapes=scratch
            + [
                pltpu.VMEM((4 * count, rows, columns), LOW),
                pltpu.SemaphoreType.DMA((4 * count,)),
                pltpu.SemaphoreType.DMA,
            ],
        ),
        out_shape=[jax.ShapeDtypeStruct((4 * count, rows, columns), LOW)] + out_shape,
        cost_estimate=SMALL,
    )(where, *refs, *operands)
    return [result[0].reshape(4 * count * rows, columns)] + list(result[1:])


def up_kernel(full, mixed, bias, active, slope):
    weight = full.reshape(full.shape[0] * full.shape[1], full.shape[2])
    for start in range(0, weight.shape[1], 256):
        columns = slice(start, start + 256)
        hidden = dot(mixed[...], weight[:, columns], ((1,), (0,))) + bias[:, columns]
        cdf = 0.5 * (1.0 + lax.erf(hidden * (0.5**0.5)))
        density = jnp.exp(-0.5 * hidden * hidden) * 0.3989422804014327
        active[:, columns] = (hidden * cdf).astype(LOW)
        slope[:, columns] = (cdf + hidden * density).astype(LOW)


def up_forward(where, gathered, count, mixed, bias):
    tokens, width = mixed.shape
    columns = bias.shape[1]
    tile = tokens // 8

    def rows_of(size):
        return pl.BlockSpec((tile, size), lambda i, z: (i, 0))

    return weighted_call(
        up_kernel,
        where,
        gathered,
        count,
        (mixed, bias),
        [rows_of(width), pl.BlockSpec((1, columns), lambda i, z: (0, 0))],
        [rows_of(columns)] * 2,
        [jax.ShapeDtypeStruct((tokens, columns), LOW)] * 2,
        (8,),
        [],
    )


def down_kernel(full, dy, slope, grad, total):
    weight = full.reshape(full.shape[0] * full.shape[1], full.shape[2])

    @pl.when(pl.program_id(0) == 0)
    def _():
        total[...] = jnp.zeros_like(total)

    for start in range(0, weight.shape[1], 256):
        columns = slice(start, start + 256)
        value = dot(dy[...], weight[:, columns], ((1,), (0,))) * slope[:, columns].astype(WIDE)
        value = value.astype(LOW)
        grad[:, columns] = value
        total[:, columns] += jnp.sum(value.astype(WIDE), axis=0, keepdims=True)


def down_backward(where, gathered, count, dy, slope):
    tokens, width = dy.shape
    columns = slope.shape[1]
    tile = tokens // 8

    def rows_of(size):
        return pl.BlockSpec((tile, size), lambda i, z: (i, 0))

    return weighted_call(
        down_kernel,
        where,
        gathered,
        count,
        (dy, slope),
        [rows_of(width), rows_of(columns)],
        [rows_of(columns), pl.BlockSpec((1, columns), lambda i, z: (0, 0))],
        [
            jax.ShapeDtypeStruct((tokens, columns), LOW),
            jax.ShapeDtypeStruct((1, columns), WIDE),
        ],
        (8,),
        [],
    )


def sum_specs(tile, width, sent):
    rows = pl.BlockSpec((tile, width), lambda i: (i, 0))
    shape = jax.ShapeDtypeStruct((4 * tile, width), LOW)
    if sent is None:
        return [], rows, shape
    one = pl.BlockSpec((tile, width), lambda i: (0, 0))
    return [rows], [rows, one], [shape, jax.ShapeDtypeStruct((tile, width), LOW)]


def put_sum(term, columns, rest):
    if len(rest) == 1:
        rest[0][:, columns] = term.astype(LOW)
        return
    sent, result, over = rest
    value = (term + sent[:, columns].astype(WIDE)).astype(LOW)
    result[:, columns] = value

    @pl.when(pl.program_id(0) == 2)
    def _():
        over[:, columns] = value


def branch_kernel(value, weight, *rest):
    for start in range(0, weight.shape[0], 512):
        columns = slice(start, start + 512)
        term = dot(value[...], weight[columns, weight.shape[1] - value.shape[1] :], ((1,), (1,)))
        put_sum(term, columns, rest)


def branch_terms(first, value, weight, sent):
    tokens, width = value.shape[0] // 2, weight.shape[0]
    tile = tokens // 4
    skip = first // tile
    extra_specs, out_specs, out_shape = sum_specs(tile, width, sent)
    return pl.pallas_call(
        branch_kernel,
        grid=(4,),
        in_specs=[
            pl.BlockSpec((tile, value.shape[1]), lambda i: (i + skip, 0)),
            pl.BlockSpec(weight.shape, lambda i: (0, 0), pipeline_mode=pl.Buffered(1)),
        ]
        + extra_specs,
        out_specs=out_specs,
        out_shape=out_shape,
        cost_estimate=SMALL,
    )(value, weight, *(() if sent is None else (sent,)))


def input_kernel(attn, hidden, attn_weight, up_weight, gains, *rest):
    for start in range(0, gains.shape[1], 512):
        columns = slice(start, start + 512)
        value = (
            dot(attn[...], attn_weight[columns, : attn.shape[1]], ((1,), (1,))) * gains[0:1, columns]
        )
        value += dot(hidden[...], up_weight[columns, :], ((1,), (1,))) * gains[1:2, columns]
        put_sum(value, columns, rest)


def input_terms(first, attn, hidden, attn_weight, up_weight, gains, sent):
    tokens = attn.shape[0] // 2
    width = gains.shape[1]
    tile = tokens // 4
    skip = first // tile

    def rows_of(size, start):
        return pl.BlockSpec((tile, size), lambda i: (i + start, 0))

    def whole(array):
        return pl.BlockSpec(array.shape, lambda i: (0, 0), pipeline_mode=pl.Buffered(1))

    extra_specs, out_specs, out_shape = sum_specs(tile, width, sent)
    return pl.pallas_call(
        input_kernel,
        grid=(4,),
        in_specs=[
            rows_of(attn.shape[1], skip),
            rows_of(hidden.shape[1], skip),
            whole(attn_weight),
            whole(up_weight),
            whole(gains),
        ]
        + extra_specs,
        out_specs=out_specs,
        out_shape=out_shape,
        cost_estimate=SMALL,
    )(attn, hidden, attn_weight, up_weight, gains, *(() if sent is None else (sent,)))


def attention_kernel(full, normed, dy, bias, cosine, sine, begin, heads, grad, total, *scratch):
    q_s, k_s, v_s, g_s, dk_s, dv_s = scratch
    weight = full.reshape(full.shape[0] * full.shape[1], full.shape[2])
    rows = normed.shape[0]
    lane = lax.broadcasted_iota(jnp.int32, (1, 128), 1)
    scale = HD ** (-0.5)

    def turn(value, sign):
        low = value[:, :128]
        sine_now = sine[0] * sign
        ahead = pltpu.roll(low, 128 - ROT // 2, 1) * jnp.where(lane < ROT // 2, -sine_now, 0.0)
        behind = pltpu.roll(low, ROT // 2, 1) * jnp.where(lane < ROT // 2, 0.0, sine_now)
        return jnp.concatenate([low * cosine[0] + ahead + behind, value[:, 128:]], axis=1)

    def project(index):
        columns = slice(index * HD, (index + 1) * HD)
        return dot(normed[...], weight[:, columns], ((1,), (0,))) + bias[:, columns]

    q_s[...] = turn(project(0), 1.0).astype(LOW)
    k_s[...] = turn(project(1), 1.0).astype(LOW)
    v_s[...] = project(2).astype(LOW)
    g_s[...] = dot(dy[...], weight[:, 3 * HD :], ((1,), (0,))).astype(LOW)
    dk_s[...] = jnp.zeros_like(dk_s)
    dv_s[...] = jnp.zeros_like(dv_s)
    tile = 320
    for start in range(0, rows, tile):
        here, seen = slice(start, start + tile), slice(0, start + tile)
        query, grad_heads = q_s[here, :], g_s[here, :]
        keys, value = k_s[seen, :], v_s[seen, :]
        scores = dot(query, keys, ((1,), (1,))) * scale
        column = lax.broadcasted_iota(jnp.int32, scores.shape, 1)
        row = lax.broadcasted_iota(jnp.int32, scores.shape, 0) + start
        allowed = (column <= row) & (column >= begin[0, here, :])
        scores = jnp.where(allowed, scores, -1e30)
        shifted = jnp.exp(scores - jnp.max(scores, axis=1, keepdims=True))
        prob = shifted / jnp.sum(shifted, axis=1, keepdims=True)
        low = prob.astype(LOW)
        heads[here, :] = dot(low, value, ((1,), (0,))).astype(LOW)
        grad_prob = dot(grad_heads, value, ((1,), (1,)))
        weighted = jnp.sum(grad_prob * prob, axis=1, keepdims=True)
        grad_scores = (prob * (grad_prob - weighted) * scale).astype(LOW)
        grad_query = dot(grad_scores, keys, ((1,), (0,)))
        cos_here = cosine[0, here, :]
        sine_here = -sine[0, here, :]
        head = grad_query[:, :128]
        ahead = pltpu.roll(head, 128 - ROT // 2, 1) * jnp.where(lane < ROT // 2, -sine_here, 0.0)
        behind = pltpu.roll(head, ROT // 2, 1) * jnp.where(lane < ROT // 2, 0.0, sine_here)
        grad[here, :128] = (head * cos_here + ahead + behind).astype(LOW)
        grad[here, 128:HD] = grad_query[:, 128:].astype(LOW)
        dk_s[seen, :] += dot(grad_scores, query, ((0,), (0,)))
        dv_s[seen, :] += dot(low, grad_heads, ((0,), (0,)))
    grad[:, HD : 2 * HD] = turn(dk_s[...], -1.0).astype(LOW)
    grad[:, 2 * HD :] = dv_s[...].astype(LOW)

    @pl.when(pl.program_id(0) == 0)
    def _():
        total[...] = jnp.zeros_like(total)

    total[...] += jnp.sum(grad[...].astype(WIDE), axis=0, keepdims=True)


def attention(where, gathered, count, normed, dy, bias, cosine, sine, begin):
    tokens, width = normed.shape
    rows = tokens // 4

    def per_sequence(size):
        return pl.BlockSpec((rows, size), lambda s, z: (s, 0))

    def table(size):
        return pl.BlockSpec((1, rows, size), lambda s, z: (s, 0, 0))

    row = pl.BlockSpec((1, 3 * HD), lambda s, z: (0, 0))
    return weighted_call(
        attention_kernel,
        where,
        gathered,
        count,
        (normed, dy, bias, cosine, sine, begin),
        [per_sequence(width), per_sequence(width), row, table(128), table(128), table(1)],
        [per_sequence(HD), per_sequence(3 * HD), row],
        [
            jax.ShapeDtypeStruct((tokens, HD), LOW),
            jax.ShapeDtypeStruct((tokens, 3 * HD), LOW),
            jax.ShapeDtypeStruct((1, 3 * HD), WIDE),
        ],
        (4,),
        [pltpu.VMEM((rows, HD), LOW)] * 4 + [pltpu.VMEM((rows, HD), WIDE)] * 2,
    )


def sum_line(value, count):
    step = 1
    while step < count:
        value = value + lax.ppermute(value, "z", [(i, i ^ step) for i in range(count)])
        step *= 2
    return value


def doc_start(lengths, place):
    passed = place[:, None] >= jnp.cumsum(lengths)[None, :]
    return jnp.sum(jnp.where(passed, lengths[None, :], 0), axis=1)


def per_device(
    inputs,
    doc_lengths,
    norm1_gain,
    norm1_bias,
    qkv_weight,
    qkv_bias,
    out_weight,
    out_bias,
    norm2_gain,
    norm2_bias,
    up_weight,
    up_bias,
    down_weight,
    down_bias,
    cotangent,
):
    rows, width = inputs.shape
    count = lax.axis_size("z")
    zi, xi, ci, yi = [lax.axis_index(axis) for axis in EVERY]
    place = xi * 2 + ci
    hidden_part = up_bias.shape[0] // 4
    part_rows = up_weight.shape[0]
    head_width = 3 * HD

    norms = jnp.stack([norm1_gain, norm1_bias, norm2_gain, norm2_bias])

    def columns_of(weight):
        return lambda t: lax.dynamic_slice_in_dim(weight, t * hidden_part, hidden_part, 1)

    def rows_of(weight):
        return lambda t: lax.dynamic_slice_in_dim(weight, t * hidden_part, hidden_part, 0).T

    def heads_of(qkv, out):
        return lambda t: jnp.concatenate(
            [pick(qkv, t, 1).reshape(part_rows, head_width), pick(out, t, 0).T], axis=1
        )

    def returned(part):
        return trade(
            lambda t: lax.dynamic_slice_in_dim(part, t * part_rows, part_rows, 0), place
        )

    where = jnp.stack([zi, place])
    half = rows // 2

    def side(array):
        return lax.dynamic_slice_in_dim(array, yi * half, half, 0)

    def stage(line, *values):
        line.right[-1], line.left[-1], values = tie(line.right[-1], line.left[-1], values)
        return values

    up_blocks = trade(columns_of(up_weight), place)
    up_blocks, x_now, x_beside, dy_beside, lengths_x = tie(
        up_blocks, inputs, swap(inputs, "c"), swap(cotangent, "c"), swap(doc_lengths, "x")
    )

    up_line = Line(pack(up_blocks), zi, count)
    up_line.hop()
    x_near = swap(side(after(x_now, up_line.block)), "x")
    norm_now, weights_now, lengths_x, lengths_now, dy_now = stage(
        up_line,
        norm_pair(x_now, x_beside, 0, norms, ()),
        (qkv_weight, out_weight),
        lengths_x,
        doc_lengths,
        (cotangent, dy_beside),
    )

    up_line.hop()
    x_far = swap(after(x_near, lengths_x), "y")
    lengths_pair = jnp.concatenate([lengths_now, lengths_x])
    attn_blocks, lengths_other, dy_flat, dy_now = stage(
        up_line,
        trade(heads_of(*weights_now), place),
        swap(lengths_pair, "c"),
        copy_pair(*dy_now, 0, ()),
        cotangent,
    )

    up_line.finish()
    dy_near = swap(side(dy_now), "x")
    across = ordered(yi, x_near, after(x_far, attn_blocks[0]), 0).reshape(inputs.shape)
    attn_line = Line(pack(attn_blocks), zi, count)
    norm_now, attn_line.block, down_now = stage(
        up_line,
        norm_pair(across, swap(across, "c"), 1, norms, norm_now),
        attn_line.block,
        down_weight,
    )
    normed, mixed = norm_now
    attn_line.right, attn_line.left = [attn_line.block], [attn_line.block]

    attn_line.hop()
    dy_far = swap(after(dy_near, mixed), "y")
    up_rows, active, slope, down_blocks = stage(
        attn_line,
        *up_forward(where, up_line, count, mixed, pick(up_bias.reshape(4, 1, -1), place, 0)),
        trade(rows_of(down_now), place),
    )

    attn_line.hop()
    dy_across = ordered(yi, dy_near, after(dy_far, active), 0).reshape(cotangent.shape)
    down_line = Line(pack(down_blocks), zi, count)
    dy_flat = copy_pair(dy_across, swap(dy_across, "c"), 1, (dy_flat,))
    dy_flat, down_line.block, grad_down, lengths_pair, lengths_other = stage(
        attn_line,
        dy_flat,
        down_line.block,
        outer(dy_flat, active),
        lengths_pair,
        lengths_other,
    )

    attn_line.finish()
    lengths_all = jnp.concatenate([lengths_pair, lengths_other])
    begin = jax.vmap(lambda one: doc_start(one, jnp.arange(rows, dtype=jnp.int32)))(lengths_all)
    ordinal = jnp.arange(rows, dtype=jnp.int32)
    position = (ordinal - begin).astype(WIDE)
    exponent = jnp.arange(ROT // 2, dtype=WIDE) * (-2.0 / ROT)
    angle = position[..., None] * jnp.power(10000.0, exponent)
    angle = jnp.concatenate([angle, angle, jnp.zeros((4, rows, 128 - ROT), WIDE)], axis=-1)
    down_sums = Sums(grad_down.reshape(count, -1, hidden_part), zi, count)
    begin, cosine, sine, down_line.block, down_sums.terms, ready, dy_flat, attn_bias = stage(
        attn_line,
        begin[..., None],
        jnp.cos(angle),
        jnp.sin(angle),
        down_line.block,
        down_sums.terms,
        down_sums.terms_now(),
        dy_flat,
        pick(qkv_bias.reshape(4, 1, -1), place, 0),
    )
    down_line.right, down_line.left = [down_line.block], [down_line.block]

    down_line.hop()
    down_sums.hop(ready)
    attn_rows, heads, grad_projected, qkv_bias_term, down_sums.right, down_sums.left = stage(
        down_line,
        *attention(
            where, attn_line, count, normed, dy_flat, attn_bias, cosine, sine, begin
        ),
        down_sums.right,
        down_sums.left,
    )
    qkv_bias_term = qkv_bias_term[0]

    def first_terms(value, weight):
        return branch_terms(2 * rows, value, weight, None)

    def own_terms(value, weight, sent):
        return branch_terms(0, value, weight, sent)

    down_line.hop()
    grad_attn, heads, attn_first, ready, down_sums.terms = stage(
        down_line,
        outer(normed, grad_projected, dy_flat, heads),
        heads,
        first_terms(heads, attn_rows),
        down_sums.terms_now(),
        down_sums.terms,
    )

    down_line.finish()
    down_sums.hop(ready)
    grad_attn, attn_mine, down_sums.right, down_sums.left = stage(
        down_line,
        grad_attn,
        own_terms(heads, attn_rows, swap(attn_first, "c")),
        down_sums.right,
        down_sums.left,
    )

    attn_part = lax.psum_scatter(grad_attn, "z", scatter_dimension=0, tiled=True)
    attn_over = cross_first(*attn_mine, yi)
    down_rows, grad_hidden, up_bias_term = down_backward(where, down_line, count, dy_flat, slope)
    up_bias_term = up_bias_term[0]
    grad_hidden, ffn_first, active, attn_over = tie(
        grad_hidden, first_terms(active, down_rows), active, attn_over
    )

    gains = norms[0::2]
    attn_over = cross_second(attn_mine[0], *attn_over, yi)
    sent, ffn_sent, grad_hidden, active = tie(
        input_terms(
            2 * rows, grad_projected, after(grad_hidden, attn_over[0]), attn_rows, up_rows, gains, None
        ),
        swap(ffn_first, "c"),
        grad_hidden,
        active,
    )

    ffn_mine, sent_now, attn_over, grad_hidden, down_sums.right, down_sums.left = tie(
        own_terms(active, down_rows, ffn_sent),
        swap(sent, "c"),
        attn_over,
        grad_hidden,
        down_sums.right,
        down_sums.left,
    )
    attn_half = crossed(*attn_over)

    down_sums.hop()
    ffn_over = cross_first(*ffn_mine, yi)
    mine = input_terms(0, grad_projected, grad_hidden, attn_rows, up_rows, gains, sent_now)
    mine, ffn_over, grad_hidden = tie(mine, ffn_over, grad_hidden)

    grad_up = outer(mixed, grad_hidden)
    up_part = lax.psum_scatter(grad_up, "z", scatter_dimension=0, tiled=True)

    def norm_terms(weight, grad, bias_term, gain, shift):
        weight = weight.astype(WIDE)
        shift_term = jnp.sum(weight * bias_term, axis=1)
        gain_term = (jnp.sum(weight * grad.astype(WIDE), axis=1) - shift * shift_term) / gain
        return gain_term, shift_term

    input_over = cross_first(*mine, yi)
    input_over, ffn_over, norm1_terms, norm2_terms, down_part = tie(
        input_over,
        cross_second(ffn_mine[0], *ffn_over, yi),
        norm_terms(
            attn_rows[:, :head_width], grad_attn[:, :head_width], qkv_bias_term, norm1_gain, norm1_bias
        ),
        norm_terms(up_rows, grad_up, up_bias_term, norm2_gain, norm2_bias),
        down_sums.finish(),
    )
    (gain1, shift1), (gain2, shift2) = norm1_terms, norm2_terms

    input_over = cross_second(mine[0], *input_over, yi)
    x_half = own_half(inputs, yi).astype(WIDE)
    attn_branch = attn_half + out_bias
    ffn_branch = crossed(*ffn_over) + down_bias
    slot = (jnp.arange(8, dtype=jnp.int32) == yi * 4 + place).astype(WIDE)[:, None]
    small = jnp.concatenate(
        [
            gain1,
            shift1,
            gain2,
            shift2,
            jnp.sum(cotangent, axis=0, dtype=WIDE) * 0.5,
            (slot * qkv_bias_term).reshape(-1),
            (slot * up_bias_term).reshape(-1),
            jnp.stack([jnp.sum(attn_branch * attn_branch), jnp.sum(ffn_branch * ffn_branch)]),
        ]
    )
    def placed(blocks, axis):
        size = blocks[0].shape[axis]
        shape = [4 * n if i == axis else n for i, n in enumerate(blocks[0].shape)]
        total = jnp.zeros(shape, WIDE)
        for step, block in enumerate(blocks):
            total = lax.dynamic_update_slice_in_dim(total, block, (place ^ step) * size, axis)
        return total

    def wide(blocks):
        return [block.astype(WIDE) for block in blocks]

    small, input_over, attn_branch, ffn_branch = tie(
        small + swap(small, "y"), input_over, attn_branch, ffn_branch
    )
    outputs = whole_rows((x_half + attn_branch + ffn_branch).astype(LOW), yi)
    input_half = crossed(*input_over)
    centre_half = x_half - jnp.mean(x_half, axis=-1, keepdims=True)
    scale_half = lax.rsqrt(jnp.mean(centre_half * centre_half, axis=-1, keepdims=True) + EPS)
    unit_half = centre_half * scale_half
    back_half = scale_half * (
        input_half
        - jnp.mean(input_half, axis=-1, keepdims=True)
        - unit_half * jnp.mean(input_half * unit_half, axis=-1, keepdims=True)
    )
    back_low = back_half.astype(LOW)
    back_rows = whole_rows(back_low, yi)
    small = after(small, back_low)
    for axis in ("c", "x"):
        small = small + swap(small, axis)
    small = sum_line(small, count)
    down_back = returned(after(down_part, back_low))
    attn_back = returned(after(attn_part, *down_back))
    down_sum = placed([block.T for block in wide(down_back)], 0)
    back_rows, attn_back, up_back, down_sum, small, outputs = tie(
        back_rows, attn_back, returned(after(up_part, *attn_back)), down_sum, small, outputs
    )
    grad_inputs = cotangent.astype(WIDE) + back_rows.astype(WIDE)

    sizes = [width] * 5 + [8 * head_width, 8 * hidden_part]
    starts = [sum(sizes[:i]) for i in range(len(sizes) + 1)]
    pieces = [small[a:b] for a, b in zip(starts[:-1], starts[1:])]
    qkv_bias_sum = pick(pieces[5].reshape(2, 4, 3, HD), yi, 0)
    up_bias_sum = pick(pieces[6].reshape(2, 4 * hidden_part), yi, 0)
    rms_pair = jnp.sqrt(small[starts[-1] :] / float(rows * 4 * count * width))

    attn_back = wide(attn_back)
    qkv_sum = placed([block[:, None, :head_width] for block in attn_back], 1)
    qkv_sum = qkv_sum.reshape(part_rows, 4, 3, HD)
    out_sum = placed([block[:, head_width:].T[None] for block in attn_back], 0)
    up_sum = placed(wide(up_back), 1)
    return (
        outputs,
        grad_inputs,
        pieces[0],
        pieces[1],
        qkv_sum,
        qkv_bias_sum,
        out_sum,
        pieces[4],
        pieces[2],
        pieces[3],
        up_sum,
        up_bias_sum,
        down_sum,
        rms_pair[0],
        rms_pair[1],
    )


def solution(mesh):
    dp = mesh.shape["dp"]
    grid = Mesh(mesh.devices.reshape(dp // 4, 2, 2, mesh.shape["tensor"]), EVERY)
    dp = ("z", "x", "c")
    in_specs = (
        P(dp, None),
        P(dp, None),
        P(),
        P(),
        P(dp, "y", None, None),
        P("y", None, None),
        P("y", None, dp),
        P(),
        P(),
        P(),
        P(dp, "y"),
        P("y"),
        P("y", dp),
        P(),
        P(dp, None),
    )
    out_specs = (
        P(dp, None),
        P(dp, None),
        P(),
        P(),
        P(dp, "y", None, None),
        P("y", None, None),
        P("y", None, dp),
        P(),
        P(),
        P(),
        P(dp, "y"),
        P("y"),
        P("y", dp),
        P(),
        P(),
    )
    return jax.shard_map(
        per_device, mesh=grid, in_specs=in_specs, out_specs=out_specs, check_vma=False
    )
```

```python
import jax
import jax.numpy as jnp
from jax import lax
from jax.experimental import pallas as pl
from jax.experimental.pallas import tpu as pltpu
from jax.sharding import Mesh
from jax.sharding import PartitionSpec as P

HD = 256
ROT = 64
EPS = 1e-05
LOW = jnp.bfloat16
WIDE = jnp.float32
GROUP = ("x", "c")
EVERY = ("z", "x", "c", "y")


SMALL = pl.CostEstimate(flops=1 << 20, bytes_accessed=1 << 20, transcendentals=0)


def dot(left, right, dims):
    return lax.dot_general(left, right, (dims, ((), ())), preferred_element_type=WIDE)


def swap(value, axis):
    return lax.ppermute(value, axis, [(0, 1), (1, 0)])


def pick(value, index, axis):
    return lax.dynamic_index_in_dim(value, index, axis, keepdims=False)


def ordered(index, own, other, axis):
    first = jnp.where(index == 0, own, other)
    second = jnp.where(index == 0, other, own)
    return jnp.stack([first, second], axis=axis)


def trade(block, place):
    return traded([block(place ^ step) for step in range(4)])


def traded(blocks):
    return blocks[:1] + [
        lax.ppermute(blocks[step], GROUP, [(i, i ^ step) for i in range(4)])
        for step in range(1, 4)
    ]


class Line:
    def __init__(self, block, zi, count):
        self.block, self.zi, self.count = block, zi, count
        self.right, self.left = [block], [block]

    def hop(self, *waits):
        step, count = len(self.right), self.count
        if step == count:
            return
        right, left = after((self.right[-1], self.left[-1]), *waits)
        self.right.append(
            lax.ppermute(right, "z", [(i, i + 1) for i in range(step - 1, count - 1)])
        )
        self.left.append(lax.ppermute(left, "z", [(i, i - 1) for i in range(1, count - step + 1)]))

    def finish(self, *waits):
        while len(self.right) < self.count:
            self.hop(*waits)
        return self.right[-1], self.left[-1]

    def refs(self):
        return [self.block] + self.right[1:] + self.left[1:]


def tie(*values):
    return lax.optimization_barrier(values)


def after(value, *waits):
    return lax.optimization_barrier((value, waits))[0] if waits else value


def cross_rows(mine, yi):
    rows = mine.shape[0] // 2
    part = rows // 4
    return jnp.stack(
        [
            lax.dynamic_slice_in_dim(mine, start + (1 - yi) * part, part, 0)
            for start in (rows // 2, rows + rows // 2)
        ]
    )


def cross_first(over, last):
    return swap(over, "x"), swap(last, "y")


def cross_kernel(yi, first, last, beyond, over_x, over_y, *rest):
    first_kept, first_sent, last_kept, last_sent, total = rest
    part = last.shape[0]

    def add(step, _):
        chunk = pl.ds(pl.multiple_of(step * 16, 16), 16)
        total[chunk, :] = (first[chunk, :].astype(WIDE) + over_x[chunk, :].astype(WIDE)).astype(LOW)
        return 0

    lax.fori_loop(0, first.shape[0] // 16, add, 0, unroll=4)
    first_kept[...] = total[pl.ds(pl.multiple_of(yi[0] * part, 16), part), :]
    first_sent[...] = total[pl.ds(pl.multiple_of((1 - yi[0]) * part, 16), part), :]

    def add_last(step, _):
        chunk = pl.ds(pl.multiple_of(step * 16, 16), 16)
        last_kept[chunk, :] = last[chunk, :].astype(WIDE) + over_y[0, chunk, :].astype(WIDE)
        value = beyond[chunk, :].astype(WIDE) + over_y[1, chunk, :].astype(WIDE)
        last_sent[chunk, :] = value.astype(LOW)
        return 0

    lax.fori_loop(0, part // 16, add_last, 0, unroll=2)


def cross_second(mine, over_x, over_y, yi):
    rows, width = mine.shape[0] // 2, mine.shape[1]
    part = rows // 4
    kept = jax.ShapeDtypeStruct((part, width), LOW)
    place = pl.BlockSpec((part, width), lambda i, yi: (0, 0))
    first, first_sent, last, last_sent = pl.pallas_call(
        cross_kernel,
        grid_spec=pltpu.PrefetchScalarGridSpec(
            num_scalar_prefetch=1,
            grid=(1,),
            in_specs=[
                pl.BlockSpec((2 * part, width), lambda i, yi: (0, 0)),
                pl.BlockSpec((part, width), lambda i, yi: (2 + yi[0], 0)),
                pl.BlockSpec((part, width), lambda i, yi: (6 + yi[0], 0)),
                pl.BlockSpec((2 * part, width), lambda i, yi: (0, 0)),
                pl.BlockSpec((2, part, width), lambda i, yi: (0, 0, 0)),
            ],
            out_specs=[place] * 4,
            scratch_shapes=[pltpu.VMEM((2 * part, width), LOW)],
        ),
        out_shape=[kept, kept, jax.ShapeDtypeStruct((part, width), WIDE), kept],
        cost_estimate=SMALL,
    )(yi.reshape(1), mine, mine, mine, over_x, over_y)
    return first, swap(first_sent, "y"), last, swap(last_sent, "x")


def crossed(own_first, sent_first, own_last, sent_last):
    return jnp.stack(
        [
            own_first.astype(WIDE) + sent_first.astype(WIDE),
            own_last + sent_last.astype(WIDE),
        ]
    )


def own_half(rows_in, yi):
    return pick(rows_in.reshape(2, 2, rows_in.shape[0] // 4, -1), yi, 1)


def whole_rows(half, other, yi):
    return ordered(yi, half, other, 1).reshape(4 * half.shape[1], half.shape[2])


def norm_kernel(first, second, norms, *rest):
    normed, mixed, rows_in = rest[-3:]
    for index, ref in enumerate((first, second)):

        @pl.when(pl.program_id(0) == index)
        def _(ref=ref):
            rows_in[...] = ref[...]

    gain1, shift1, gain2, shift2 = [norms[i : i + 1, :] for i in range(4)]

    def norm(step, _):
        chunk = pl.ds(pl.multiple_of(step * 16, 16), 16)
        value = rows_in[chunk, :].astype(WIDE)
        centre = value - jnp.mean(value, axis=-1, keepdims=True)
        unit = centre * lax.rsqrt(jnp.mean(centre * centre, axis=-1, keepdims=True) + EPS)
        normed[chunk, :] = (unit * gain1 + shift1).astype(LOW)
        mixed[chunk, :] = (unit * gain2 + shift2).astype(LOW)
        return 0

    lax.fori_loop(0, rows_in.shape[0] // 16, norm, 0, unroll=4)


def norm_pair(first, second, offset, norms, before):
    rows, width = first.shape
    tile = rows // 2

    def out_place(s, t):
        return (2 * s + offset) * 2 + t, 0

    return pl.pallas_call(
        norm_kernel,
        grid=(2, 2),
        in_specs=[
            pl.BlockSpec((tile, width), lambda s, t: (jnp.where(s == 0, t, 1), 0)),
            pl.BlockSpec((tile, width), lambda s, t: (jnp.where(s == 0, 0, t), 0)),
            pl.BlockSpec((4, width), lambda s, t: (0, 0)),
        ]
        + [pl.BlockSpec(memory_space=pl.ANY)] * len(before),
        out_specs=[pl.BlockSpec((tile, width), out_place)] * 2,
        out_shape=[jax.ShapeDtypeStruct((4 * rows, width), LOW)] * 2,
        scratch_shapes=[pltpu.VMEM((tile, width), LOW)],
        input_output_aliases={3 + i: i for i in range(len(before))},
        cost_estimate=SMALL,
    )(first, second, norms, *before)


def copy_kernel(*refs):
    for index, ref in enumerate(refs[:2]):

        @pl.when(pl.program_id(0) == index)
        def _(ref=ref):
            refs[-1][...] = ref[...]


def copy_pair(first, second, offset, before):
    rows, width = first.shape
    tile = rows // 2
    return pl.pallas_call(
        copy_kernel,
        grid=(2, 2),
        in_specs=[
            pl.BlockSpec((tile, width), lambda s, t: (jnp.where(s == 0, t, 1), 0)),
            pl.BlockSpec((tile, width), lambda s, t: (jnp.where(s == 0, 0, t), 0)),
        ]
        + [pl.BlockSpec(memory_space=pl.ANY)] * len(before),
        out_specs=pl.BlockSpec((tile, width), lambda s, t: ((2 * s + offset) * 2 + t, 0)),
        out_shape=jax.ShapeDtypeStruct((4 * rows, width), LOW),
        input_output_aliases={2: 0} if before else {},
        cost_estimate=SMALL,
    )(first, second, *before)


def pack_kernel(*refs):
    rows = refs[0].shape[0]
    for index, ref in enumerate(refs[:-1]):
        refs[-1][index * rows : (index + 1) * rows, :] = ref[...]


def pack(blocks):
    rows, columns = blocks[0].shape
    return pl.pallas_call(
        pack_kernel,
        out_shape=jax.ShapeDtypeStruct((len(blocks) * rows, columns), LOW),
        cost_estimate=SMALL,
    )(*blocks)


def outer_kernel(*refs):
    result, pairs, start = refs[-1], refs[:-1], 0
    for left, right in zip(pairs[0::2], pairs[1::2]):
        columns = slice(start, start + right.shape[1])
        result[:, columns] = dot(left[...], right[...], ((0,), (0,))).astype(LOW)
        start = columns.stop


def outer(*arrays):
    tokens, width = arrays[0].shape
    tile = width // 4
    columns = sum(right.shape[1] for right in arrays[1::2])
    in_specs = []
    for right in arrays[1::2]:
        in_specs += [
            pl.BlockSpec((tokens, tile), lambda i: (0, i)),
            pl.BlockSpec(right.shape, lambda i: (0, 0), pipeline_mode=pl.Buffered(1)),
        ]
    return pl.pallas_call(
        outer_kernel,
        grid=(4,),
        in_specs=in_specs,
        out_specs=pl.BlockSpec((tile, columns), lambda i: (i, 0)),
        out_shape=jax.ShapeDtypeStruct((width, columns), LOW),
        cost_estimate=SMALL,
    )(*arrays)


def collect(where, refs, count, full, result, copies, kept):
    zi, place = where[0], where[1]
    rows = full.shape[1]

    def move(ref, base, block):
        for step in range(4):
            pltpu.make_async_copy(
                ref.at[pl.ds(base + step * rows, rows)],
                full.at[4 * block + (place ^ step)],
                copies.at[4 * block + step],
            ).start()

    for block in range(count):
        if len(refs) == 1:
            move(refs[0], block * 4 * rows, block)
            continue
        for step in range(count):
            pairs = [(step, block + step), (count - 1 + step, block - step)]
            for index, owner in pairs[: 2 if step else 1]:
                if 0 <= owner < count:

                    @pl.when(zi == owner)
                    def _(index=index):
                        move(refs[index], 0, block)

    for block in range(count):
        for step in range(4):
            pltpu.make_async_copy(
                refs[0].at[pl.ds(0, rows)],
                full.at[4 * block + (place ^ step)],
                copies.at[4 * block + step],
            ).wait()
    pltpu.make_async_copy(full, result, kept).start()


def weighted_call(kernel, where, gathered, count, operands, in_specs, out_specs, out_shape, grid, scratch):
    refs = gathered.refs() if isinstance(gathered, Line) else [gathered]
    rows, columns = refs[0].shape
    rows = rows // 4 if len(refs) > 1 else rows // (4 * count)
    last = grid[0] - 1

    def body(where_ref, *args):
        parts, args = args[: len(refs)], args[len(refs) :]
        inputs, args = args[: len(operands)], args[len(operands) :]
        result, args = args[0], args[1:]
        full, copies, kept = args[-3:]

        @pl.when(pl.program_id(0) == 0)
        def _():
            collect(where_ref, parts, count, full, result, copies, kept)

        kernel(full, *inputs, *args[:-3])

        @pl.when(pl.program_id(0) == last)
        def _():
            pltpu.make_async_copy(full, result, kept).wait()

    result = pl.pallas_call(
        body,
        grid_spec=pltpu.PrefetchScalarGridSpec(
            num_scalar_prefetch=1,
            grid=grid,
            in_specs=[pl.BlockSpec(memory_space=pl.ANY)] * len(refs) + in_specs,
            out_specs=[pl.BlockSpec(memory_space=pl.ANY)] + out_specs,
            scratch_shapes=scratch
            + [
                pltpu.VMEM((4 * count, rows, columns), LOW),
                pltpu.SemaphoreType.DMA((4 * count,)),
                pltpu.SemaphoreType.DMA,
            ],
        ),
        out_shape=[jax.ShapeDtypeStruct((4 * count, rows, columns), LOW)] + out_shape,
        cost_estimate=SMALL,
    )(where, *refs, *operands)
    return [result[0].reshape(4 * count * rows, columns)] + list(result[1:])


def up_kernel(full, mixed, bias, active, slope):
    weight = full.reshape(full.shape[0] * full.shape[1], full.shape[2])
    for start in range(0, weight.shape[1], 256):
        columns = slice(start, start + 256)
        hidden = dot(mixed[...], weight[:, columns], ((1,), (0,))) + bias[:, columns]
        cdf = 0.5 * (1.0 + lax.erf(hidden * (0.5**0.5)))
        density = jnp.exp(-0.5 * hidden * hidden) * 0.3989422804014327
        active[:, columns] = (hidden * cdf).astype(LOW)
        slope[:, columns] = (cdf + hidden * density).astype(LOW)


def up_forward(where, gathered, count, mixed, bias):
    tokens, width = mixed.shape
    columns = bias.shape[1]
    tile = tokens // 8

    def rows_of(size):
        return pl.BlockSpec((tile, size), lambda i, z: (i, 0))

    return weighted_call(
        up_kernel,
        where,
        gathered,
        count,
        (mixed, bias),
        [rows_of(width), pl.BlockSpec((1, columns), lambda i, z: (0, 0))],
        [rows_of(columns)] * 2,
        [jax.ShapeDtypeStruct((tokens, columns), LOW)] * 2,
        (8,),
        [],
    )


def down_kernel(full, dy, slope, grad, total):
    weight = full.reshape(full.shape[0] * full.shape[1], full.shape[2])

    @pl.when(pl.program_id(0) == 0)
    def _():
        total[...] = jnp.zeros_like(total)

    for start in range(0, weight.shape[1], 256):
        columns = slice(start, start + 256)
        value = dot(dy[...], weight[:, columns], ((1,), (0,))) * slope[:, columns].astype(WIDE)
        value = value.astype(LOW)
        grad[:, columns] = value
        total[:, columns] += jnp.sum(value.astype(WIDE), axis=0, keepdims=True)


def down_backward(where, gathered, count, dy, slope):
    tokens, width = dy.shape
    columns = slope.shape[1]
    tile = tokens // 8

    def rows_of(size):
        return pl.BlockSpec((tile, size), lambda i, z: (i, 0))

    return weighted_call(
        down_kernel,
        where,
        gathered,
        count,
        (dy, slope),
        [rows_of(width), rows_of(columns)],
        [rows_of(columns), pl.BlockSpec((1, columns), lambda i, z: (0, 0))],
        [
            jax.ShapeDtypeStruct((tokens, columns), LOW),
            jax.ShapeDtypeStruct((1, columns), WIDE),
        ],
        (8,),
        [],
    )


def sum_specs(tile, width, sent):
    rows = pl.BlockSpec((tile, width), lambda i: (i, 0))
    shape = jax.ShapeDtypeStruct((4 * tile, width), LOW)
    if sent is None:
        return [], rows, shape
    one = pl.BlockSpec((tile, width), lambda i: (0, 0))
    return [rows], [rows, one], [shape, jax.ShapeDtypeStruct((tile, width), LOW)]


def put_sum(term, columns, rest):
    if len(rest) == 1:
        rest[0][:, columns] = term.astype(LOW)
        return
    sent, result, over = rest
    value = (term + sent[:, columns].astype(WIDE)).astype(LOW)
    result[:, columns] = value

    @pl.when(pl.program_id(0) == 2)
    def _():
        over[:, columns] = value


def branch_kernel(value, weight, *rest):
    for start in range(0, weight.shape[0], 512):
        columns = slice(start, start + 512)
        term = dot(value[...], weight[columns, weight.shape[1] - value.shape[1] :], ((1,), (1,)))
        put_sum(term, columns, rest)


def branch_terms(first, value, weight, sent):
    tokens, width = value.shape[0] // 2, weight.shape[0]
    tile = tokens // 4
    skip = first // tile
    extra_specs, out_specs, out_shape = sum_specs(tile, width, sent)
    return pl.pallas_call(
        branch_kernel,
        grid=(4,),
        in_specs=[
            pl.BlockSpec((tile, value.shape[1]), lambda i: (i + skip, 0)),
            pl.BlockSpec(weight.shape, lambda i: (0, 0), pipeline_mode=pl.Buffered(1)),
        ]
        + extra_specs,
        out_specs=out_specs,
        out_shape=out_shape,
        cost_estimate=SMALL,
    )(value, weight, *(() if sent is None else (sent,)))


def input_kernel(attn, hidden, attn_weight, up_weight, gains, *rest):
    for start in range(0, gains.shape[1], 512):
        columns = slice(start, start + 512)
        value = (
            dot(attn[...], attn_weight[columns, : attn.shape[1]], ((1,), (1,))) * gains[0:1, columns]
        )
        value += dot(hidden[...], up_weight[columns, :], ((1,), (1,))) * gains[1:2, columns]
        put_sum(value, columns, rest)


def input_terms(first, attn, hidden, attn_weight, up_weight, gains, sent):
    tokens = attn.shape[0] // 2
    width = gains.shape[1]
    tile = tokens // 4
    skip = first // tile

    def rows_of(size, start):
        return pl.BlockSpec((tile, size), lambda i: (i + start, 0))

    def whole(array):
        return pl.BlockSpec(array.shape, lambda i: (0, 0), pipeline_mode=pl.Buffered(1))

    extra_specs, out_specs, out_shape = sum_specs(tile, width, sent)
    return pl.pallas_call(
        input_kernel,
        grid=(4,),
        in_specs=[
            rows_of(attn.shape[1], skip),
            rows_of(hidden.shape[1], skip),
            whole(attn_weight),
            whole(up_weight),
            whole(gains),
        ]
        + extra_specs,
        out_specs=out_specs,
        out_shape=out_shape,
        cost_estimate=SMALL,
    )(attn, hidden, attn_weight, up_weight, gains, *(() if sent is None else (sent,)))


def attention_kernel(full, normed, dy, bias, cosine, sine, begin, heads, grad, total, *scratch):
    q_s, k_s, v_s, g_s, dk_s, dv_s = scratch
    weight = full.reshape(full.shape[0] * full.shape[1], full.shape[2])
    rows = normed.shape[0]
    lane = lax.broadcasted_iota(jnp.int32, (1, 128), 1)
    scale = HD ** (-0.5)

    def turn(value, sign):
        low = value[:, :128]
        sine_now = sine[0] * sign
        ahead = pltpu.roll(low, 128 - ROT // 2, 1) * jnp.where(lane < ROT // 2, -sine_now, 0.0)
        behind = pltpu.roll(low, ROT // 2, 1) * jnp.where(lane < ROT // 2, 0.0, sine_now)
        return jnp.concatenate([low * cosine[0] + ahead + behind, value[:, 128:]], axis=1)

    def project(index):
        columns = slice(index * HD, (index + 1) * HD)
        return dot(normed[...], weight[:, columns], ((1,), (0,))) + bias[:, columns]

    q_s[...] = turn(project(0), 1.0).astype(LOW)
    k_s[...] = turn(project(1), 1.0).astype(LOW)
    v_s[...] = project(2).astype(LOW)
    g_s[...] = dot(dy[...], weight[:, 3 * HD :], ((1,), (0,))).astype(LOW)
    dk_s[...] = jnp.zeros_like(dk_s)
    dv_s[...] = jnp.zeros_like(dv_s)
    tile = 320
    for start in range(0, rows, tile):
        here, seen = slice(start, start + tile), slice(0, start + tile)
        query, grad_heads = q_s[here, :], g_s[here, :]
        keys, value = k_s[seen, :], v_s[seen, :]
        scores = dot(query, keys, ((1,), (1,))) * scale
        column = lax.broadcasted_iota(jnp.int32, scores.shape, 1)
        row = lax.broadcasted_iota(jnp.int32, scores.shape, 0) + start
        allowed = (column <= row) & (column >= begin[0, here, :])
        scores = jnp.where(allowed, scores, -1e30)
        shifted = jnp.exp(scores - jnp.max(scores, axis=1, keepdims=True))
        prob = shifted / jnp.sum(shifted, axis=1, keepdims=True)
        low = prob.astype(LOW)
        heads[here, :] = dot(low, value, ((1,), (0,))).astype(LOW)
        grad_prob = dot(grad_heads, value, ((1,), (1,)))
        weighted = jnp.sum(grad_prob * prob, axis=1, keepdims=True)
        grad_scores = (prob * (grad_prob - weighted) * scale).astype(LOW)
        grad_query = dot(grad_scores, keys, ((1,), (0,)))
        cos_here = cosine[0, here, :]
        sine_here = -sine[0, here, :]
        head = grad_query[:, :128]
        ahead = pltpu.roll(head, 128 - ROT // 2, 1) * jnp.where(lane < ROT // 2, -sine_here, 0.0)
        behind = pltpu.roll(head, ROT // 2, 1) * jnp.where(lane < ROT // 2, 0.0, sine_here)
        grad[here, :128] = (head * cos_here + ahead + behind).astype(LOW)
        grad[here, 128:HD] = grad_query[:, 128:].astype(LOW)
        dk_s[seen, :] += dot(grad_scores, query, ((0,), (0,)))
        dv_s[seen, :] += dot(low, grad_heads, ((0,), (0,)))
    grad[:, HD : 2 * HD] = turn(dk_s[...], -1.0).astype(LOW)
    grad[:, 2 * HD :] = dv_s[...].astype(LOW)

    @pl.when(pl.program_id(0) == 0)
    def _():
        total[...] = jnp.zeros_like(total)

    total[...] += jnp.sum(grad[...].astype(WIDE), axis=0, keepdims=True)


def attention(where, gathered, count, normed, dy, bias, cosine, sine, begin):
    tokens, width = normed.shape
    rows = tokens // 4

    def per_sequence(size):
        return pl.BlockSpec((rows, size), lambda s, z: (s, 0))

    def table(size):
        return pl.BlockSpec((1, rows, size), lambda s, z: (s, 0, 0))

    row = pl.BlockSpec((1, 3 * HD), lambda s, z: (0, 0))
    return weighted_call(
        attention_kernel,
        where,
        gathered,
        count,
        (normed, dy, bias, cosine, sine, begin),
        [per_sequence(width), per_sequence(width), row, table(128), table(128), table(1)],
        [per_sequence(HD), per_sequence(3 * HD), row],
        [
            jax.ShapeDtypeStruct((tokens, HD), LOW),
            jax.ShapeDtypeStruct((tokens, 3 * HD), LOW),
            jax.ShapeDtypeStruct((1, 3 * HD), WIDE),
        ],
        (4,),
        [pltpu.VMEM((rows, HD), LOW)] * 4 + [pltpu.VMEM((rows, HD), WIDE)] * 2,
    )


def sum_line(value, count):
    step = 1
    while step < count:
        value = value + lax.ppermute(value, "z", [(i, i ^ step) for i in range(count)])
        step *= 2
    return value


def up_back_kernel(place, *refs):
    result = refs[-1]
    columns = refs[0].shape[1]
    for step in range(4):
        start = pl.multiple_of((place[0] ^ step) * columns, columns)
        result[:, pl.ds(start, columns)] = refs[step][...].astype(WIDE)


def down_back_kernel(place, *refs):
    result = refs[-1]
    columns = refs[0].shape[1]
    for step in range(4):
        start = pl.multiple_of((place[0] ^ step) * columns, columns)
        result[pl.ds(start, columns), :] = refs[step][...].astype(WIDE).T


def attn_back_kernel(place, *refs):
    qkv, out = refs[-2:]
    for step in range(4):
        head = place[0] ^ step
        block = refs[step][...].astype(WIDE)
        for part in range(3):
            qkv[:, part, pl.ds(head, 1), :] = block[:, None, part * HD : (part + 1) * HD]
        out[pl.ds(head, 1)] = block[:, 3 * HD :].T[None]


def gradient_of(kernel, place, blocks, shapes):
    whole = [pl.BlockSpec(memory_space=pltpu.VMEM)] * 4
    return pl.pallas_call(
        kernel,
        in_specs=[pl.BlockSpec(memory_space=pltpu.SMEM)] + whole,
        out_specs=[pl.BlockSpec(memory_space=pltpu.VMEM)] * len(shapes),
        out_shape=[jax.ShapeDtypeStruct(shape, WIDE) for shape in shapes],
        cost_estimate=SMALL,
    )(place.reshape(1), *blocks)


def doc_start(lengths, place):
    passed = place[:, None] >= jnp.cumsum(lengths)[None, :]
    return jnp.sum(jnp.where(passed, lengths[None, :], 0), axis=1)


def per_device(
    inputs,
    doc_lengths,
    norm1_gain,
    norm1_bias,
    qkv_weight,
    qkv_bias,
    out_weight,
    out_bias,
    norm2_gain,
    norm2_bias,
    up_weight,
    up_bias,
    down_weight,
    down_bias,
    cotangent,
):
    rows, width = inputs.shape
    count = lax.axis_size("z")
    zi, xi, ci, yi = [lax.axis_index(axis) for axis in EVERY]
    place = xi * 2 + ci
    hidden_part = up_bias.shape[0] // 4
    part_rows = up_weight.shape[0]
    head_width = 3 * HD

    norms = jnp.stack([norm1_gain, norm1_bias, norm2_gain, norm2_bias])

    def columns_of(weight):
        return lambda t: lax.dynamic_slice_in_dim(weight, t * hidden_part, hidden_part, 1)

    def rows_of(weight):
        return lambda t: lax.dynamic_slice_in_dim(weight, t * hidden_part, hidden_part, 0).T

    def heads_of(qkv, out):
        return lambda t: jnp.concatenate(
            [pick(qkv, t, 1).reshape(part_rows, head_width), pick(out, t, 0).T], axis=1
        )

    def pieces_of(part):
        return [
            lax.dynamic_slice_in_dim(part, (place ^ step) * part_rows, part_rows, 0)
            for step in range(4)
        ]

    def returned(part):
        return traded(pieces_of(part))

    where = jnp.stack([zi, place])
    half = rows // 2

    def side(array):
        return lax.dynamic_slice_in_dim(array, yi * half, half, 0)

    def stage(line, *values):
        line.right[-1], values = tie(line.right[-1], values)
        line.left[-1], values = tie(line.left[-1], values)
        return values

    up_blocks = trade(columns_of(up_weight), place)
    up_blocks, x_now, x_beside, dy_beside, lengths_x = tie(
        up_blocks, inputs, swap(inputs, "c"), swap(cotangent, "c"), swap(doc_lengths, "x")
    )

    up_line = Line(pack(up_blocks), zi, count)
    up_line.hop()
    x_near = swap(side(after(x_now, up_line.block)), "x")
    heads_now = heads_of(*after((qkv_weight, out_weight), up_line.block))
    norm_now, heads_now, lengths_x, lengths_now, dy_now = stage(
        up_line,
        norm_pair(x_now, x_beside, 0, norms, ()),
        [heads_now(place ^ step) for step in range(4)],
        lengths_x,
        doc_lengths,
        (cotangent, dy_beside),
    )

    up_line.hop()
    x_far = swap(after(x_near, lengths_x), "y")
    lengths_pair = jnp.concatenate([lengths_now, lengths_x])
    attn_blocks, lengths_other, dy_flat, dy_now = stage(
        up_line,
        traded(heads_now),
        swap(lengths_pair, "c"),
        copy_pair(*dy_now, 0, ()),
        cotangent,
    )

    up_line.finish()
    dy_near = swap(side(dy_now), "x")
    across = ordered(yi, x_near, after(x_far, attn_blocks[0]), 0).reshape(inputs.shape)
    attn_line = Line(pack(attn_blocks), zi, count)
    norm_now, attn_line.block, down_now = stage(
        up_line,
        norm_pair(across, swap(across, "c"), 1, norms, norm_now),
        attn_line.block,
        down_weight,
    )
    normed, mixed = norm_now
    attn_line.right, attn_line.left = [attn_line.block], [attn_line.block]

    attn_line.hop()
    dy_far = swap(after(dy_near, mixed), "y")
    up_rows, active, slope, down_blocks = stage(
        attn_line,
        *up_forward(where, up_line, count, mixed, pick(up_bias.reshape(4, 1, -1), place, 0)),
        trade(rows_of(down_now), place),
    )

    attn_line.hop()
    dy_across = ordered(yi, dy_near, after(dy_far, active), 0).reshape(cotangent.shape)
    down_line = Line(pack(down_blocks), zi, count)
    dy_flat = copy_pair(dy_across, swap(dy_across, "c"), 1, (dy_flat,))
    lengths_all = jnp.concatenate([lengths_pair, lengths_other])
    begin = jax.vmap(lambda one: doc_start(one, jnp.arange(rows, dtype=jnp.int32)))(lengths_all)
    dy_flat, down_line.block, active, begin = stage(
        attn_line, dy_flat, down_line.block, active, begin
    )

    attn_line.finish()
    grad_down = outer(dy_flat, active)
    ordinal = jnp.arange(rows, dtype=jnp.int32)
    position = (ordinal - begin).astype(WIDE)
    exponent = jnp.arange(ROT // 2, dtype=WIDE) * (-2.0 / ROT)
    angle = position[..., None] * jnp.power(10000.0, exponent)
    angle = jnp.concatenate([angle, angle, jnp.zeros((4, rows, 128 - ROT), WIDE)], axis=-1)
    begin, cosine, sine, down_line.block, grad_down, dy_flat, attn_bias = stage(
        attn_line,
        begin[..., None],
        jnp.cos(angle),
        jnp.sin(angle),
        down_line.block,
        grad_down,
        dy_flat,
        pick(qkv_bias.reshape(4, 1, -1), place, 0),
    )
    down_line.right, down_line.left = [down_line.block], [down_line.block]

    down_line.hop()
    attn_rows, heads, grad_projected, qkv_bias_term = stage(
        down_line,
        *attention(
            where, attn_line, count, normed, dy_flat, attn_bias, cosine, sine, begin
        ),
    )
    qkv_bias_term = qkv_bias_term[0]

    def first_terms(value, weight):
        return branch_terms(2 * rows, value, weight, None)

    def own_terms(value, weight, sent):
        return branch_terms(0, value, weight, sent)

    down_line.hop()
    grad_attn, heads, attn_first = stage(
        down_line,
        outer(normed, grad_projected, dy_flat, heads),
        heads,
        first_terms(heads, attn_rows),
    )

    down_line.finish()
    grad_attn, grad_down, attn_mine = stage(
        down_line,
        grad_attn,
        grad_down,
        own_terms(heads, attn_rows, swap(attn_first, "c")),
    )

    down_part = lax.psum_scatter(grad_down, "z", scatter_dimension=0, tiled=True)
    attn_part = lax.psum_scatter(grad_attn, "z", scatter_dimension=0, tiled=True)
    attn_over = cross_first(attn_mine[1], cross_rows(attn_mine[0], yi))
    down_rows, grad_hidden, up_bias_term = down_backward(where, down_line, count, dy_flat, slope)
    up_bias_term = up_bias_term[0]
    grad_hidden, ffn_first, active, attn_over = tie(
        grad_hidden, first_terms(active, down_rows), active, attn_over
    )

    gains = norms[0::2]
    attn_over = cross_second(attn_mine[0], *attn_over, yi)
    sent, ffn_sent, grad_hidden, active = tie(
        input_terms(
            2 * rows, grad_projected, after(grad_hidden, attn_over[0]), attn_rows, up_rows, gains, None
        ),
        swap(ffn_first, "c"),
        grad_hidden,
        active,
    )

    ffn_mine, sent_now, attn_over, grad_hidden = tie(
        own_terms(active, down_rows, ffn_sent), swap(sent, "c"), attn_over, grad_hidden
    )
    attn_half = crossed(*attn_over)

    ffn_over = cross_first(ffn_mine[1], cross_rows(ffn_mine[0], yi))
    mine = input_terms(0, grad_projected, grad_hidden, attn_rows, up_rows, gains, sent_now)
    mine, grad_hidden, ffn_over = tie(mine, grad_hidden, ffn_over)

    last_rows = cross_rows(mine[0], yi)
    input_over = cross_first(mine[1], last_rows)
    ffn_over = after(ffn_over, last_rows)
    ffn_over = cross_second(ffn_mine[0], *ffn_over, yi)
    grad_up = outer(mixed, grad_hidden)

    def norm_terms(weight, grad, bias_term, gain, shift):
        weight = weight.astype(WIDE)
        shift_term = jnp.sum(weight * bias_term, axis=1)
        gain_term = (jnp.sum(weight * grad.astype(WIDE), axis=1) - shift * shift_term) / gain
        return gain_term, shift_term

    input_over, ffn_over, grad_attn, grad_up = tie(input_over, ffn_over, grad_attn, grad_up)
    up_part = lax.psum_scatter(grad_up, "z", scatter_dimension=0, tiled=True)
    input_over = cross_second(mine[0], *input_over, yi)
    grad_attn, grad_up = after((grad_attn, grad_up), input_over[0])
    gain1, shift1 = norm_terms(
        attn_rows[:, :head_width], grad_attn[:, :head_width], qkv_bias_term, norm1_gain, norm1_bias
    )
    gain2, shift2 = norm_terms(up_rows, grad_up, up_bias_term, norm2_gain, norm2_bias)
    x_half = own_half(inputs, yi).astype(WIDE)
    attn_branch = attn_half + out_bias
    ffn_branch = crossed(*ffn_over) + down_bias
    slot = (jnp.arange(8, dtype=jnp.int32) == yi * 4 + place).astype(WIDE)[:, None]
    small = jnp.concatenate(
        [
            gain1,
            shift1,
            gain2,
            shift2,
            jnp.sum(cotangent, axis=0, dtype=WIDE) * 0.5,
            (slot * qkv_bias_term).reshape(-1),
            (slot * up_bias_term).reshape(-1),
            jnp.stack([jnp.sum(attn_branch * attn_branch), jnp.sum(ffn_branch * ffn_branch)]),
        ]
    )
    for axis in ("c", "y"):
        small = small + swap(small, axis)
    small, input_over, attn_branch, ffn_branch = tie(small, input_over, attn_branch, ffn_branch)
    out_low = (x_half + attn_branch + ffn_branch).astype(LOW)
    out_other = swap(out_low, "y")
    input_half = crossed(*input_over)
    centre_half = x_half - jnp.mean(x_half, axis=-1, keepdims=True)
    scale_half = lax.rsqrt(jnp.mean(centre_half * centre_half, axis=-1, keepdims=True) + EPS)
    unit_half = centre_half * scale_half
    back_half = scale_half * (
        input_half
        - jnp.mean(input_half, axis=-1, keepdims=True)
        - unit_half * jnp.mean(input_half * unit_half, axis=-1, keepdims=True)
    )
    back_low = back_half.astype(LOW)
    back_other = swap(back_low, "y")
    small = after(small, back_low)
    small = small + swap(small, "x")
    down_back = returned(after(down_part, small))
    attn_back = returned(after(attn_part, small))
    small = sum_line(small, count)
    all_columns = 4 * hidden_part
    (down_sum,) = gradient_of(down_back_kernel, place, down_back, [(all_columns, part_rows)])
    qkv_sum, out_sum = gradient_of(
        attn_back_kernel, place, attn_back, [(part_rows, 3, 4, HD), (4, HD, part_rows)]
    )
    up_part, small, down_sum, qkv_sum, out_sum = tie(up_part, small, down_sum, qkv_sum, out_sum)
    up_pieces = pieces_of(up_part)
    out_other, back_other = after((out_other, back_other), *up_pieces)
    outputs = whole_rows(out_low, out_other, yi)
    back_rows = whole_rows(back_low, back_other, yi)
    grad_inputs = cotangent.astype(WIDE) + back_rows.astype(WIDE)
    (up_sum,) = gradient_of(up_back_kernel, place, traded(up_pieces), [(part_rows, all_columns)])

    sizes = [width] * 5 + [8 * head_width, 8 * hidden_part]
    starts = [sum(sizes[:i]) for i in range(len(sizes) + 1)]
    pieces = [small[a:b] for a, b in zip(starts[:-1], starts[1:])]
    qkv_bias_sum = pick(pieces[5].reshape(2, 4, 3, HD), yi, 0)
    up_bias_sum = pick(pieces[6].reshape(2, 4 * hidden_part), yi, 0)
    rms_pair = jnp.sqrt(small[starts[-1] :] / float(rows * 4 * count * width))

    qkv_sum = jnp.transpose(qkv_sum, (0, 2, 1, 3))
    return (
        outputs,
        grad_inputs,
        pieces[0],
        pieces[1],
        qkv_sum,
        qkv_bias_sum,
        out_sum,
        pieces[4],
        pieces[2],
        pieces[3],
        up_sum,
        up_bias_sum,
        down_sum,
        rms_pair[0],
        rms_pair[1],
    )


def solution(mesh):
    dp = mesh.shape["dp"]
    grid = Mesh(mesh.devices.reshape(dp // 4, 2, 2, mesh.shape["tensor"]), EVERY)
    dp = ("z", "x", "c")
    in_specs = (
        P(dp, None),
        P(dp, None),
        P(),
        P(),
        P(dp, "y", None, None),
        P("y", None, None),
        P("y", None, dp),
        P(),
        P(),
        P(),
        P(dp, "y"),
        P("y"),
        P("y", dp),
        P(),
        P(dp, None),
    )
    out_specs = (
        P(dp, None),
        P(dp, None),
        P(),
        P(),
        P(dp, "y", None, None),
        P("y", None, None),
        P("y", None, dp),
        P(),
        P(),
        P(),
        P(dp, "y"),
        P("y"),
        P("y", dp),
        P(),
        P(),
    )
    return jax.shard_map(
        per_device, mesh=grid, in_specs=in_specs, out_specs=out_specs, check_vma=False
    )
```

```python
import jax
import jax.numpy as jnp
from jax import lax
from jax.experimental import pallas as pl
from jax.experimental.pallas import tpu as pltpu
from jax.sharding import Mesh
from jax.sharding import PartitionSpec as P

HD = 256
ROT = 64
EPS = 1e-05
LOW = jnp.bfloat16
WIDE = jnp.float32
GROUP = ("x", "c")
EVERY = ("z", "x", "c", "y")


SMALL = pl.CostEstimate(flops=1 << 20, bytes_accessed=1 << 20, transcendentals=0)


def dot(left, right, dims):
    return lax.dot_general(left, right, (dims, ((), ())), preferred_element_type=WIDE)


def swap(value, axis):
    return lax.ppermute(value, axis, [(0, 1), (1, 0)])


def pick(value, index, axis):
    return lax.dynamic_index_in_dim(value, index, axis, keepdims=False)


def ordered(index, own, other, axis):
    first = jnp.where(index == 0, own, other)
    second = jnp.where(index == 0, other, own)
    return jnp.stack([first, second], axis=axis)


def trade(block, place):
    return traded([block(place ^ step) for step in range(4)])


def traded(blocks):
    return blocks[:1] + [
        lax.ppermute(blocks[step], GROUP, [(i, i ^ step) for i in range(4)])
        for step in range(1, 4)
    ]


class Ring:
    def __init__(self, block, count):
        self.count, self.blocks = count, [block]

    def hop(self, *waits):
        if len(self.blocks) < self.count:
            sent = after(self.blocks[-1], *waits)
            self.blocks.append(
                lax.ppermute(sent, "z", [(i, (i + 1) % self.count) for i in range(self.count)])
            )

    def finish(self):
        while len(self.blocks) < self.count:
            self.hop()


def tie(*values):
    return lax.optimization_barrier(values)


def after(value, *waits):
    return lax.optimization_barrier((value, waits))[0] if waits else value


def cross_rows(mine, yi):
    rows = mine.shape[0] // 2
    part = rows // 4
    return jnp.stack(
        [
            lax.dynamic_slice_in_dim(mine, start + (1 - yi) * part, part, 0)
            for start in (rows // 2, rows + rows // 2)
        ]
    )


def cross_first(over, last):
    return swap(over, "x"), swap(last, "y")


def cross_kernel(yi, first, last, beyond, over_x, over_y, *rest):
    first_kept, first_sent, last_kept, last_sent, total = rest
    part = last.shape[0]

    def add(step, _):
        chunk = pl.ds(pl.multiple_of(step * 16, 16), 16)
        total[chunk, :] = (first[chunk, :].astype(WIDE) + over_x[chunk, :].astype(WIDE)).astype(LOW)
        return 0

    lax.fori_loop(0, first.shape[0] // 16, add, 0, unroll=4)
    first_kept[...] = total[pl.ds(pl.multiple_of(yi[0] * part, 16), part), :]
    first_sent[...] = total[pl.ds(pl.multiple_of((1 - yi[0]) * part, 16), part), :]

    def add_last(step, _):
        chunk = pl.ds(pl.multiple_of(step * 16, 16), 16)
        last_kept[chunk, :] = last[chunk, :].astype(WIDE) + over_y[0, chunk, :].astype(WIDE)
        value = beyond[chunk, :].astype(WIDE) + over_y[1, chunk, :].astype(WIDE)
        last_sent[chunk, :] = value.astype(LOW)
        return 0

    lax.fori_loop(0, part // 16, add_last, 0, unroll=2)


def cross_second(mine, over_x, over_y, yi):
    rows, width = mine.shape[0] // 2, mine.shape[1]
    part = rows // 4
    kept = jax.ShapeDtypeStruct((part, width), LOW)
    place = pl.BlockSpec((part, width), lambda i, yi: (0, 0))
    first, first_sent, last, last_sent = pl.pallas_call(
        cross_kernel,
        grid_spec=pltpu.PrefetchScalarGridSpec(
            num_scalar_prefetch=1,
            grid=(1,),
            in_specs=[
                pl.BlockSpec((2 * part, width), lambda i, yi: (0, 0)),
                pl.BlockSpec((part, width), lambda i, yi: (2 + yi[0], 0)),
                pl.BlockSpec((part, width), lambda i, yi: (6 + yi[0], 0)),
                pl.BlockSpec((2 * part, width), lambda i, yi: (0, 0)),
                pl.BlockSpec((2, part, width), lambda i, yi: (0, 0, 0)),
            ],
            out_specs=[place] * 4,
            scratch_shapes=[pltpu.VMEM((2 * part, width), LOW)],
        ),
        out_shape=[kept, kept, jax.ShapeDtypeStruct((part, width), WIDE), kept],
        cost_estimate=SMALL,
    )(yi.reshape(1), mine, mine, mine, over_x, over_y)
    return first, swap(first_sent, "y"), last, swap(last_sent, "x")


def crossed(own_first, sent_first, own_last, sent_last):
    return jnp.stack(
        [
            own_first.astype(WIDE) + sent_first.astype(WIDE),
            own_last + sent_last.astype(WIDE),
        ]
    )


def own_half(rows_in, yi):
    return pick(rows_in.reshape(2, 2, rows_in.shape[0] // 4, -1), yi, 1)


def whole_rows(half, other, yi):
    return ordered(yi, half, other, 1).reshape(4 * half.shape[1], half.shape[2])


def norm_kernel(first, second, norms, *rest):
    normed, mixed, rows_in = rest[-3:]
    for index, ref in enumerate((first, second)):

        @pl.when(pl.program_id(0) == index)
        def _(ref=ref):
            rows_in[...] = ref[...]

    gain1, shift1, gain2, shift2 = [norms[i : i + 1, :] for i in range(4)]

    def norm(step, _):
        chunk = pl.ds(pl.multiple_of(step * 16, 16), 16)
        value = rows_in[chunk, :].astype(WIDE)
        centre = value - jnp.mean(value, axis=-1, keepdims=True)
        unit = centre * lax.rsqrt(jnp.mean(centre * centre, axis=-1, keepdims=True) + EPS)
        normed[chunk, :] = (unit * gain1 + shift1).astype(LOW)
        mixed[chunk, :] = (unit * gain2 + shift2).astype(LOW)
        return 0

    lax.fori_loop(0, rows_in.shape[0] // 16, norm, 0, unroll=4)


def norm_pair(first, second, offset, norms, before):
    rows, width = first.shape
    tile = rows // 2

    def out_place(s, t):
        return (2 * s + offset) * 2 + t, 0

    return pl.pallas_call(
        norm_kernel,
        grid=(2, 2),
        in_specs=[
            pl.BlockSpec((tile, width), lambda s, t: (jnp.where(s == 0, t, 1), 0)),
            pl.BlockSpec((tile, width), lambda s, t: (jnp.where(s == 0, 0, t), 0)),
            pl.BlockSpec((4, width), lambda s, t: (0, 0)),
        ]
        + [pl.BlockSpec(memory_space=pl.ANY)] * len(before),
        out_specs=[pl.BlockSpec((tile, width), out_place)] * 2,
        out_shape=[jax.ShapeDtypeStruct((4 * rows, width), LOW)] * 2,
        scratch_shapes=[pltpu.VMEM((tile, width), LOW)],
        input_output_aliases={3 + i: i for i in range(len(before))},
        cost_estimate=SMALL,
    )(first, second, norms, *before)


def copy_kernel(*refs):
    for index, ref in enumerate(refs[:2]):

        @pl.when(pl.program_id(0) == index)
        def _(ref=ref):
            refs[-1][...] = ref[...]


def copy_pair(first, second, offset, before):
    rows, width = first.shape
    tile = rows // 2
    return pl.pallas_call(
        copy_kernel,
        grid=(2, 2),
        in_specs=[
            pl.BlockSpec((tile, width), lambda s, t: (jnp.where(s == 0, t, 1), 0)),
            pl.BlockSpec((tile, width), lambda s, t: (jnp.where(s == 0, 0, t), 0)),
        ]
        + [pl.BlockSpec(memory_space=pl.ANY)] * len(before),
        out_specs=pl.BlockSpec((tile, width), lambda s, t: ((2 * s + offset) * 2 + t, 0)),
        out_shape=jax.ShapeDtypeStruct((4 * rows, width), LOW),
        input_output_aliases={2: 0} if before else {},
        cost_estimate=SMALL,
    )(first, second, *before)


def pack_kernel(*refs):
    rows = refs[0].shape[0]
    for index, ref in enumerate(refs[:-1]):
        refs[-1][index * rows : (index + 1) * rows, :] = ref[...]


def pack(blocks):
    rows, columns = blocks[0].shape
    return pl.pallas_call(
        pack_kernel,
        out_shape=jax.ShapeDtypeStruct((len(blocks) * rows, columns), LOW),
        cost_estimate=SMALL,
    )(*blocks)


def outer_kernel(*refs):
    result, pairs, start = refs[-1], refs[:-1], 0
    for left, right in zip(pairs[0::2], pairs[1::2]):
        columns = slice(start, start + right.shape[1])
        result[:, columns] = dot(left[...], right[...], ((0,), (0,))).astype(LOW)
        start = columns.stop


def outer(*arrays):
    tokens, width = arrays[0].shape
    tile = width // 4
    columns = sum(right.shape[1] for right in arrays[1::2])
    in_specs = []
    for right in arrays[1::2]:
        in_specs += [
            pl.BlockSpec((tokens, tile), lambda i: (0, i)),
            pl.BlockSpec(right.shape, lambda i: (0, 0), pipeline_mode=pl.Buffered(1)),
        ]
    return pl.pallas_call(
        outer_kernel,
        grid=(4,),
        in_specs=in_specs,
        out_specs=pl.BlockSpec((tile, columns), lambda i: (i, 0)),
        out_shape=jax.ShapeDtypeStruct((width, columns), LOW),
        cost_estimate=SMALL,
    )(*arrays)


def collect(where, refs, count, full, result, copies, kept):
    zi, place = where[0], where[1]
    rows = full.shape[1]

    def move(ref, block):
        for step in range(4):
            pltpu.make_async_copy(
                ref.at[pl.ds(step * rows, rows)],
                full.at[4 * block + (place ^ step)],
                copies.at[4 * block + step],
            ).start()

    for block in range(count):
        for step in range(count):

            @pl.when(zi == (block + step) % count)
            def _(step=step):
                move(refs[step], block)

    for block in range(count):
        for step in range(4):
            pltpu.make_async_copy(
                refs[0].at[pl.ds(0, rows)],
                full.at[4 * block + (place ^ step)],
                copies.at[4 * block + step],
            ).wait()
    pltpu.make_async_copy(full, result, kept).start()


def weighted_call(kernel, where, gathered, count, operands, in_specs, out_specs, out_shape, grid, scratch):
    refs = gathered.blocks
    rows, columns = refs[0].shape
    rows = rows // 4
    last = grid[0] - 1

    def body(where_ref, *args):
        parts, args = args[: len(refs)], args[len(refs) :]
        inputs, args = args[: len(operands)], args[len(operands) :]
        result, args = args[0], args[1:]
        full, copies, kept = args[-3:]

        @pl.when(pl.program_id(0) == 0)
        def _():
            collect(where_ref, parts, count, full, result, copies, kept)

        kernel(full, *inputs, *args[:-3])

        @pl.when(pl.program_id(0) == last)
        def _():
            pltpu.make_async_copy(full, result, kept).wait()

    result = pl.pallas_call(
        body,
        grid_spec=pltpu.PrefetchScalarGridSpec(
            num_scalar_prefetch=1,
            grid=grid,
            in_specs=[pl.BlockSpec(memory_space=pl.ANY)] * len(refs) + in_specs,
            out_specs=[pl.BlockSpec(memory_space=pl.ANY)] + out_specs,
            scratch_shapes=scratch
            + [
                pltpu.VMEM((4 * count, rows, columns), LOW),
                pltpu.SemaphoreType.DMA((4 * count,)),
                pltpu.SemaphoreType.DMA,
            ],
        ),
        out_shape=[jax.ShapeDtypeStruct((4 * count, rows, columns), LOW)] + out_shape,
        cost_estimate=SMALL,
    )(where, *refs, *operands)
    return [result[0].reshape(4 * count * rows, columns)] + list(result[1:])


def up_kernel(full, mixed, bias, active, slope):
    weight = full.reshape(full.shape[0] * full.shape[1], full.shape[2])
    for start in range(0, weight.shape[1], 256):
        columns = slice(start, start + 256)
        hidden = dot(mixed[...], weight[:, columns], ((1,), (0,))) + bias[:, columns]
        cdf = 0.5 * (1.0 + lax.erf(hidden * (0.5**0.5)))
        density = jnp.exp(-0.5 * hidden * hidden) * 0.3989422804014327
        active[:, columns] = (hidden * cdf).astype(LOW)
        slope[:, columns] = (cdf + hidden * density).astype(LOW)


def up_forward(where, gathered, count, mixed, bias):
    tokens, width = mixed.shape
    columns = bias.shape[1]
    tile = tokens // 8

    def rows_of(size):
        return pl.BlockSpec((tile, size), lambda i, z: (i, 0))

    return weighted_call(
        up_kernel,
        where,
        gathered,
        count,
        (mixed, bias),
        [rows_of(width), pl.BlockSpec((1, columns), lambda i, z: (0, 0))],
        [rows_of(columns)] * 2,
        [jax.ShapeDtypeStruct((tokens, columns), LOW)] * 2,
        (8,),
        [],
    )


def down_kernel(full, dy, slope, grad, total):
    weight = full.reshape(full.shape[0] * full.shape[1], full.shape[2])

    @pl.when(pl.program_id(0) == 0)
    def _():
        total[...] = jnp.zeros_like(total)

    for start in range(0, weight.shape[1], 256):
        columns = slice(start, start + 256)
        value = dot(dy[...], weight[:, columns], ((1,), (0,))) * slope[:, columns].astype(WIDE)
        value = value.astype(LOW)
        grad[:, columns] = value
        total[:, columns] += jnp.sum(value.astype(WIDE), axis=0, keepdims=True)


def down_backward(where, gathered, count, dy, slope):
    tokens, width = dy.shape
    columns = slope.shape[1]
    tile = tokens // 8

    def rows_of(size):
        return pl.BlockSpec((tile, size), lambda i, z: (i, 0))

    return weighted_call(
        down_kernel,
        where,
        gathered,
        count,
        (dy, slope),
        [rows_of(width), rows_of(columns)],
        [rows_of(columns), pl.BlockSpec((1, columns), lambda i, z: (0, 0))],
        [
            jax.ShapeDtypeStruct((tokens, columns), LOW),
            jax.ShapeDtypeStruct((1, columns), WIDE),
        ],
        (8,),
        [],
    )


def sum_specs(tile, width, sent):
    rows = pl.BlockSpec((tile, width), lambda i: (i, 0))
    shape = jax.ShapeDtypeStruct((4 * tile, width), LOW)
    if sent is None:
        return [], rows, shape
    one = pl.BlockSpec((tile, width), lambda i: (0, 0))
    return [rows], [rows, one], [shape, jax.ShapeDtypeStruct((tile, width), LOW)]


def put_sum(term, columns, rest):
    if len(rest) == 1:
        rest[0][:, columns] = term.astype(LOW)
        return
    sent, result, over = rest
    value = (term + sent[:, columns].astype(WIDE)).astype(LOW)
    result[:, columns] = value

    @pl.when(pl.program_id(0) == 2)
    def _():
        over[:, columns] = value


def branch_kernel(value, weight, *rest):
    for start in range(0, weight.shape[0], 512):
        columns = slice(start, start + 512)
        term = dot(value[...], weight[columns, weight.shape[1] - value.shape[1] :], ((1,), (1,)))
        put_sum(term, columns, rest)


def branch_terms(first, value, weight, sent):
    tokens, width = value.shape[0] // 2, weight.shape[0]
    tile = tokens // 4
    skip = first // tile
    extra_specs, out_specs, out_shape = sum_specs(tile, width, sent)
    return pl.pallas_call(
        branch_kernel,
        grid=(4,),
        in_specs=[
            pl.BlockSpec((tile, value.shape[1]), lambda i: (i + skip, 0)),
            pl.BlockSpec(weight.shape, lambda i: (0, 0), pipeline_mode=pl.Buffered(1)),
        ]
        + extra_specs,
        out_specs=out_specs,
        out_shape=out_shape,
        cost_estimate=SMALL,
    )(value, weight, *(() if sent is None else (sent,)))


def input_kernel(attn, hidden, attn_weight, up_weight, gains, *rest):
    for start in range(0, gains.shape[1], 512):
        columns = slice(start, start + 512)
        value = (
            dot(attn[...], attn_weight[columns, : attn.shape[1]], ((1,), (1,))) * gains[0:1, columns]
        )
        value += dot(hidden[...], up_weight[columns, :], ((1,), (1,))) * gains[1:2, columns]
        put_sum(value, columns, rest)


def input_terms(first, attn, hidden, attn_weight, up_weight, gains, sent):
    tokens = attn.shape[0] // 2
    width = gains.shape[1]
    tile = tokens // 4
    skip = first // tile

    def rows_of(size, start):
        return pl.BlockSpec((tile, size), lambda i: (i + start, 0))

    def whole(array):
        return pl.BlockSpec(array.shape, lambda i: (0, 0), pipeline_mode=pl.Buffered(1))

    extra_specs, out_specs, out_shape = sum_specs(tile, width, sent)
    return pl.pallas_call(
        input_kernel,
        grid=(4,),
        in_specs=[
            rows_of(attn.shape[1], skip),
            rows_of(hidden.shape[1], skip),
            whole(attn_weight),
            whole(up_weight),
            whole(gains),
        ]
        + extra_specs,
        out_specs=out_specs,
        out_shape=out_shape,
        cost_estimate=SMALL,
    )(attn, hidden, attn_weight, up_weight, gains, *(() if sent is None else (sent,)))


def attention_kernel(full, normed, dy, bias, cosine, sine, begin, heads, grad, total, *scratch):
    q_s, k_s, v_s, g_s, dk_s, dv_s = scratch
    weight = full.reshape(full.shape[0] * full.shape[1], full.shape[2])
    rows = normed.shape[0]
    lane = lax.broadcasted_iota(jnp.int32, (1, 128), 1)
    scale = HD ** (-0.5)

    def turn(value, sign):
        low = value[:, :128]
        sine_now = sine[0] * sign
        ahead = pltpu.roll(low, 128 - ROT // 2, 1) * jnp.where(lane < ROT // 2, -sine_now, 0.0)
        behind = pltpu.roll(low, ROT // 2, 1) * jnp.where(lane < ROT // 2, 0.0, sine_now)
        return jnp.concatenate([low * cosine[0] + ahead + behind, value[:, 128:]], axis=1)

    def project(index):
        columns = slice(index * HD, (index + 1) * HD)
        return dot(normed[...], weight[:, columns], ((1,), (0,))) + bias[:, columns]

    q_s[...] = turn(project(0), 1.0).astype(LOW)
    k_s[...] = turn(project(1), 1.0).astype(LOW)
    v_s[...] = project(2).astype(LOW)
    g_s[...] = dot(dy[...], weight[:, 3 * HD :], ((1,), (0,))).astype(LOW)
    dk_s[...] = jnp.zeros_like(dk_s)
    dv_s[...] = jnp.zeros_like(dv_s)
    tile = 320
    for start in range(0, rows, tile):
        here, seen = slice(start, start + tile), slice(0, start + tile)
        query, grad_heads = q_s[here, :], g_s[here, :]
        keys, value = k_s[seen, :], v_s[seen, :]
        scores = dot(query, keys, ((1,), (1,))) * scale
        column = lax.broadcasted_iota(jnp.int32, scores.shape, 1)
        row = lax.broadcasted_iota(jnp.int32, scores.shape, 0) + start
        allowed = (column <= row) & (column >= begin[0, here, :])
        scores = jnp.where(allowed, scores, -1e30)
        shifted = jnp.exp(scores - jnp.max(scores, axis=1, keepdims=True))
        prob = shifted / jnp.sum(shifted, axis=1, keepdims=True)
        low = prob.astype(LOW)
        heads[here, :] = dot(low, value, ((1,), (0,))).astype(LOW)
        grad_prob = dot(grad_heads, value, ((1,), (1,)))
        weighted = jnp.sum(grad_prob * prob, axis=1, keepdims=True)
        grad_scores = (prob * (grad_prob - weighted) * scale).astype(LOW)
        grad_query = dot(grad_scores, keys, ((1,), (0,)))
        cos_here = cosine[0, here, :]
        sine_here = -sine[0, here, :]
        head = grad_query[:, :128]
        ahead = pltpu.roll(head, 128 - ROT // 2, 1) * jnp.where(lane < ROT // 2, -sine_here, 0.0)
        behind = pltpu.roll(head, ROT // 2, 1) * jnp.where(lane < ROT // 2, 0.0, sine_here)
        grad[here, :128] = (head * cos_here + ahead + behind).astype(LOW)
        grad[here, 128:HD] = grad_query[:, 128:].astype(LOW)
        dk_s[seen, :] += dot(grad_scores, query, ((0,), (0,)))
        dv_s[seen, :] += dot(low, grad_heads, ((0,), (0,)))
    grad[:, HD : 2 * HD] = turn(dk_s[...], -1.0).astype(LOW)
    grad[:, 2 * HD :] = dv_s[...].astype(LOW)

    @pl.when(pl.program_id(0) == 0)
    def _():
        total[...] = jnp.zeros_like(total)

    total[...] += jnp.sum(grad[...].astype(WIDE), axis=0, keepdims=True)


def attention(where, gathered, count, normed, dy, bias, cosine, sine, begin):
    tokens, width = normed.shape
    rows = tokens // 4

    def per_sequence(size):
        return pl.BlockSpec((rows, size), lambda s, z: (s, 0))

    def table(size):
        return pl.BlockSpec((1, rows, size), lambda s, z: (s, 0, 0))

    row = pl.BlockSpec((1, 3 * HD), lambda s, z: (0, 0))
    return weighted_call(
        attention_kernel,
        where,
        gathered,
        count,
        (normed, dy, bias, cosine, sine, begin),
        [per_sequence(width), per_sequence(width), row, table(128), table(128), table(1)],
        [per_sequence(HD), per_sequence(3 * HD), row],
        [
            jax.ShapeDtypeStruct((tokens, HD), LOW),
            jax.ShapeDtypeStruct((tokens, 3 * HD), LOW),
            jax.ShapeDtypeStruct((1, 3 * HD), WIDE),
        ],
        (4,),
        [pltpu.VMEM((rows, HD), LOW)] * 4 + [pltpu.VMEM((rows, HD), WIDE)] * 2,
    )


def sum_line(value, count):
    step = 1
    while step < count:
        value = value + lax.ppermute(value, "z", [(i, i ^ step) for i in range(count)])
        step *= 2
    return value


def up_back_kernel(place, *refs):
    result = refs[-1]
    columns = refs[0].shape[1]
    for step in range(4):
        start = pl.multiple_of((place[0] ^ step) * columns, columns)
        result[:, pl.ds(start, columns)] = refs[step][...].astype(WIDE)


def down_back_kernel(place, *refs):
    result = refs[-1]
    columns = refs[0].shape[1]
    for step in range(4):
        start = pl.multiple_of((place[0] ^ step) * columns, columns)
        result[pl.ds(start, columns), :] = refs[step][...].astype(WIDE).T


def attn_back_kernel(place, *refs):
    qkv, out = refs[-2:]
    for step in range(4):
        head = place[0] ^ step
        block = refs[step][...].astype(WIDE)
        for part in range(3):
            qkv[:, part, pl.ds(head, 1), :] = block[:, None, part * HD : (part + 1) * HD]
        out[pl.ds(head, 1)] = block[:, 3 * HD :].T[None]


def gradient_of(kernel, place, blocks, shapes):
    whole = [pl.BlockSpec(memory_space=pltpu.VMEM)] * 4
    return pl.pallas_call(
        kernel,
        in_specs=[pl.BlockSpec(memory_space=pltpu.SMEM)] + whole,
        out_specs=[pl.BlockSpec(memory_space=pltpu.VMEM)] * len(shapes),
        out_shape=[jax.ShapeDtypeStruct(shape, WIDE) for shape in shapes],
        cost_estimate=SMALL,
    )(place.reshape(1), *blocks)


def doc_start(lengths, place):
    passed = place[:, None] >= jnp.cumsum(lengths)[None, :]
    return jnp.sum(jnp.where(passed, lengths[None, :], 0), axis=1)


def per_device(
    inputs,
    doc_lengths,
    norm1_gain,
    norm1_bias,
    qkv_weight,
    qkv_bias,
    out_weight,
    out_bias,
    norm2_gain,
    norm2_bias,
    up_weight,
    up_bias,
    down_weight,
    down_bias,
    cotangent,
):
    rows, width = inputs.shape
    count = lax.axis_size("z")
    zi, xi, ci, yi = [lax.axis_index(axis) for axis in EVERY]
    place = xi * 2 + ci
    hidden_part = up_bias.shape[0] // 4
    part_rows = up_weight.shape[0]
    head_width = 3 * HD

    norms = jnp.stack([norm1_gain, norm1_bias, norm2_gain, norm2_bias])

    def columns_of(weight):
        return lambda t: lax.dynamic_slice_in_dim(weight, t * hidden_part, hidden_part, 1)

    def rows_of(weight):
        return lambda t: lax.dynamic_slice_in_dim(weight, t * hidden_part, hidden_part, 0).T

    def heads_of(qkv, out):
        return lambda t: jnp.concatenate(
            [pick(qkv, t, 1).reshape(part_rows, head_width), pick(out, t, 0).T], axis=1
        )

    def pieces_of(part):
        return [
            lax.dynamic_slice_in_dim(part, (place ^ step) * part_rows, part_rows, 0)
            for step in range(4)
        ]

    def returned(part):
        return traded(pieces_of(part))

    where = jnp.stack([zi, place])
    half = rows // 2

    def side(array):
        return lax.dynamic_slice_in_dim(array, yi * half, half, 0)

    def stage(line, *values):
        line.blocks[-1], values = tie(line.blocks[-1], values)
        return values

    up_blocks = trade(columns_of(up_weight), place)
    up_blocks, x_now, x_beside, dy_beside, lengths_x = tie(
        up_blocks, inputs, swap(inputs, "c"), swap(cotangent, "c"), swap(doc_lengths, "x")
    )

    up_line = Ring(pack(up_blocks), count)
    up_line.hop()
    x_near = swap(side(after(x_now, up_line.blocks[0])), "x")
    heads_now = heads_of(*after((qkv_weight, out_weight), up_line.blocks[0]))
    norm_now, heads_now, lengths_x, lengths_now, dy_now = stage(
        up_line,
        norm_pair(x_now, x_beside, 0, norms, ()),
        [heads_now(place ^ step) for step in range(4)],
        lengths_x,
        doc_lengths,
        (cotangent, dy_beside),
    )

    up_line.hop()
    x_far = swap(after(x_near, lengths_x), "y")
    lengths_pair = jnp.concatenate([lengths_now, lengths_x])
    attn_blocks, lengths_other, dy_flat, dy_now = stage(
        up_line,
        traded(heads_now),
        swap(lengths_pair, "c"),
        copy_pair(*dy_now, 0, ()),
        cotangent,
    )

    up_line.finish()
    dy_near = swap(side(dy_now), "x")
    across = ordered(yi, x_near, after(x_far, attn_blocks[0]), 0).reshape(inputs.shape)
    attn_line = Ring(pack(attn_blocks), count)
    down_rows_of = rows_of(after(down_weight, attn_line.blocks[0]))
    norm_now, attn_line.blocks[0], down_blocks = stage(
        up_line,
        norm_pair(across, swap(across, "c"), 1, norms, norm_now),
        attn_line.blocks[0],
        [down_rows_of(place ^ step) for step in range(4)],
    )
    normed, mixed = norm_now

    attn_line.hop()
    dy_far = swap(after(dy_near, mixed), "y")
    up_rows, active, slope, down_blocks = stage(
        attn_line,
        *up_forward(where, up_line, count, mixed, pick(up_bias.reshape(4, 1, -1), place, 0)),
        traded(down_blocks),
    )

    attn_line.hop()
    dy_across = ordered(yi, dy_near, after(dy_far, active), 0).reshape(cotangent.shape)
    down_line = Ring(pack(down_blocks), count)
    dy_flat = copy_pair(dy_across, swap(dy_across, "c"), 1, (dy_flat,))
    lengths_all = jnp.concatenate([lengths_pair, lengths_other])
    begin = jax.vmap(lambda one: doc_start(one, jnp.arange(rows, dtype=jnp.int32)))(lengths_all)
    dy_flat, down_line.blocks[0], active, begin = stage(
        attn_line, dy_flat, down_line.blocks[0], active, begin
    )

    attn_line.finish()
    grad_down = outer(dy_flat, active)
    ordinal = jnp.arange(rows, dtype=jnp.int32)
    position = (ordinal - begin).astype(WIDE)
    exponent = jnp.arange(ROT // 2, dtype=WIDE) * (-2.0 / ROT)
    angle = position[..., None] * jnp.power(10000.0, exponent)
    angle = jnp.concatenate([angle, angle, jnp.zeros((4, rows, 128 - ROT), WIDE)], axis=-1)
    begin, cosine, sine, down_line.blocks[0], grad_down, dy_flat, attn_bias = stage(
        attn_line,
        begin[..., None],
        jnp.cos(angle),
        jnp.sin(angle),
        down_line.blocks[0],
        grad_down,
        dy_flat,
        pick(qkv_bias.reshape(4, 1, -1), place, 0),
    )

    down_line.hop()
    attn_rows, heads, grad_projected, qkv_bias_term = stage(
        down_line,
        *attention(
            where, attn_line, count, normed, dy_flat, attn_bias, cosine, sine, begin
        ),
    )
    qkv_bias_term = qkv_bias_term[0]

    def first_terms(value, weight):
        return branch_terms(2 * rows, value, weight, None)

    def own_terms(value, weight, sent):
        return branch_terms(0, value, weight, sent)

    down_line.hop()
    grad_attn, heads, attn_first = stage(
        down_line,
        outer(normed, grad_projected, dy_flat, heads),
        heads,
        first_terms(heads, attn_rows),
    )

    down_line.finish()
    grad_attn, grad_down, attn_mine = stage(
        down_line,
        grad_attn,
        grad_down,
        own_terms(heads, attn_rows, swap(attn_first, "c")),
    )

    down_part = lax.psum_scatter(grad_down, "z", scatter_dimension=0, tiled=True)
    attn_part = lax.psum_scatter(grad_attn, "z", scatter_dimension=0, tiled=True)
    attn_over = cross_first(attn_mine[1], cross_rows(attn_mine[0], yi))
    down_rows, grad_hidden, up_bias_term = down_backward(where, down_line, count, dy_flat, slope)
    up_bias_term = up_bias_term[0]
    grad_hidden, ffn_first, active, attn_over = tie(
        grad_hidden, first_terms(active, down_rows), active, attn_over
    )

    gains = norms[0::2]
    attn_over = cross_second(attn_mine[0], *attn_over, yi)
    sent, ffn_sent, grad_hidden, active = tie(
        input_terms(
            2 * rows, grad_projected, after(grad_hidden, attn_over[0]), attn_rows, up_rows, gains, None
        ),
        swap(ffn_first, "c"),
        grad_hidden,
        active,
    )

    ffn_mine, sent_now, attn_over, grad_hidden = tie(
        own_terms(active, down_rows, ffn_sent), swap(sent, "c"), attn_over, grad_hidden
    )
    attn_half = crossed(*attn_over)

    ffn_over = cross_first(ffn_mine[1], cross_rows(ffn_mine[0], yi))
    mine = input_terms(0, grad_projected, grad_hidden, attn_rows, up_rows, gains, sent_now)
    mine, grad_hidden, ffn_over = tie(mine, grad_hidden, ffn_over)

    last_rows = cross_rows(mine[0], yi)
    input_over = cross_first(mine[1], last_rows)
    ffn_over = after(ffn_over, last_rows)
    ffn_over = cross_second(ffn_mine[0], *ffn_over, yi)
    grad_up = outer(mixed, grad_hidden)

    def norm_terms(weight, grad, bias_term, gain, shift):
        weight = weight.astype(WIDE)
        shift_term = jnp.sum(weight * bias_term, axis=1)
        gain_term = (jnp.sum(weight * grad.astype(WIDE), axis=1) - shift * shift_term) / gain
        return gain_term, shift_term

    input_over, ffn_over, grad_attn, grad_up = tie(input_over, ffn_over, grad_attn, grad_up)
    up_part = lax.psum_scatter(grad_up, "z", scatter_dimension=0, tiled=True)
    input_over = cross_second(mine[0], *input_over, yi)
    grad_attn, grad_up = after((grad_attn, grad_up), input_over[0])
    gain1, shift1 = norm_terms(
        attn_rows[:, :head_width], grad_attn[:, :head_width], qkv_bias_term, norm1_gain, norm1_bias
    )
    gain2, shift2 = norm_terms(up_rows, grad_up, up_bias_term, norm2_gain, norm2_bias)
    x_half = own_half(inputs, yi).astype(WIDE)
    attn_branch = attn_half + out_bias
    ffn_branch = crossed(*ffn_over) + down_bias
    slot = (jnp.arange(8, dtype=jnp.int32) == yi * 4 + place).astype(WIDE)[:, None]
    small = jnp.concatenate(
        [
            gain1,
            shift1,
            gain2,
            shift2,
            jnp.sum(cotangent, axis=0, dtype=WIDE) * 0.5,
            (slot * qkv_bias_term).reshape(-1),
            (slot * up_bias_term).reshape(-1),
            jnp.stack([jnp.sum(attn_branch * attn_branch), jnp.sum(ffn_branch * ffn_branch)]),
        ]
    )
    for axis in ("c", "y"):
        small = small + swap(small, axis)
    small, input_over, attn_branch, ffn_branch = tie(small, input_over, attn_branch, ffn_branch)
    out_low = (x_half + attn_branch + ffn_branch).astype(LOW)
    out_other = swap(out_low, "y")
    input_half = crossed(*input_over)
    centre_half = x_half - jnp.mean(x_half, axis=-1, keepdims=True)
    scale_half = lax.rsqrt(jnp.mean(centre_half * centre_half, axis=-1, keepdims=True) + EPS)
    unit_half = centre_half * scale_half
    back_half = scale_half * (
        input_half
        - jnp.mean(input_half, axis=-1, keepdims=True)
        - unit_half * jnp.mean(input_half * unit_half, axis=-1, keepdims=True)
    )
    back_low = back_half.astype(LOW)
    back_other = swap(back_low, "y")
    small = after(small, back_low)
    small = small + swap(small, "x")
    down_back = returned(after(down_part, small))
    attn_back = returned(after(attn_part, small))
    small = sum_line(small, count)
    all_columns = 4 * hidden_part
    (down_sum,) = gradient_of(down_back_kernel, place, down_back, [(all_columns, part_rows)])
    qkv_sum, out_sum = gradient_of(
        attn_back_kernel, place, attn_back, [(part_rows, 3, 4, HD), (4, HD, part_rows)]
    )
    outputs = whole_rows(out_low, after(out_other, qkv_sum, small), yi)
    up_part, small, down_sum, qkv_sum, out_sum, outputs = tie(
        up_part, small, down_sum, qkv_sum, out_sum, outputs
    )
    up_pieces = pieces_of(up_part)
    back_other = after(back_other, *up_pieces)
    back_rows = whole_rows(back_low, back_other, yi)
    grad_inputs = cotangent.astype(WIDE) + back_rows.astype(WIDE)
    (up_sum,) = gradient_of(up_back_kernel, place, traded(up_pieces), [(part_rows, all_columns)])

    sizes = [width] * 5 + [8 * head_width, 8 * hidden_part]
    starts = [sum(sizes[:i]) for i in range(len(sizes) + 1)]
    pieces = [small[a:b] for a, b in zip(starts[:-1], starts[1:])]
    qkv_bias_sum = pick(pieces[5].reshape(2, 4, 3, HD), yi, 0)
    up_bias_sum = pick(pieces[6].reshape(2, 4 * hidden_part), yi, 0)
    rms_pair = jnp.sqrt(small[starts[-1] :] / float(rows * 4 * count * width))

    qkv_sum = jnp.transpose(qkv_sum, (0, 2, 1, 3))
    return (
        outputs,
        grad_inputs,
        pieces[0],
        pieces[1],
        qkv_sum,
        qkv_bias_sum,
        out_sum,
        pieces[4],
        pieces[2],
        pieces[3],
        up_sum,
        up_bias_sum,
        down_sum,
        rms_pair[0],
        rms_pair[1],
    )


def solution(mesh):
    dp = mesh.shape["dp"]
    grid = Mesh(mesh.devices.reshape(dp // 4, 2, 2, mesh.shape["tensor"]), EVERY)
    dp = ("z", "x", "c")
    in_specs = (
        P(dp, None),
        P(dp, None),
        P(),
        P(),
        P(dp, "y", None, None),
        P("y", None, None),
        P("y", None, dp),
        P(),
        P(),
        P(),
        P(dp, "y"),
        P("y"),
        P("y", dp),
        P(),
        P(dp, None),
    )
    out_specs = (
        P(dp, None),
        P(dp, None),
        P(),
        P(),
        P(dp, "y", None, None),
        P("y", None, None),
        P("y", None, dp),
        P(),
        P(),
        P(),
        P(dp, "y"),
        P("y"),
        P("y", dp),
        P(),
        P(),
    )
    return jax.shard_map(
        per_device, mesh=grid, in_specs=in_specs, out_specs=out_specs, check_vma=False
    )
```

```python
import jax
import jax.numpy as jnp
from jax import lax
from jax.experimental import pallas as pl
from jax.experimental.pallas import tpu as pltpu
from jax.sharding import Mesh
from jax.sharding import PartitionSpec as P

HD = 256
ROT = 64
EPS = 1e-05
LOW = jnp.bfloat16
WIDE = jnp.float32
GROUP = ("x", "c")
EVERY = ("z", "x", "c", "y")


SMALL = pl.CostEstimate(flops=1 << 20, bytes_accessed=1 << 20, transcendentals=0)


def dot(left, right, dims):
    return lax.dot_general(left, right, (dims, ((), ())), preferred_element_type=WIDE)


def swap(value, axis):
    return lax.ppermute(value, axis, [(0, 1), (1, 0)])


def pick(value, index, axis):
    return lax.dynamic_index_in_dim(value, index, axis, keepdims=False)


def ordered(index, own, other, axis):
    first = jnp.where(index == 0, own, other)
    second = jnp.where(index == 0, other, own)
    return jnp.stack([first, second], axis=axis)


def trade(block, place):
    return traded([block(place ^ step) for step in range(4)])


def traded(blocks):
    return blocks[:1] + [
        lax.ppermute(blocks[step], GROUP, [(i, i ^ step) for i in range(4)])
        for step in range(1, 4)
    ]


class Ring:
    def __init__(self, block, count):
        self.count, self.blocks = count, [block]

    def hop(self, *waits):
        if len(self.blocks) < self.count:
            sent = after(self.blocks[-1], *waits)
            self.blocks.append(
                lax.ppermute(sent, "z", [(i, (i + 1) % self.count) for i in range(self.count)])
            )

    def finish(self):
        while len(self.blocks) < self.count:
            self.hop()


def tie(*values):
    return lax.optimization_barrier(values)


def after(value, *waits):
    return lax.optimization_barrier((value, waits))[0] if waits else value


def cross_rows(mine, yi):
    rows = mine.shape[0] // 2
    part = rows // 4
    return jnp.stack(
        [
            lax.dynamic_slice_in_dim(mine, start + (1 - yi) * part, part, 0)
            for start in (rows // 2, rows + rows // 2)
        ]
    )


def cross_first(over, last):
    return swap(over, "x"), swap(last, "y")


def cross_kernel(yi, first, last, beyond, over_x, over_y, *rest):
    first_kept, first_sent, last_kept, last_sent, total = rest
    part = last.shape[0]

    def add(step, _):
        chunk = pl.ds(pl.multiple_of(step * 16, 16), 16)
        total[chunk, :] = (first[chunk, :].astype(WIDE) + over_x[chunk, :].astype(WIDE)).astype(LOW)
        return 0

    lax.fori_loop(0, first.shape[0] // 16, add, 0, unroll=4)
    first_kept[...] = total[pl.ds(pl.multiple_of(yi[0] * part, 16), part), :]
    first_sent[...] = total[pl.ds(pl.multiple_of((1 - yi[0]) * part, 16), part), :]

    def add_last(step, _):
        chunk = pl.ds(pl.multiple_of(step * 16, 16), 16)
        last_kept[chunk, :] = last[chunk, :].astype(WIDE) + over_y[0, chunk, :].astype(WIDE)
        value = beyond[chunk, :].astype(WIDE) + over_y[1, chunk, :].astype(WIDE)
        last_sent[chunk, :] = value.astype(LOW)
        return 0

    lax.fori_loop(0, part // 16, add_last, 0, unroll=2)


def cross_second(mine, over_x, over_y, yi):
    rows, width = mine.shape[0] // 2, mine.shape[1]
    part = rows // 4
    kept = jax.ShapeDtypeStruct((part, width), LOW)
    place = pl.BlockSpec((part, width), lambda i, yi: (0, 0))
    first, first_sent, last, last_sent = pl.pallas_call(
        cross_kernel,
        grid_spec=pltpu.PrefetchScalarGridSpec(
            num_scalar_prefetch=1,
            grid=(1,),
            in_specs=[
                pl.BlockSpec((2 * part, width), lambda i, yi: (0, 0)),
                pl.BlockSpec((part, width), lambda i, yi: (2 + yi[0], 0)),
                pl.BlockSpec((part, width), lambda i, yi: (6 + yi[0], 0)),
                pl.BlockSpec((2 * part, width), lambda i, yi: (0, 0)),
                pl.BlockSpec((2, part, width), lambda i, yi: (0, 0, 0)),
            ],
            out_specs=[place] * 4,
            scratch_shapes=[pltpu.VMEM((2 * part, width), LOW)],
        ),
        out_shape=[kept, kept, jax.ShapeDtypeStruct((part, width), WIDE), kept],
        cost_estimate=SMALL,
    )(yi.reshape(1), mine, mine, mine, over_x, over_y)
    return first, swap(first_sent, "y"), last, swap(last_sent, "x")


def crossed(own_first, sent_first, own_last, sent_last):
    return jnp.stack(
        [
            own_first.astype(WIDE) + sent_first.astype(WIDE),
            own_last + sent_last.astype(WIDE),
        ]
    )


def own_half(rows_in, yi):
    return pick(rows_in.reshape(2, 2, rows_in.shape[0] // 4, -1), yi, 1)


def whole_rows(half, other, yi):
    return ordered(yi, half, other, 1).reshape(4 * half.shape[1], half.shape[2])


def norm_kernel(first, second, norms, *rest):
    normed, mixed, rows_in = rest[-3:]
    for index, ref in enumerate((first, second)):

        @pl.when(pl.program_id(0) == index)
        def _(ref=ref):
            rows_in[...] = ref[...]

    gain1, shift1, gain2, shift2 = [norms[i : i + 1, :] for i in range(4)]

    def norm(step, _):
        chunk = pl.ds(pl.multiple_of(step * 16, 16), 16)
        value = rows_in[chunk, :].astype(WIDE)
        centre = value - jnp.mean(value, axis=-1, keepdims=True)
        unit = centre * lax.rsqrt(jnp.mean(centre * centre, axis=-1, keepdims=True) + EPS)
        normed[chunk, :] = (unit * gain1 + shift1).astype(LOW)
        mixed[chunk, :] = (unit * gain2 + shift2).astype(LOW)
        return 0

    lax.fori_loop(0, rows_in.shape[0] // 16, norm, 0, unroll=4)


def norm_pair(first, second, offset, norms, before):
    rows, width = first.shape
    tile = rows // 2

    def out_place(s, t):
        return (2 * s + offset) * 2 + t, 0

    return pl.pallas_call(
        norm_kernel,
        grid=(2, 2),
        in_specs=[
            pl.BlockSpec((tile, width), lambda s, t: (jnp.where(s == 0, t, 1), 0)),
            pl.BlockSpec((tile, width), lambda s, t: (jnp.where(s == 0, 0, t), 0)),
            pl.BlockSpec((4, width), lambda s, t: (0, 0)),
        ]
        + [pl.BlockSpec(memory_space=pl.ANY)] * len(before),
        out_specs=[pl.BlockSpec((tile, width), out_place)] * 2,
        out_shape=[jax.ShapeDtypeStruct((4 * rows, width), LOW)] * 2,
        scratch_shapes=[pltpu.VMEM((tile, width), LOW)],
        input_output_aliases={3 + i: i for i in range(len(before))},
        cost_estimate=SMALL,
    )(first, second, norms, *before)


def copy_kernel(*refs):
    for index, ref in enumerate(refs[:2]):

        @pl.when(pl.program_id(0) == index)
        def _(ref=ref):
            refs[-1][...] = ref[...]


def copy_pair(first, second, offset, before):
    rows, width = first.shape
    tile = rows // 2
    return pl.pallas_call(
        copy_kernel,
        grid=(2, 2),
        in_specs=[
            pl.BlockSpec((tile, width), lambda s, t: (jnp.where(s == 0, t, 1), 0)),
            pl.BlockSpec((tile, width), lambda s, t: (jnp.where(s == 0, 0, t), 0)),
        ]
        + [pl.BlockSpec(memory_space=pl.ANY)] * len(before),
        out_specs=pl.BlockSpec((tile, width), lambda s, t: ((2 * s + offset) * 2 + t, 0)),
        out_shape=jax.ShapeDtypeStruct((4 * rows, width), LOW),
        input_output_aliases={2: 0} if before else {},
        cost_estimate=SMALL,
    )(first, second, *before)


def pack_kernel(*refs):
    rows = refs[0].shape[0]
    for index, ref in enumerate(refs[:-1]):
        refs[-1][index * rows : (index + 1) * rows, :] = ref[...]


def pack(blocks):
    rows, columns = blocks[0].shape
    return pl.pallas_call(
        pack_kernel,
        out_shape=jax.ShapeDtypeStruct((len(blocks) * rows, columns), LOW),
        cost_estimate=SMALL,
    )(*blocks)


def outer_kernel(*refs):
    result, pairs, start = refs[-1], refs[:-1], 0
    for left, right in zip(pairs[0::2], pairs[1::2]):
        columns = slice(start, start + right.shape[1])
        result[:, columns] = dot(left[...], right[...], ((0,), (0,))).astype(LOW)
        start = columns.stop


def outer(*arrays):
    tokens, width = arrays[0].shape
    tile = width // 4
    columns = sum(right.shape[1] for right in arrays[1::2])
    in_specs = []
    for right in arrays[1::2]:
        in_specs += [
            pl.BlockSpec((tokens, tile), lambda i: (0, i)),
            pl.BlockSpec(right.shape, lambda i: (0, 0), pipeline_mode=pl.Buffered(1)),
        ]
    return pl.pallas_call(
        outer_kernel,
        grid=(4,),
        in_specs=in_specs,
        out_specs=pl.BlockSpec((tile, columns), lambda i: (i, 0)),
        out_shape=jax.ShapeDtypeStruct((width, columns), LOW),
        cost_estimate=SMALL,
    )(*arrays)


def collect(where, refs, count, full, result, copies, kept):
    zi, place = where[0], where[1]
    rows = full.shape[1]

    def move(ref, block):
        for step in range(4):
            pltpu.make_async_copy(
                ref.at[pl.ds(step * rows, rows)],
                full.at[4 * block + (place ^ step)],
                copies.at[4 * block + step],
            ).start()

    for block in range(count):
        for step in range(count):

            @pl.when(zi == (block + step) % count)
            def _(step=step):
                move(refs[step], block)

    for block in range(count):
        for step in range(4):
            pltpu.make_async_copy(
                refs[0].at[pl.ds(0, rows)],
                full.at[4 * block + (place ^ step)],
                copies.at[4 * block + step],
            ).wait()
    pltpu.make_async_copy(full, result, kept).start()


def weighted_call(kernel, where, gathered, count, operands, in_specs, out_specs, out_shape, grid, scratch):
    refs = gathered.blocks
    rows, columns = refs[0].shape
    rows = rows // 4
    last = grid[0] - 1

    def body(where_ref, *args):
        parts, args = args[: len(refs)], args[len(refs) :]
        inputs, args = args[: len(operands)], args[len(operands) :]
        result, args = args[0], args[1:]
        full, copies, kept = args[-3:]

        @pl.when(pl.program_id(0) == 0)
        def _():
            collect(where_ref, parts, count, full, result, copies, kept)

        kernel(full, *inputs, *args[:-3])

        @pl.when(pl.program_id(0) == last)
        def _():
            pltpu.make_async_copy(full, result, kept).wait()

    result = pl.pallas_call(
        body,
        grid_spec=pltpu.PrefetchScalarGridSpec(
            num_scalar_prefetch=1,
            grid=grid,
            in_specs=[pl.BlockSpec(memory_space=pl.ANY)] * len(refs) + in_specs,
            out_specs=[pl.BlockSpec(memory_space=pl.ANY)] + out_specs,
            scratch_shapes=scratch
            + [
                pltpu.VMEM((4 * count, rows, columns), LOW),
                pltpu.SemaphoreType.DMA((4 * count,)),
                pltpu.SemaphoreType.DMA,
            ],
        ),
        out_shape=[jax.ShapeDtypeStruct((4 * count, rows, columns), LOW)] + out_shape,
        cost_estimate=SMALL,
    )(where, *refs, *operands)
    return [result[0].reshape(4 * count * rows, columns)] + list(result[1:])


def up_kernel(full, mixed, bias, active, slope):
    weight = full.reshape(full.shape[0] * full.shape[1], full.shape[2])
    for start in range(0, weight.shape[1], 256):
        columns = slice(start, start + 256)
        hidden = dot(mixed[...], weight[:, columns], ((1,), (0,))) + bias[:, columns]
        cdf = 0.5 * (1.0 + lax.erf(hidden * (0.5**0.5)))
        density = jnp.exp(-0.5 * hidden * hidden) * 0.3989422804014327
        active[:, columns] = (hidden * cdf).astype(LOW)
        slope[:, columns] = (cdf + hidden * density).astype(LOW)


def up_forward(where, gathered, count, mixed, bias):
    tokens, width = mixed.shape
    columns = bias.shape[1]
    tile = tokens // 8

    def rows_of(size):
        return pl.BlockSpec((tile, size), lambda i, z: (i, 0))

    return weighted_call(
        up_kernel,
        where,
        gathered,
        count,
        (mixed, bias),
        [rows_of(width), pl.BlockSpec((1, columns), lambda i, z: (0, 0))],
        [rows_of(columns)] * 2,
        [jax.ShapeDtypeStruct((tokens, columns), LOW)] * 2,
        (8,),
        [],
    )


def down_kernel(full, dy, slope, grad, total):
    weight = full.reshape(full.shape[0] * full.shape[1], full.shape[2])

    @pl.when(pl.program_id(0) == 0)
    def _():
        total[...] = jnp.zeros_like(total)

    for start in range(0, weight.shape[1], 256):
        columns = slice(start, start + 256)
        value = dot(dy[...], weight[:, columns], ((1,), (0,))) * slope[:, columns].astype(WIDE)
        value = value.astype(LOW)
        grad[:, columns] = value
        total[:, columns] += jnp.sum(value.astype(WIDE), axis=0, keepdims=True)


def down_backward(where, gathered, count, dy, slope):
    tokens, width = dy.shape
    columns = slope.shape[1]
    tile = tokens // 8

    def rows_of(size):
        return pl.BlockSpec((tile, size), lambda i, z: (i, 0))

    return weighted_call(
        down_kernel,
        where,
        gathered,
        count,
        (dy, slope),
        [rows_of(width), rows_of(columns)],
        [rows_of(columns), pl.BlockSpec((1, columns), lambda i, z: (0, 0))],
        [
            jax.ShapeDtypeStruct((tokens, columns), LOW),
            jax.ShapeDtypeStruct((1, columns), WIDE),
        ],
        (8,),
        [],
    )


def sum_specs(tile, width, sent):
    rows = pl.BlockSpec((tile, width), lambda i: (i, 0))
    shape = jax.ShapeDtypeStruct((4 * tile, width), LOW)
    if sent is None:
        return [], rows, shape
    one = pl.BlockSpec((tile, width), lambda i: (0, 0))
    return [rows], [rows, one], [shape, jax.ShapeDtypeStruct((tile, width), LOW)]


def put_sum(term, columns, rest):
    if len(rest) == 1:
        rest[0][:, columns] = term.astype(LOW)
        return
    sent, result, over = rest
    value = (term + sent[:, columns].astype(WIDE)).astype(LOW)
    result[:, columns] = value

    @pl.when(pl.program_id(0) == 2)
    def _():
        over[:, columns] = value


def branch_kernel(value, weight, *rest):
    for start in range(0, weight.shape[0], 512):
        columns = slice(start, start + 512)
        term = dot(value[...], weight[columns, weight.shape[1] - value.shape[1] :], ((1,), (1,)))
        put_sum(term, columns, rest)


def branch_terms(first, value, weight, sent):
    tokens, width = value.shape[0] // 2, weight.shape[0]
    tile = tokens // 4
    skip = first // tile
    extra_specs, out_specs, out_shape = sum_specs(tile, width, sent)
    return pl.pallas_call(
        branch_kernel,
        grid=(4,),
        in_specs=[
            pl.BlockSpec((tile, value.shape[1]), lambda i: (i + skip, 0)),
            pl.BlockSpec(weight.shape, lambda i: (0, 0), pipeline_mode=pl.Buffered(1)),
        ]
        + extra_specs,
        out_specs=out_specs,
        out_shape=out_shape,
        cost_estimate=SMALL,
    )(value, weight, *(() if sent is None else (sent,)))


def input_kernel(attn, hidden, attn_weight, up_weight, gains, *rest):
    for start in range(0, gains.shape[1], 512):
        columns = slice(start, start + 512)
        value = (
            dot(attn[...], attn_weight[columns, : attn.shape[1]], ((1,), (1,))) * gains[0:1, columns]
        )
        value += dot(hidden[...], up_weight[columns, :], ((1,), (1,))) * gains[1:2, columns]
        put_sum(value, columns, rest)


def input_terms(first, attn, hidden, attn_weight, up_weight, gains, sent):
    tokens = attn.shape[0] // 2
    width = gains.shape[1]
    tile = tokens // 4
    skip = first // tile

    def rows_of(size, start):
        return pl.BlockSpec((tile, size), lambda i: (i + start, 0))

    def whole(array):
        return pl.BlockSpec(array.shape, lambda i: (0, 0), pipeline_mode=pl.Buffered(1))

    extra_specs, out_specs, out_shape = sum_specs(tile, width, sent)
    return pl.pallas_call(
        input_kernel,
        grid=(4,),
        in_specs=[
            rows_of(attn.shape[1], skip),
            rows_of(hidden.shape[1], skip),
            whole(attn_weight),
            whole(up_weight),
            whole(gains),
        ]
        + extra_specs,
        out_specs=out_specs,
        out_shape=out_shape,
        cost_estimate=SMALL,
    )(attn, hidden, attn_weight, up_weight, gains, *(() if sent is None else (sent,)))


def attention_kernel(full, normed, dy, bias, cosine, sine, begin, heads, grad, total, *scratch):
    q_s, k_s, v_s, g_s, dk_s, dv_s = scratch
    weight = full.reshape(full.shape[0] * full.shape[1], full.shape[2])
    rows = normed.shape[0]
    lane = lax.broadcasted_iota(jnp.int32, (1, 128), 1)
    scale = HD ** (-0.5)

    def turn(value, sign):
        low = value[:, :128]
        sine_now = sine[0] * sign
        ahead = pltpu.roll(low, 128 - ROT // 2, 1) * jnp.where(lane < ROT // 2, -sine_now, 0.0)
        behind = pltpu.roll(low, ROT // 2, 1) * jnp.where(lane < ROT // 2, 0.0, sine_now)
        return jnp.concatenate([low * cosine[0] + ahead + behind, value[:, 128:]], axis=1)

    def project(index):
        columns = slice(index * HD, (index + 1) * HD)
        return dot(normed[...], weight[:, columns], ((1,), (0,))) + bias[:, columns]

    q_s[...] = turn(project(0), 1.0).astype(LOW)
    k_s[...] = turn(project(1), 1.0).astype(LOW)
    v_s[...] = project(2).astype(LOW)
    g_s[...] = dot(dy[...], weight[:, 3 * HD :], ((1,), (0,))).astype(LOW)
    dk_s[...] = jnp.zeros_like(dk_s)
    dv_s[...] = jnp.zeros_like(dv_s)
    tile = 320
    for start in range(0, rows, tile):
        here, seen = slice(start, start + tile), slice(0, start + tile)
        query, grad_heads = q_s[here, :], g_s[here, :]
        keys, value = k_s[seen, :], v_s[seen, :]
        scores = dot(query, keys, ((1,), (1,))) * scale
        column = lax.broadcasted_iota(jnp.int32, scores.shape, 1)
        row = lax.broadcasted_iota(jnp.int32, scores.shape, 0) + start
        allowed = (column <= row) & (column >= begin[0, here, :])
        scores = jnp.where(allowed, scores, -1e30)
        shifted = jnp.exp(scores - jnp.max(scores, axis=1, keepdims=True))
        prob = shifted / jnp.sum(shifted, axis=1, keepdims=True)
        low = prob.astype(LOW)
        heads[here, :] = dot(low, value, ((1,), (0,))).astype(LOW)
        grad_prob = dot(grad_heads, value, ((1,), (1,)))
        weighted = jnp.sum(grad_prob * prob, axis=1, keepdims=True)
        grad_scores = (prob * (grad_prob - weighted) * scale).astype(LOW)
        grad_query = dot(grad_scores, keys, ((1,), (0,)))
        cos_here = cosine[0, here, :]
        sine_here = -sine[0, here, :]
        head = grad_query[:, :128]
        ahead = pltpu.roll(head, 128 - ROT // 2, 1) * jnp.where(lane < ROT // 2, -sine_here, 0.0)
        behind = pltpu.roll(head, ROT // 2, 1) * jnp.where(lane < ROT // 2, 0.0, sine_here)
        grad[here, :128] = (head * cos_here + ahead + behind).astype(LOW)
        grad[here, 128:HD] = grad_query[:, 128:].astype(LOW)
        dk_s[seen, :] += dot(grad_scores, query, ((0,), (0,)))
        dv_s[seen, :] += dot(low, grad_heads, ((0,), (0,)))
    grad[:, HD : 2 * HD] = turn(dk_s[...], -1.0).astype(LOW)
    grad[:, 2 * HD :] = dv_s[...].astype(LOW)

    @pl.when(pl.program_id(0) == 0)
    def _():
        total[...] = jnp.zeros_like(total)

    total[...] += jnp.sum(grad[...].astype(WIDE), axis=0, keepdims=True)


def attention(where, gathered, count, normed, dy, bias, cosine, sine, begin):
    tokens, width = normed.shape
    rows = tokens // 4

    def per_sequence(size):
        return pl.BlockSpec((rows, size), lambda s, z: (s, 0))

    def table(size):
        return pl.BlockSpec((1, rows, size), lambda s, z: (s, 0, 0))

    row = pl.BlockSpec((1, 3 * HD), lambda s, z: (0, 0))
    return weighted_call(
        attention_kernel,
        where,
        gathered,
        count,
        (normed, dy, bias, cosine, sine, begin),
        [per_sequence(width), per_sequence(width), row, table(128), table(128), table(1)],
        [per_sequence(HD), per_sequence(3 * HD), row],
        [
            jax.ShapeDtypeStruct((tokens, HD), LOW),
            jax.ShapeDtypeStruct((tokens, 3 * HD), LOW),
            jax.ShapeDtypeStruct((1, 3 * HD), WIDE),
        ],
        (4,),
        [pltpu.VMEM((rows, HD), LOW)] * 4 + [pltpu.VMEM((rows, HD), WIDE)] * 2,
    )


def sum_line(value, count):
    step = 1
    while step < count:
        value = value + lax.ppermute(value, "z", [(i, i ^ step) for i in range(count)])
        step *= 2
    return value


def up_back_kernel(place, *refs):
    result = refs[-1]
    columns = refs[0].shape[1]
    for step in range(4):
        start = pl.multiple_of((place[0] ^ step) * columns, columns)
        result[:, pl.ds(start, columns)] = refs[step][...].astype(WIDE)


def down_back_kernel(place, *refs):
    result = refs[-1]
    columns = refs[0].shape[1]
    for step in range(4):
        start = pl.multiple_of((place[0] ^ step) * columns, columns)
        result[pl.ds(start, columns), :] = refs[step][...].astype(WIDE).T


def attn_back_kernel(place, *refs):
    qkv, out = refs[-2:]
    for step in range(4):
        head = place[0] ^ step
        block = refs[step][...].astype(WIDE)
        for part in range(3):
            qkv[:, part, pl.ds(head, 1), :] = block[:, None, part * HD : (part + 1) * HD]
        out[pl.ds(head, 1)] = block[:, 3 * HD :].T[None]


def gradient_of(kernel, place, blocks, shapes):
    whole = [pl.BlockSpec(memory_space=pltpu.VMEM)] * 4
    return pl.pallas_call(
        kernel,
        in_specs=[pl.BlockSpec(memory_space=pltpu.SMEM)] + whole,
        out_specs=[pl.BlockSpec(memory_space=pltpu.VMEM)] * len(shapes),
        out_shape=[jax.ShapeDtypeStruct(shape, WIDE) for shape in shapes],
        cost_estimate=SMALL,
    )(place.reshape(1), *blocks)


def doc_start(lengths, place):
    passed = place[:, None] >= jnp.cumsum(lengths)[None, :]
    return jnp.sum(jnp.where(passed, lengths[None, :], 0), axis=1)


def per_device(
    inputs,
    doc_lengths,
    norm1_gain,
    norm1_bias,
    qkv_weight,
    qkv_bias,
    out_weight,
    out_bias,
    norm2_gain,
    norm2_bias,
    up_weight,
    up_bias,
    down_weight,
    down_bias,
    cotangent,
):
    rows, width = inputs.shape
    count = lax.axis_size("z")
    zi, xi, ci, yi = [lax.axis_index(axis) for axis in EVERY]
    place = xi * 2 + ci
    hidden_part = up_bias.shape[0] // 4
    part_rows = up_weight.shape[0]
    head_width = 3 * HD

    norms = jnp.stack([norm1_gain, norm1_bias, norm2_gain, norm2_bias])

    def columns_of(weight):
        return lambda t: lax.dynamic_slice_in_dim(weight, t * hidden_part, hidden_part, 1)

    def rows_of(weight):
        return lambda t: lax.dynamic_slice_in_dim(weight, t * hidden_part, hidden_part, 0).T

    def heads_of(qkv, out):
        return lambda t: jnp.concatenate(
            [pick(qkv, t, 1).reshape(part_rows, head_width), pick(out, t, 0).T], axis=1
        )

    def pieces_of(part):
        return [
            lax.dynamic_slice_in_dim(part, (place ^ step) * part_rows, part_rows, 0)
            for step in range(4)
        ]

    def returned(part):
        return traded(pieces_of(part))

    where = jnp.stack([zi, place])
    half = rows // 2

    def side(array):
        return lax.dynamic_slice_in_dim(array, yi * half, half, 0)

    def stage(line, *values):
        line.blocks[-1], values = tie(line.blocks[-1], values)
        return values

    up_blocks = trade(columns_of(up_weight), place)
    up_blocks, x_now, x_beside, dy_beside, lengths_x = tie(
        up_blocks, inputs, swap(inputs, "c"), swap(cotangent, "c"), swap(doc_lengths, "x")
    )

    up_line = Ring(pack(up_blocks), count)
    up_line.hop()
    x_near = swap(side(after(x_now, up_line.blocks[0])), "x")
    heads_now = heads_of(*after((qkv_weight, out_weight), up_line.blocks[0]))
    norm_now, heads_now, lengths_x, lengths_now, dy_now = stage(
        up_line,
        norm_pair(x_now, x_beside, 0, norms, ()),
        [heads_now(place ^ step) for step in range(4)],
        lengths_x,
        doc_lengths,
        (cotangent, dy_beside),
    )

    up_line.hop()
    x_far = swap(after(x_near, lengths_x), "y")
    lengths_pair = jnp.concatenate([lengths_now, lengths_x])
    attn_blocks, lengths_other, dy_flat, dy_now = stage(
        up_line,
        traded(heads_now),
        swap(lengths_pair, "c"),
        copy_pair(*dy_now, 0, ()),
        cotangent,
    )

    up_line.finish()
    dy_near = swap(side(dy_now), "x")
    across = ordered(yi, x_near, after(x_far, attn_blocks[0]), 0).reshape(inputs.shape)
    attn_line = Ring(pack(attn_blocks), count)
    down_rows_of = rows_of(after(down_weight, attn_line.blocks[0]))
    norm_now, attn_line.blocks[0], down_blocks = stage(
        up_line,
        norm_pair(across, swap(across, "c"), 1, norms, norm_now),
        attn_line.blocks[0],
        [down_rows_of(place ^ step) for step in range(4)],
    )
    normed, mixed = norm_now

    attn_line.hop()
    dy_far = swap(after(dy_near, mixed), "y")
    up_rows, active, slope, down_blocks = stage(
        attn_line,
        *up_forward(where, up_line, count, mixed, pick(up_bias.reshape(4, 1, -1), place, 0)),
        traded(down_blocks),
    )

    attn_line.hop()
    dy_across = ordered(yi, dy_near, after(dy_far, active), 0).reshape(cotangent.shape)
    down_line = Ring(pack(down_blocks), count)
    dy_flat = copy_pair(dy_across, swap(dy_across, "c"), 1, (dy_flat,))
    lengths_all = jnp.concatenate([lengths_pair, lengths_other])
    begin = jax.vmap(lambda one: doc_start(one, jnp.arange(rows, dtype=jnp.int32)))(lengths_all)
    dy_flat, down_line.blocks[0], active, begin = stage(
        attn_line, dy_flat, down_line.blocks[0], active, begin
    )

    attn_line.finish()
    grad_down = outer(dy_flat, active)
    ordinal = jnp.arange(rows, dtype=jnp.int32)
    position = (ordinal - begin).astype(WIDE)
    exponent = jnp.arange(ROT // 2, dtype=WIDE) * (-2.0 / ROT)
    angle = position[..., None] * jnp.power(10000.0, exponent)
    angle = jnp.concatenate([angle, angle, jnp.zeros((4, rows, 128 - ROT), WIDE)], axis=-1)
    begin, cosine, sine, down_line.blocks[0], grad_down, dy_flat, attn_bias = stage(
        attn_line,
        begin[..., None],
        jnp.cos(angle),
        jnp.sin(angle),
        down_line.blocks[0],
        grad_down,
        dy_flat,
        pick(qkv_bias.reshape(4, 1, -1), place, 0),
    )

    down_line.hop()
    attn_rows, heads, grad_projected, qkv_bias_term = stage(
        down_line,
        *attention(
            where, attn_line, count, normed, dy_flat, attn_bias, cosine, sine, begin
        ),
    )
    qkv_bias_term = qkv_bias_term[0]

    def first_terms(value, weight):
        return branch_terms(2 * rows, value, weight, None)

    def own_terms(value, weight, sent):
        return branch_terms(0, value, weight, sent)

    down_line.hop()
    grad_attn, heads, attn_first = stage(
        down_line,
        outer(normed, grad_projected, dy_flat, heads),
        heads,
        first_terms(heads, attn_rows),
    )

    down_line.finish()
    grad_attn, grad_down, attn_mine = stage(
        down_line,
        grad_attn,
        grad_down,
        own_terms(heads, attn_rows, swap(attn_first, "c")),
    )

    down_part = lax.psum_scatter(grad_down, "z", scatter_dimension=0, tiled=True)
    attn_part = lax.psum_scatter(grad_attn, "z", scatter_dimension=0, tiled=True)
    attn_over = cross_first(attn_mine[1], cross_rows(attn_mine[0], yi))
    down_rows, grad_hidden, up_bias_term = down_backward(where, down_line, count, dy_flat, slope)
    up_bias_term = up_bias_term[0]
    grad_hidden, ffn_first, active, attn_over = tie(
        grad_hidden, first_terms(active, down_rows), active, attn_over
    )

    gains = norms[0::2]
    attn_over = cross_second(attn_mine[0], *attn_over, yi)
    sent, ffn_sent, grad_hidden, active = tie(
        input_terms(
            2 * rows, grad_projected, after(grad_hidden, attn_over[0]), attn_rows, up_rows, gains, None
        ),
        swap(ffn_first, "c"),
        grad_hidden,
        active,
    )

    ffn_mine, sent_now, attn_over, grad_hidden = tie(
        own_terms(active, down_rows, ffn_sent), swap(sent, "c"), attn_over, grad_hidden
    )
    attn_half = crossed(*attn_over)

    ffn_over = cross_first(ffn_mine[1], cross_rows(ffn_mine[0], yi))
    mine = input_terms(0, grad_projected, grad_hidden, attn_rows, up_rows, gains, sent_now)
    mine, grad_hidden, ffn_over = tie(mine, grad_hidden, ffn_over)

    last_rows = cross_rows(mine[0], yi)
    input_over = cross_first(mine[1], last_rows)
    ffn_over = after(ffn_over, last_rows)
    ffn_over = cross_second(ffn_mine[0], *ffn_over, yi)
    grad_up = outer(mixed, grad_hidden)

    def norm_terms(weight, grad, bias_term, gain, shift):
        weight = weight.astype(WIDE)
        shift_term = jnp.sum(weight * bias_term, axis=1)
        gain_term = (jnp.sum(weight * grad.astype(WIDE), axis=1) - shift * shift_term) / gain
        return gain_term, shift_term

    attn_branch = attn_half + out_bias
    attn_square = jnp.sum(attn_branch * attn_branch)
    input_over, ffn_over, grad_attn, grad_up, attn_branch, attn_square = tie(
        input_over, ffn_over, grad_attn, grad_up, attn_branch, attn_square
    )
    up_part = lax.psum_scatter(grad_up, "z", scatter_dimension=0, tiled=True)
    input_over = cross_second(mine[0], *input_over, yi)
    grad_attn, grad_up = after((grad_attn, grad_up), input_over[0])
    gain1, shift1 = norm_terms(
        attn_rows[:, :head_width], grad_attn[:, :head_width], qkv_bias_term, norm1_gain, norm1_bias
    )
    gain2, shift2 = norm_terms(up_rows, grad_up, up_bias_term, norm2_gain, norm2_bias)
    x_half = own_half(inputs, yi).astype(WIDE)
    ffn_branch = crossed(*ffn_over) + down_bias
    slot = (jnp.arange(8, dtype=jnp.int32) == yi * 4 + place).astype(WIDE)[:, None]
    small = jnp.concatenate(
        [
            gain1,
            shift1,
            gain2,
            shift2,
            jnp.sum(cotangent, axis=0, dtype=WIDE) * 0.5,
            (slot * qkv_bias_term).reshape(-1),
            (slot * up_bias_term).reshape(-1),
            jnp.stack([attn_square, jnp.sum(ffn_branch * ffn_branch)]),
        ]
    )
    for axis in ("c", "y"):
        small = small + swap(small, axis)
    small, input_over, attn_branch, ffn_branch = tie(small, input_over, attn_branch, ffn_branch)
    out_low = (x_half + attn_branch + ffn_branch).astype(LOW)
    out_other = swap(out_low, "y")
    input_half = crossed(*input_over)
    centre_half = x_half - jnp.mean(x_half, axis=-1, keepdims=True)
    scale_half = lax.rsqrt(jnp.mean(centre_half * centre_half, axis=-1, keepdims=True) + EPS)
    unit_half = centre_half * scale_half
    back_half = scale_half * (
        input_half
        - jnp.mean(input_half, axis=-1, keepdims=True)
        - unit_half * jnp.mean(input_half * unit_half, axis=-1, keepdims=True)
    )
    back_low = back_half.astype(LOW)
    back_other = swap(back_low, "y")
    small = after(small, back_low)
    small = small + swap(small, "x")
    down_back = returned(after(down_part, small))
    attn_back = returned(after(attn_part, small))
    small = sum_line(small, count)
    all_columns = 4 * hidden_part
    (down_sum,) = gradient_of(down_back_kernel, place, down_back, [(all_columns, part_rows)])
    qkv_sum, out_sum = gradient_of(
        attn_back_kernel, place, attn_back, [(part_rows, 3, 4, HD), (4, HD, part_rows)]
    )
    outputs = whole_rows(out_low, after(out_other, qkv_sum, small), yi)
    up_part, small, down_sum, qkv_sum, out_sum, outputs = tie(
        up_part, small, down_sum, qkv_sum, out_sum, outputs
    )
    up_pieces = pieces_of(up_part)
    back_other = after(back_other, *up_pieces)
    back_rows = whole_rows(back_low, back_other, yi)
    grad_inputs = cotangent.astype(WIDE) + back_rows.astype(WIDE)
    (up_sum,) = gradient_of(up_back_kernel, place, traded(up_pieces), [(part_rows, all_columns)])

    sizes = [width] * 5 + [8 * head_width, 8 * hidden_part]
    starts = [sum(sizes[:i]) for i in range(len(sizes) + 1)]
    pieces = [small[a:b] for a, b in zip(starts[:-1], starts[1:])]
    qkv_bias_sum = pick(pieces[5].reshape(2, 4, 3, HD), yi, 0)
    up_bias_sum = pick(pieces[6].reshape(2, 4 * hidden_part), yi, 0)
    rms_pair = jnp.sqrt(small[starts[-1] :] / float(rows * 4 * count * width))

    qkv_sum = jnp.transpose(qkv_sum, (0, 2, 1, 3))
    return (
        outputs,
        grad_inputs,
        pieces[0],
        pieces[1],
        qkv_sum,
        qkv_bias_sum,
        out_sum,
        pieces[4],
        pieces[2],
        pieces[3],
        up_sum,
        up_bias_sum,
        down_sum,
        rms_pair[0],
        rms_pair[1],
    )


def solution(mesh):
    dp = mesh.shape["dp"]
    grid = Mesh(mesh.devices.reshape(dp // 4, 2, 2, mesh.shape["tensor"]), EVERY)
    dp = ("z", "x", "c")
    in_specs = (
        P(dp, None),
        P(dp, None),
        P(),
        P(),
        P(dp, "y", None, None),
        P("y", None, None),
        P("y", None, dp),
        P(),
        P(),
        P(),
        P(dp, "y"),
        P("y"),
        P("y", dp),
        P(),
        P(dp, None),
    )
    out_specs = (
        P(dp, None),
        P(dp, None),
        P(),
        P(),
        P(dp, "y", None, None),
        P("y", None, None),
        P("y", None, dp),
        P(),
        P(),
        P(),
        P(dp, "y"),
        P("y"),
        P("y", dp),
        P(),
        P(),
    )
    return jax.shard_map(
        per_device, mesh=grid, in_specs=in_specs, out_specs=out_specs, check_vma=False
    )
```

```python
import jax
import jax.numpy as jnp
from jax import lax
from jax.experimental import pallas as pl
from jax.experimental.pallas import tpu as pltpu
from jax.sharding import Mesh
from jax.sharding import PartitionSpec as P

HD = 256
ROT = 64
EPS = 1e-05
LOW = jnp.bfloat16
WIDE = jnp.float32
GROUP = ("x", "c")
EVERY = ("z", "x", "c", "y")


SMALL = pl.CostEstimate(flops=1 << 20, bytes_accessed=1 << 20, transcendentals=0)


def dot(left, right, dims):
    return lax.dot_general(left, right, (dims, ((), ())), preferred_element_type=WIDE)


def swap(value, axis):
    return lax.ppermute(value, axis, [(0, 1), (1, 0)])


def pick(value, index, axis):
    return lax.dynamic_index_in_dim(value, index, axis, keepdims=False)


def ordered(index, own, other, axis):
    first = jnp.where(index == 0, own, other)
    second = jnp.where(index == 0, other, own)
    return jnp.stack([first, second], axis=axis)


def trade(block, place):
    return traded([block(place ^ step) for step in range(4)])


def traded(blocks):
    return blocks[:1] + [
        lax.ppermute(blocks[step], GROUP, [(i, i ^ step) for i in range(4)])
        for step in range(1, 4)
    ]


class Ring:
    def __init__(self, block, count):
        self.count, self.blocks = count, [block]

    def hop(self, *waits):
        if len(self.blocks) < self.count:
            sent = after(self.blocks[-1], *waits)
            self.blocks.append(
                lax.ppermute(sent, "z", [(i, (i + 1) % self.count) for i in range(self.count)])
            )

    def finish(self):
        while len(self.blocks) < self.count:
            self.hop()


def tie(*values):
    return lax.optimization_barrier(values)


def after(value, *waits):
    return lax.optimization_barrier((value, waits))[0] if waits else value


def cross_rows(mine, yi):
    rows = mine.shape[0] // 2
    part = rows // 4
    return jnp.stack(
        [
            lax.dynamic_slice_in_dim(mine, start + (1 - yi) * part, part, 0)
            for start in (rows // 2, rows + rows // 2)
        ]
    )


def cross_first(over, last):
    return swap(over, "x"), swap(last, "y")


def cross_kernel(yi, first, last, beyond, over_x, over_y, *rest):
    first_kept, first_sent, last_kept, last_sent, total = rest
    part = last.shape[0]

    def add(step, _):
        chunk = pl.ds(pl.multiple_of(step * 16, 16), 16)
        total[chunk, :] = (first[chunk, :].astype(WIDE) + over_x[chunk, :].astype(WIDE)).astype(LOW)
        return 0

    lax.fori_loop(0, first.shape[0] // 16, add, 0, unroll=4)
    first_kept[...] = total[pl.ds(pl.multiple_of(yi[0] * part, 16), part), :]
    first_sent[...] = total[pl.ds(pl.multiple_of((1 - yi[0]) * part, 16), part), :]

    def add_last(step, _):
        chunk = pl.ds(pl.multiple_of(step * 16, 16), 16)
        last_kept[chunk, :] = last[chunk, :].astype(WIDE) + over_y[0, chunk, :].astype(WIDE)
        value = beyond[chunk, :].astype(WIDE) + over_y[1, chunk, :].astype(WIDE)
        last_sent[chunk, :] = value.astype(LOW)
        return 0

    lax.fori_loop(0, part // 16, add_last, 0, unroll=2)


def cross_second(mine, over_x, over_y, yi):
    rows, width = mine.shape[0] // 2, mine.shape[1]
    part = rows // 4
    kept = jax.ShapeDtypeStruct((part, width), LOW)
    place = pl.BlockSpec((part, width), lambda i, yi: (0, 0))
    first, first_sent, last, last_sent = pl.pallas_call(
        cross_kernel,
        grid_spec=pltpu.PrefetchScalarGridSpec(
            num_scalar_prefetch=1,
            grid=(1,),
            in_specs=[
                pl.BlockSpec((2 * part, width), lambda i, yi: (0, 0)),
                pl.BlockSpec((part, width), lambda i, yi: (2 + yi[0], 0)),
                pl.BlockSpec((part, width), lambda i, yi: (6 + yi[0], 0)),
                pl.BlockSpec((2 * part, width), lambda i, yi: (0, 0)),
                pl.BlockSpec((2, part, width), lambda i, yi: (0, 0, 0)),
            ],
            out_specs=[place] * 4,
            scratch_shapes=[pltpu.VMEM((2 * part, width), LOW)],
        ),
        out_shape=[kept, kept, jax.ShapeDtypeStruct((part, width), WIDE), kept],
        cost_estimate=SMALL,
    )(yi.reshape(1), mine, mine, mine, over_x, over_y)
    return first, swap(first_sent, "y"), last, swap(last_sent, "x")


def crossed(own_first, sent_first, own_last, sent_last):
    return jnp.stack(
        [
            own_first.astype(WIDE) + sent_first.astype(WIDE),
            own_last + sent_last.astype(WIDE),
        ]
    )


def own_half(rows_in, yi):
    return pick(rows_in.reshape(2, 2, rows_in.shape[0] // 4, -1), yi, 1)


def whole_rows(half, other, yi):
    return ordered(yi, half, other, 1).reshape(4 * half.shape[1], half.shape[2])


def norm_kernel(first, second, norms, *rest):
    normed, mixed, rows_in = rest[-3:]
    for index, ref in enumerate((first, second)):

        @pl.when(pl.program_id(0) == index)
        def _(ref=ref):
            rows_in[...] = ref[...]

    gain1, shift1, gain2, shift2 = [norms[i : i + 1, :] for i in range(4)]

    def norm(step, _):
        chunk = pl.ds(pl.multiple_of(step * 16, 16), 16)
        value = rows_in[chunk, :].astype(WIDE)
        centre = value - jnp.mean(value, axis=-1, keepdims=True)
        unit = centre * lax.rsqrt(jnp.mean(centre * centre, axis=-1, keepdims=True) + EPS)
        normed[chunk, :] = (unit * gain1 + shift1).astype(LOW)
        mixed[chunk, :] = (unit * gain2 + shift2).astype(LOW)
        return 0

    lax.fori_loop(0, rows_in.shape[0] // 16, norm, 0, unroll=4)


def norm_pair(first, second, offset, norms, before):
    rows, width = first.shape
    tile = rows // 2

    def out_place(s, t):
        return (2 * s + offset) * 2 + t, 0

    return pl.pallas_call(
        norm_kernel,
        grid=(2, 2),
        in_specs=[
            pl.BlockSpec((tile, width), lambda s, t: (jnp.where(s == 0, t, 1), 0)),
            pl.BlockSpec((tile, width), lambda s, t: (jnp.where(s == 0, 0, t), 0)),
            pl.BlockSpec((4, width), lambda s, t: (0, 0)),
        ]
        + [pl.BlockSpec(memory_space=pl.ANY)] * len(before),
        out_specs=[pl.BlockSpec((tile, width), out_place)] * 2,
        out_shape=[jax.ShapeDtypeStruct((4 * rows, width), LOW)] * 2,
        scratch_shapes=[pltpu.VMEM((tile, width), LOW)],
        input_output_aliases={3 + i: i for i in range(len(before))},
        cost_estimate=SMALL,
    )(first, second, norms, *before)


def copy_kernel(*refs):
    for index, ref in enumerate(refs[:2]):

        @pl.when(pl.program_id(0) == index)
        def _(ref=ref):
            refs[-1][...] = ref[...]


def copy_pair(first, second, offset, before):
    rows, width = first.shape
    tile = rows // 2
    return pl.pallas_call(
        copy_kernel,
        grid=(2, 2),
        in_specs=[
            pl.BlockSpec((tile, width), lambda s, t: (jnp.where(s == 0, t, 1), 0)),
            pl.BlockSpec((tile, width), lambda s, t: (jnp.where(s == 0, 0, t), 0)),
        ]
        + [pl.BlockSpec(memory_space=pl.ANY)] * len(before),
        out_specs=pl.BlockSpec((tile, width), lambda s, t: ((2 * s + offset) * 2 + t, 0)),
        out_shape=jax.ShapeDtypeStruct((4 * rows, width), LOW),
        input_output_aliases={2: 0} if before else {},
        cost_estimate=SMALL,
    )(first, second, *before)


def pack_kernel(*refs):
    rows = refs[0].shape[0]
    for index, ref in enumerate(refs[:-1]):
        refs[-1][index * rows : (index + 1) * rows, :] = ref[...]


def pack(blocks):
    rows, columns = blocks[0].shape
    return pl.pallas_call(
        pack_kernel,
        out_shape=jax.ShapeDtypeStruct((len(blocks) * rows, columns), LOW),
        cost_estimate=SMALL,
    )(*blocks)


def outer_kernel(*refs):
    result, pairs, start = refs[-1], refs[:-1], 0
    for left, right in zip(pairs[0::2], pairs[1::2]):
        columns = slice(start, start + right.shape[1])
        result[:, columns] = dot(left[...], right[...], ((0,), (0,))).astype(LOW)
        start = columns.stop


def outer(*arrays):
    tokens, width = arrays[0].shape
    tile = width // 4
    columns = sum(right.shape[1] for right in arrays[1::2])
    in_specs = []
    for right in arrays[1::2]:
        in_specs += [
            pl.BlockSpec((tokens, tile), lambda i: (0, i)),
            pl.BlockSpec(right.shape, lambda i: (0, 0), pipeline_mode=pl.Buffered(1)),
        ]
    return pl.pallas_call(
        outer_kernel,
        grid=(4,),
        in_specs=in_specs,
        out_specs=pl.BlockSpec((tile, columns), lambda i: (i, 0)),
        out_shape=jax.ShapeDtypeStruct((width, columns), LOW),
        cost_estimate=SMALL,
    )(*arrays)


def collect(where, refs, count, full, result, copies, kept):
    zi, place = where[0], where[1]
    rows = full.shape[1]

    def move(ref, block):
        for step in range(4):
            pltpu.make_async_copy(
                ref.at[pl.ds(step * rows, rows)],
                full.at[4 * block + (place ^ step)],
                copies.at[4 * block + step],
            ).start()

    for block in range(count):
        for step in range(count):

            @pl.when(zi == (block + step) % count)
            def _(step=step):
                move(refs[step], block)

    for block in range(count):
        for step in range(4):
            pltpu.make_async_copy(
                refs[0].at[pl.ds(0, rows)],
                full.at[4 * block + (place ^ step)],
                copies.at[4 * block + step],
            ).wait()
    pltpu.make_async_copy(full, result, kept).start()


def weighted_call(kernel, where, gathered, count, operands, in_specs, out_specs, out_shape, grid, scratch):
    refs = gathered.blocks
    rows, columns = refs[0].shape
    rows = rows // 4
    last = grid[0] - 1

    def body(where_ref, *args):
        parts, args = args[: len(refs)], args[len(refs) :]
        inputs, args = args[: len(operands)], args[len(operands) :]
        result, args = args[0], args[1:]
        full, copies, kept = args[-3:]

        @pl.when(pl.program_id(0) == 0)
        def _():
            collect(where_ref, parts, count, full, result, copies, kept)

        kernel(full, *inputs, *args[:-3])

        @pl.when(pl.program_id(0) == last)
        def _():
            pltpu.make_async_copy(full, result, kept).wait()

    result = pl.pallas_call(
        body,
        grid_spec=pltpu.PrefetchScalarGridSpec(
            num_scalar_prefetch=1,
            grid=grid,
            in_specs=[pl.BlockSpec(memory_space=pl.ANY)] * len(refs) + in_specs,
            out_specs=[pl.BlockSpec(memory_space=pl.ANY)] + out_specs,
            scratch_shapes=scratch
            + [
                pltpu.VMEM((4 * count, rows, columns), LOW),
                pltpu.SemaphoreType.DMA((4 * count,)),
                pltpu.SemaphoreType.DMA,
            ],
        ),
        out_shape=[jax.ShapeDtypeStruct((4 * count, rows, columns), LOW)] + out_shape,
        cost_estimate=SMALL,
    )(where, *refs, *operands)
    return [result[0].reshape(4 * count * rows, columns)] + list(result[1:])


def up_kernel(full, mixed, bias, active, slope):
    weight = full.reshape(full.shape[0] * full.shape[1], full.shape[2])
    for start in range(0, weight.shape[1], 256):
        columns = slice(start, start + 256)
        hidden = dot(mixed[...], weight[:, columns], ((1,), (0,))) + bias[:, columns]
        cdf = 0.5 * (1.0 + lax.erf(hidden * (0.5**0.5)))
        density = jnp.exp(-0.5 * hidden * hidden) * 0.3989422804014327
        active[:, columns] = (hidden * cdf).astype(LOW)
        slope[:, columns] = (cdf + hidden * density).astype(LOW)


def up_forward(where, gathered, count, mixed, bias):
    tokens, width = mixed.shape
    columns = bias.shape[1]
    tile = tokens // 8

    def rows_of(size):
        return pl.BlockSpec((tile, size), lambda i, z: (i, 0))

    return weighted_call(
        up_kernel,
        where,
        gathered,
        count,
        (mixed, bias),
        [rows_of(width), pl.BlockSpec((1, columns), lambda i, z: (0, 0))],
        [rows_of(columns)] * 2,
        [jax.ShapeDtypeStruct((tokens, columns), LOW)] * 2,
        (8,),
        [],
    )


def down_kernel(full, dy, slope, grad, total):
    weight = full.reshape(full.shape[0] * full.shape[1], full.shape[2])

    @pl.when(pl.program_id(0) == 0)
    def _():
        total[...] = jnp.zeros_like(total)

    for start in range(0, weight.shape[1], 256):
        columns = slice(start, start + 256)
        value = dot(dy[...], weight[:, columns], ((1,), (0,))) * slope[:, columns].astype(WIDE)
        value = value.astype(LOW)
        grad[:, columns] = value
        total[:, columns] += jnp.sum(value.astype(WIDE), axis=0, keepdims=True)


def down_backward(where, gathered, count, dy, slope):
    tokens, width = dy.shape
    columns = slope.shape[1]
    tile = tokens // 8

    def rows_of(size):
        return pl.BlockSpec((tile, size), lambda i, z: (i, 0))

    return weighted_call(
        down_kernel,
        where,
        gathered,
        count,
        (dy, slope),
        [rows_of(width), rows_of(columns)],
        [rows_of(columns), pl.BlockSpec((1, columns), lambda i, z: (0, 0))],
        [
            jax.ShapeDtypeStruct((tokens, columns), LOW),
            jax.ShapeDtypeStruct((1, columns), WIDE),
        ],
        (8,),
        [],
    )


def sum_specs(tile, width, sent):
    rows = pl.BlockSpec((tile, width), lambda i: (i, 0))
    shape = jax.ShapeDtypeStruct((4 * tile, width), LOW)
    if sent is None:
        return [], rows, shape
    one = pl.BlockSpec((tile, width), lambda i: (0, 0))
    return [rows], [rows, one], [shape, jax.ShapeDtypeStruct((tile, width), LOW)]


def put_sum(term, columns, rest):
    if len(rest) == 1:
        rest[0][:, columns] = term.astype(LOW)
        return
    sent, result, over = rest
    value = (term + sent[:, columns].astype(WIDE)).astype(LOW)
    result[:, columns] = value

    @pl.when(pl.program_id(0) == 2)
    def _():
        over[:, columns] = value


def branch_kernel(value, weight, *rest):
    for start in range(0, weight.shape[0], 512):
        columns = slice(start, start + 512)
        term = dot(value[...], weight[columns, weight.shape[1] - value.shape[1] :], ((1,), (1,)))
        put_sum(term, columns, rest)


def branch_terms(first, value, weight, sent):
    tokens, width = value.shape[0] // 2, weight.shape[0]
    tile = tokens // 4
    skip = first // tile
    extra_specs, out_specs, out_shape = sum_specs(tile, width, sent)
    return pl.pallas_call(
        branch_kernel,
        grid=(4,),
        in_specs=[
            pl.BlockSpec((tile, value.shape[1]), lambda i: (i + skip, 0)),
            pl.BlockSpec(weight.shape, lambda i: (0, 0), pipeline_mode=pl.Buffered(1)),
        ]
        + extra_specs,
        out_specs=out_specs,
        out_shape=out_shape,
        cost_estimate=SMALL,
    )(value, weight, *(() if sent is None else (sent,)))


def input_kernel(attn, hidden, attn_weight, up_weight, gains, *rest):
    for start in range(0, gains.shape[1], 512):
        columns = slice(start, start + 512)
        value = (
            dot(attn[...], attn_weight[columns, : attn.shape[1]], ((1,), (1,))) * gains[0:1, columns]
        )
        value += dot(hidden[...], up_weight[columns, :], ((1,), (1,))) * gains[1:2, columns]
        put_sum(value, columns, rest)


def input_terms(first, attn, hidden, attn_weight, up_weight, gains, sent):
    tokens = attn.shape[0] // 2
    width = gains.shape[1]
    tile = tokens // 4
    skip = first // tile

    def rows_of(size, start):
        return pl.BlockSpec((tile, size), lambda i: (i + start, 0))

    def whole(array):
        return pl.BlockSpec(array.shape, lambda i: (0, 0), pipeline_mode=pl.Buffered(1))

    extra_specs, out_specs, out_shape = sum_specs(tile, width, sent)
    return pl.pallas_call(
        input_kernel,
        grid=(4,),
        in_specs=[
            rows_of(attn.shape[1], skip),
            rows_of(hidden.shape[1], skip),
            whole(attn_weight),
            whole(up_weight),
            whole(gains),
        ]
        + extra_specs,
        out_specs=out_specs,
        out_shape=out_shape,
        cost_estimate=SMALL,
    )(attn, hidden, attn_weight, up_weight, gains, *(() if sent is None else (sent,)))


def attention_kernel(full, normed, dy, bias, cosine, sine, begin, heads, grad, total, *scratch):
    q_s, k_s, v_s, g_s, dk_s, dv_s = scratch
    weight = full.reshape(full.shape[0] * full.shape[1], full.shape[2])
    rows = normed.shape[0]
    lane = lax.broadcasted_iota(jnp.int32, (1, 128), 1)
    scale = HD ** (-0.5)

    def turn(value, sign):
        low = value[:, :128]
        sine_now = sine[0] * sign
        ahead = pltpu.roll(low, 128 - ROT // 2, 1) * jnp.where(lane < ROT // 2, -sine_now, 0.0)
        behind = pltpu.roll(low, ROT // 2, 1) * jnp.where(lane < ROT // 2, 0.0, sine_now)
        return jnp.concatenate([low * cosine[0] + ahead + behind, value[:, 128:]], axis=1)

    def project(index):
        columns = slice(index * HD, (index + 1) * HD)
        return dot(normed[...], weight[:, columns], ((1,), (0,))) + bias[:, columns]

    q_s[...] = turn(project(0), 1.0).astype(LOW)
    k_s[...] = turn(project(1), 1.0).astype(LOW)
    v_s[...] = project(2).astype(LOW)
    g_s[...] = dot(dy[...], weight[:, 3 * HD :], ((1,), (0,))).astype(LOW)
    dk_s[...] = jnp.zeros_like(dk_s)
    dv_s[...] = jnp.zeros_like(dv_s)
    tile = 320
    for start in range(0, rows, tile):
        here, seen = slice(start, start + tile), slice(0, start + tile)
        query, grad_heads = q_s[here, :], g_s[here, :]
        keys, value = k_s[seen, :], v_s[seen, :]
        scores = dot(query, keys, ((1,), (1,))) * scale
        column = lax.broadcasted_iota(jnp.int32, scores.shape, 1)
        row = lax.broadcasted_iota(jnp.int32, scores.shape, 0) + start
        allowed = (column <= row) & (column >= begin[0, here, :])
        scores = jnp.where(allowed, scores, -1e30)
        shifted = jnp.exp(scores - jnp.max(scores, axis=1, keepdims=True))
        prob = shifted / jnp.sum(shifted, axis=1, keepdims=True)
        low = prob.astype(LOW)
        heads[here, :] = dot(low, value, ((1,), (0,))).astype(LOW)
        grad_prob = dot(grad_heads, value, ((1,), (1,)))
        weighted = jnp.sum(grad_prob * prob, axis=1, keepdims=True)
        grad_scores = (prob * (grad_prob - weighted) * scale).astype(LOW)
        grad_query = dot(grad_scores, keys, ((1,), (0,)))
        cos_here = cosine[0, here, :]
        sine_here = -sine[0, here, :]
        head = grad_query[:, :128]
        ahead = pltpu.roll(head, 128 - ROT // 2, 1) * jnp.where(lane < ROT // 2, -sine_here, 0.0)
        behind = pltpu.roll(head, ROT // 2, 1) * jnp.where(lane < ROT // 2, 0.0, sine_here)
        grad[here, :128] = (head * cos_here + ahead + behind).astype(LOW)
        grad[here, 128:HD] = grad_query[:, 128:].astype(LOW)
        dk_s[seen, :] += dot(grad_scores, query, ((0,), (0,)))
        dv_s[seen, :] += dot(low, grad_heads, ((0,), (0,)))
    grad[:, HD : 2 * HD] = turn(dk_s[...], -1.0).astype(LOW)
    grad[:, 2 * HD :] = dv_s[...].astype(LOW)

    @pl.when(pl.program_id(0) == 0)
    def _():
        total[...] = jnp.zeros_like(total)

    total[...] += jnp.sum(grad[...].astype(WIDE), axis=0, keepdims=True)


def attention(where, gathered, count, normed, dy, bias, cosine, sine, begin):
    tokens, width = normed.shape
    rows = tokens // 4

    def per_sequence(size):
        return pl.BlockSpec((rows, size), lambda s, z: (s, 0))

    def table(size):
        return pl.BlockSpec((1, rows, size), lambda s, z: (s, 0, 0))

    row = pl.BlockSpec((1, 3 * HD), lambda s, z: (0, 0))
    return weighted_call(
        attention_kernel,
        where,
        gathered,
        count,
        (normed, dy, bias, cosine, sine, begin),
        [per_sequence(width), per_sequence(width), row, table(128), table(128), table(1)],
        [per_sequence(HD), per_sequence(3 * HD), row],
        [
            jax.ShapeDtypeStruct((tokens, HD), LOW),
            jax.ShapeDtypeStruct((tokens, 3 * HD), LOW),
            jax.ShapeDtypeStruct((1, 3 * HD), WIDE),
        ],
        (4,),
        [pltpu.VMEM((rows, HD), LOW)] * 4 + [pltpu.VMEM((rows, HD), WIDE)] * 2,
    )


def sum_line(value, count):
    step = 1
    while step < count:
        value = value + lax.ppermute(value, "z", [(i, i ^ step) for i in range(count)])
        step *= 2
    return value


def up_back_kernel(place, *refs):
    result = refs[-1]
    columns = refs[0].shape[1]
    for step in range(4):
        start = pl.multiple_of((place[0] ^ step) * columns, columns)
        result[:, pl.ds(start, columns)] = refs[step][...].astype(WIDE)


def down_back_kernel(place, *refs):
    result = refs[-1]
    columns = refs[0].shape[1]
    for step in range(4):
        start = pl.multiple_of((place[0] ^ step) * columns, columns)
        result[pl.ds(start, columns), :] = refs[step][...].astype(WIDE).T


def attn_back_kernel(place, *refs):
    qkv, out = refs[-2:]
    for step in range(4):
        head = place[0] ^ step
        block = refs[step][...].astype(WIDE)
        for part in range(3):
            qkv[:, part, pl.ds(head, 1), :] = block[:, None, part * HD : (part + 1) * HD]
        out[pl.ds(head, 1)] = block[:, 3 * HD :].T[None]


def gradient_of(kernel, place, blocks, shapes):
    whole = [pl.BlockSpec(memory_space=pltpu.VMEM)] * 4
    return pl.pallas_call(
        kernel,
        in_specs=[pl.BlockSpec(memory_space=pltpu.SMEM)] + whole,
        out_specs=[pl.BlockSpec(memory_space=pltpu.VMEM)] * len(shapes),
        out_shape=[jax.ShapeDtypeStruct(shape, WIDE) for shape in shapes],
        cost_estimate=SMALL,
    )(place.reshape(1), *blocks)


def doc_start(lengths, place):
    passed = place[:, None] >= jnp.cumsum(lengths)[None, :]
    return jnp.sum(jnp.where(passed, lengths[None, :], 0), axis=1)


def per_device(
    inputs,
    doc_lengths,
    norm1_gain,
    norm1_bias,
    qkv_weight,
    qkv_bias,
    out_weight,
    out_bias,
    norm2_gain,
    norm2_bias,
    up_weight,
    up_bias,
    down_weight,
    down_bias,
    cotangent,
):
    rows, width = inputs.shape
    count = lax.axis_size("z")
    zi, xi, ci, yi = [lax.axis_index(axis) for axis in EVERY]
    place = xi * 2 + ci
    hidden_part = up_bias.shape[0] // 4
    part_rows = up_weight.shape[0]
    head_width = 3 * HD

    norms = jnp.stack([norm1_gain, norm1_bias, norm2_gain, norm2_bias])

    def columns_of(weight):
        return lambda t: lax.dynamic_slice_in_dim(weight, t * hidden_part, hidden_part, 1)

    def rows_of(weight):
        return lambda t: lax.dynamic_slice_in_dim(weight, t * hidden_part, hidden_part, 0).T

    def heads_of(qkv, out):
        return lambda t: jnp.concatenate(
            [pick(qkv, t, 1).reshape(part_rows, head_width), pick(out, t, 0).T], axis=1
        )

    def pieces_of(part):
        return [
            lax.dynamic_slice_in_dim(part, (place ^ step) * part_rows, part_rows, 0)
            for step in range(4)
        ]

    def returned(part):
        return traded(pieces_of(part))

    where = jnp.stack([zi, place])
    half = rows // 2

    def side(array):
        return lax.dynamic_slice_in_dim(array, yi * half, half, 0)

    def stage(line, *values):
        line.blocks[-1], values = tie(line.blocks[-1], values)
        return values

    up_blocks = trade(columns_of(up_weight), place)
    up_blocks, x_now, x_beside, dy_beside, lengths_x = tie(
        up_blocks, inputs, swap(inputs, "c"), swap(cotangent, "c"), swap(doc_lengths, "x")
    )

    up_line = Ring(pack(up_blocks), count)
    up_line.hop()
    x_near = swap(side(after(x_now, up_line.blocks[0])), "x")
    heads_now = heads_of(*after((qkv_weight, out_weight), up_line.blocks[0]))
    norm_now, heads_now, lengths_x, lengths_now, dy_now = stage(
        up_line,
        norm_pair(x_now, x_beside, 0, norms, ()),
        [heads_now(place ^ step) for step in range(4)],
        lengths_x,
        doc_lengths,
        (cotangent, dy_beside),
    )

    up_line.hop()
    x_far = swap(after(x_near, lengths_x), "y")
    lengths_pair = jnp.concatenate([lengths_now, lengths_x])
    attn_blocks, lengths_other, dy_flat, dy_now = stage(
        up_line,
        traded(heads_now),
        swap(lengths_pair, "c"),
        copy_pair(*dy_now, 0, ()),
        cotangent,
    )

    up_line.finish()
    dy_near = swap(side(dy_now), "x")
    across = ordered(yi, x_near, after(x_far, attn_blocks[0]), 0).reshape(inputs.shape)
    attn_line = Ring(pack(attn_blocks), count)
    down_rows_of = rows_of(after(down_weight, attn_line.blocks[0]))
    norm_now, attn_line.blocks[0], down_blocks = stage(
        up_line,
        norm_pair(across, swap(across, "c"), 1, norms, norm_now),
        attn_line.blocks[0],
        [down_rows_of(place ^ step) for step in range(4)],
    )
    normed, mixed = norm_now

    attn_line.hop()
    dy_far = swap(after(dy_near, mixed), "y")
    up_rows, active, slope, down_blocks = stage(
        attn_line,
        *up_forward(where, up_line, count, mixed, pick(up_bias.reshape(4, 1, -1), place, 0)),
        traded(down_blocks),
    )

    attn_line.hop()
    dy_across = ordered(yi, dy_near, after(dy_far, active), 0).reshape(cotangent.shape)
    down_line = Ring(pack(down_blocks), count)
    dy_flat = copy_pair(dy_across, swap(dy_across, "c"), 1, (dy_flat,))
    lengths_all = jnp.concatenate([lengths_pair, lengths_other])
    begin = jax.vmap(lambda one: doc_start(one, jnp.arange(rows, dtype=jnp.int32)))(lengths_all)
    dy_flat, down_line.blocks[0], active, begin = stage(
        attn_line, dy_flat, down_line.blocks[0], active, begin
    )

    attn_line.finish()
    grad_down = outer(dy_flat, active)
    ordinal = jnp.arange(rows, dtype=jnp.int32)
    position = (ordinal - begin).astype(WIDE)
    exponent = jnp.arange(ROT // 2, dtype=WIDE) * (-2.0 / ROT)
    angle = position[..., None] * jnp.power(10000.0, exponent)
    angle = jnp.concatenate([angle, angle, jnp.zeros((4, rows, 128 - ROT), WIDE)], axis=-1)
    begin, cosine, sine, down_line.blocks[0], grad_down, dy_flat, attn_bias = stage(
        attn_line,
        begin[..., None],
        jnp.cos(angle),
        jnp.sin(angle),
        down_line.blocks[0],
        grad_down,
        dy_flat,
        pick(qkv_bias.reshape(4, 1, -1), place, 0),
    )

    down_line.hop()
    attn_rows, heads, grad_projected, qkv_bias_term = stage(
        down_line,
        *attention(
            where, attn_line, count, normed, dy_flat, attn_bias, cosine, sine, begin
        ),
    )
    qkv_bias_term = qkv_bias_term[0]

    def first_terms(value, weight):
        return branch_terms(2 * rows, value, weight, None)

    def own_terms(value, weight, sent):
        return branch_terms(0, value, weight, sent)

    down_line.hop()
    grad_attn, heads, attn_first = stage(
        down_line,
        outer(normed, grad_projected, dy_flat, heads),
        heads,
        first_terms(heads, attn_rows),
    )

    down_line.finish()
    grad_attn, grad_down, attn_mine = stage(
        down_line,
        grad_attn,
        grad_down,
        own_terms(heads, attn_rows, swap(attn_first, "c")),
    )

    down_part = lax.psum_scatter(grad_down, "z", scatter_dimension=0, tiled=True)
    attn_part = lax.psum_scatter(grad_attn, "z", scatter_dimension=0, tiled=True)
    attn_over = cross_first(attn_mine[1], cross_rows(attn_mine[0], yi))
    down_rows, grad_hidden, up_bias_term = down_backward(where, down_line, count, dy_flat, slope)
    up_bias_term = up_bias_term[0]
    grad_hidden, ffn_first, active, attn_over = tie(
        grad_hidden, first_terms(active, down_rows), active, attn_over
    )

    gains = norms[0::2]
    attn_over = cross_second(attn_mine[0], *attn_over, yi)
    sent, ffn_sent, grad_hidden, active = tie(
        input_terms(
            2 * rows, grad_projected, after(grad_hidden, attn_over[0]), attn_rows, up_rows, gains, None
        ),
        swap(ffn_first, "c"),
        grad_hidden,
        active,
    )

    ffn_mine, sent_now, attn_over, grad_hidden = tie(
        own_terms(active, down_rows, ffn_sent), swap(sent, "c"), attn_over, grad_hidden
    )
    attn_half = crossed(*attn_over)

    ffn_over = cross_first(ffn_mine[1], cross_rows(ffn_mine[0], yi))
    mine = input_terms(0, grad_projected, grad_hidden, attn_rows, up_rows, gains, sent_now)
    mine, grad_hidden, ffn_over = tie(mine, grad_hidden, ffn_over)

    last_rows = cross_rows(mine[0], yi)
    input_over = cross_first(mine[1], last_rows)
    ffn_over = after(ffn_over, last_rows)
    ffn_over = cross_second(ffn_mine[0], *ffn_over, yi)
    grad_up = outer(mixed, grad_hidden)

    def norm_terms(weight, grad, bias_term, gain, shift):
        weight = weight.astype(WIDE)
        shift_term = jnp.sum(weight * bias_term, axis=1)
        gain_term = (jnp.sum(weight * grad.astype(WIDE), axis=1) - shift * shift_term) / gain
        return gain_term, shift_term

    attn_branch = attn_half + out_bias
    attn_square = jnp.sum(attn_branch * attn_branch)
    gain1, shift1 = norm_terms(
        attn_rows[:, :head_width], after(grad_attn, grad_up)[:, :head_width], qkv_bias_term, norm1_gain, norm1_bias
    )
    input_over, ffn_over, grad_up, attn_branch, attn_square, gain1, shift1 = tie(
        input_over, ffn_over, grad_up, attn_branch, attn_square, gain1, shift1
    )
    up_part = lax.psum_scatter(grad_up, "z", scatter_dimension=0, tiled=True)
    input_over = cross_second(mine[0], *input_over, yi)
    grad_up = after(grad_up, input_over[0])
    gain2, shift2 = norm_terms(up_rows, grad_up, up_bias_term, norm2_gain, norm2_bias)
    x_half = own_half(inputs, yi).astype(WIDE)
    ffn_branch = crossed(*ffn_over) + down_bias
    slot = (jnp.arange(8, dtype=jnp.int32) == yi * 4 + place).astype(WIDE)[:, None]
    small = jnp.concatenate(
        [
            gain1,
            shift1,
            gain2,
            shift2,
            jnp.sum(cotangent, axis=0, dtype=WIDE) * 0.5,
            (slot * qkv_bias_term).reshape(-1),
            (slot * up_bias_term).reshape(-1),
            jnp.stack([attn_square, jnp.sum(ffn_branch * ffn_branch)]),
        ]
    )
    for axis in ("c", "y"):
        small = small + swap(small, axis)
    small, input_over, attn_branch, ffn_branch = tie(small, input_over, attn_branch, ffn_branch)
    out_low = (x_half + attn_branch + ffn_branch).astype(LOW)
    out_other = swap(out_low, "y")
    input_half = crossed(*input_over)
    centre_half = x_half - jnp.mean(x_half, axis=-1, keepdims=True)
    scale_half = lax.rsqrt(jnp.mean(centre_half * centre_half, axis=-1, keepdims=True) + EPS)
    unit_half = centre_half * scale_half
    back_half = scale_half * (
        input_half
        - jnp.mean(input_half, axis=-1, keepdims=True)
        - unit_half * jnp.mean(input_half * unit_half, axis=-1, keepdims=True)
    )
    back_low = back_half.astype(LOW)
    back_other = swap(back_low, "y")
    small = after(small, back_low)
    small = small + swap(small, "x")
    down_back = returned(after(down_part, small))
    attn_back = returned(after(attn_part, small))
    small = sum_line(small, count)
    all_columns = 4 * hidden_part
    (down_sum,) = gradient_of(down_back_kernel, place, down_back, [(all_columns, part_rows)])
    qkv_sum, out_sum = gradient_of(
        attn_back_kernel, place, attn_back, [(part_rows, 3, 4, HD), (4, HD, part_rows)]
    )
    outputs = whole_rows(out_low, after(out_other, qkv_sum, small), yi)
    up_part, small, down_sum, qkv_sum, out_sum, outputs = tie(
        up_part, small, down_sum, qkv_sum, out_sum, outputs
    )
    up_pieces = pieces_of(up_part)
    back_other = after(back_other, *up_pieces)
    back_rows = whole_rows(back_low, back_other, yi)
    grad_inputs = cotangent.astype(WIDE) + back_rows.astype(WIDE)
    (up_sum,) = gradient_of(up_back_kernel, place, traded(up_pieces), [(part_rows, all_columns)])

    sizes = [width] * 5 + [8 * head_width, 8 * hidden_part]
    starts = [sum(sizes[:i]) for i in range(len(sizes) + 1)]
    pieces = [small[a:b] for a, b in zip(starts[:-1], starts[1:])]
    qkv_bias_sum = pick(pieces[5].reshape(2, 4, 3, HD), yi, 0)
    up_bias_sum = pick(pieces[6].reshape(2, 4 * hidden_part), yi, 0)
    rms_pair = jnp.sqrt(small[starts[-1] :] / float(rows * 4 * count * width))

    qkv_sum = jnp.transpose(qkv_sum, (0, 2, 1, 3))
    return (
        outputs,
        grad_inputs,
        pieces[0],
        pieces[1],
        qkv_sum,
        qkv_bias_sum,
        out_sum,
        pieces[4],
        pieces[2],
        pieces[3],
        up_sum,
        up_bias_sum,
        down_sum,
        rms_pair[0],
        rms_pair[1],
    )


def solution(mesh):
    dp = mesh.shape["dp"]
    grid = Mesh(mesh.devices.reshape(dp // 4, 2, 2, mesh.shape["tensor"]), EVERY)
    dp = ("z", "x", "c")
    in_specs = (
        P(dp, None),
        P(dp, None),
        P(),
        P(),
        P(dp, "y", None, None),
        P("y", None, None),
        P("y", None, dp),
        P(),
        P(),
        P(),
        P(dp, "y"),
        P("y"),
        P("y", dp),
        P(),
        P(dp, None),
    )
    out_specs = (
        P(dp, None),
        P(dp, None),
        P(),
        P(),
        P(dp, "y", None, None),
        P("y", None, None),
        P("y", None, dp),
        P(),
        P(),
        P(),
        P(dp, "y"),
        P("y"),
        P("y", dp),
        P(),
        P(),
    )
    return jax.shard_map(
        per_device, mesh=grid, in_specs=in_specs, out_specs=out_specs, check_vma=False
    )
```
